32 devices in a mesh: dp: 16 (over z, y, x), mp: 2 (over core).
Axes of the slice: x: 2, y: 2, z: 4, core: 2. Of those that a mesh axis runs over, the one named last changes fastest.
Arguments:
- partial_grads: bfloat16 [16, 2, 2, 512, 1024], P('dp', None, None, None, 'mp')
- factors: bfloat16 [2, 4, 512, 1024], P('mp', None, 'dp'), as said below
- inverse_factors: bfloat16 [2, 4, 512, 1024], P('mp', None, 'dp'), as said below
- probes: bfloat16 [2, 4, 512, 512], P('mp', None, 'dp'), may hold values from -6 to 6
- slot_table: int32 [2, 4], P('mp'), may hold values from 0 to 3, as said below
Outputs:
- preconditioned: bfloat16 [2, 2, 512, 1024], P(None, None, 'dp', 'mp')
- new_factors: bfloat16 [2, 4, 512, 1024], P('mp', None, 'dp')
The draws below stay inside these ranges and needn't reach their ends.
Inputs may be any that keep to these rules, and one draw needn't show every extreme that they name: `slot_table`: in each row the 4 entries are distinct slots; slot j belongs to owner j // 4 (an owner is a group of 16 consecutive dp devices; the starting program sends slots 2k and 2k+1 to dp device 16k for updating), and in every row some owner holds 4 blocks. `factors`: both halves of every slot are upper triangular with a positive diagonal. `inverse_factors`: both halves of every slot are upper triangular with a positive diagonal.
All inputs are finite; a program needn't handle non-finite values. Where the reference program divides by a largest or mean magnitude, that divisor is 1e-20 or more.
Results may differ from the reference program's by a relative error of at most 0.011.
Values may be sent and summed in bfloat16 or wider, within the bound.
No kernel may reach another device: no remote copies, remote signals or barrier semaphores. Data moves between devices by JAX's collectives and lax.ppermute only.
A program may use at most 64 MiB of HBM per device.

```python
import math
import jax
import jax.numpy as jnp
from jax import lax

BLOCK = 512
EXPERTS = 2
BROW = 2
GROUP = 16
BLK_COL = 4
SLOTS = 4
OWN_SLOTS = 4
WCOLS = 1024
N_DP = 16
N_MP = 2


def draw_partial_grads(key, part):
    full_shape = (N_DP, EXPERTS, BROW, BLOCK, WCOLS)
    noise_key = jax.random.fold_in(key, 11)
    row_key = jax.random.fold_in(key, 12)
    col_key = jax.random.fold_in(key, 13)
    row_index = jnp.arange(BLOCK, dtype=jnp.float32)
    rise_scale = jnp.exp(0.55 * row_index / BLOCK)
    row_scale = jnp.exp(jax.random.uniform(row_key, (EXPERTS, BROW, BLOCK), minval=0.0, maxval=math.log(10.0))) * rise_scale
    col_scale = jnp.exp(jax.random.uniform(col_key, (WCOLS,), minval=0.0, maxval=math.log(4.0)))
    values = jax.random.normal(noise_key, full_shape)
    scaled = 0.25 * values * row_scale[None, :, :, :, None] * col_scale
    return scaled.astype(jnp.float32).astype(jnp.bfloat16)


def triangular_draw(key, first_tag, second_tag):
    full_shape = (N_MP, OWN_SLOTS, 2, BLOCK, BLOCK)
    diag_key = jax.random.fold_in(key, first_tag)
    upper_key = jax.random.fold_in(key, second_tag)
    diag_values = jnp.exp(jax.random.uniform(diag_key, full_shape[:-1], minval=math.log(0.7), maxval=math.log(1.4)))
    upper_values = jax.random.normal(upper_key, full_shape)
    row_index = jnp.arange(BLOCK)[:, None]
    col_index = jnp.arange(BLOCK)[None, :]
    upper_mask = col_index > row_index
    eye_mask = col_index == row_index
    matrix = jnp.where(upper_mask, upper_values * (0.35 / math.sqrt(BLOCK)), 0.0)
    matrix = matrix + jnp.where(eye_mask, diag_values[..., :, None], 0.0)
    matrix = matrix.transpose(0, 1, 3, 2, 4).reshape(N_MP, OWN_SLOTS, BLOCK, 2 * BLOCK)
    return matrix.astype(jnp.float32).astype(jnp.bfloat16)


def draw_factors(key, part):
    return triangular_draw(key, 21, 22)


def draw_inverse_factors(key, part):
    return triangular_draw(key, 31, 32)


def draw_slot_table(key, part):
    owners = N_DP // GROUP
    rest_count = BLK_COL - SLOTS

    def one_column(col_key):
        first_key = jax.random.fold_in(col_key, 1)
        second_key = jax.random.fold_in(col_key, 2)
        third_key = jax.random.fold_in(col_key, 3)
        fourth_key = jax.random.fold_in(col_key, 4)
        owner_order = jax.random.permutation(first_key, owners)
        busy_slots = owner_order[0] * SLOTS + jax.random.permutation(second_key, SLOTS)
        extra_slots = owner_order[1:1 + rest_count] * SLOTS + jax.random.randint(third_key, (rest_count,), 0, SLOTS)
        listed = jnp.concatenate([busy_slots, extra_slots]).astype(jnp.int32)
        shuffle = jax.random.permutation(fourth_key, BLK_COL)
        return jnp.zeros((BLK_COL,), jnp.int32).at[shuffle].set(listed)
    column_keys = jax.vmap(lambda index_value: jax.random.fold_in(key, index_value))(jnp.arange(N_MP))
    return jax.vmap(one_column)(column_keys)


def block_scale(key, dims, split, low, largest):
    factor_of, own = 1.0, jax.random.fold_in(key, 6)
    for position, parts in split:
        draws = jnp.exp(jax.random.uniform(jax.random.fold_in(own, position), (parts,), jnp.float32, low / len(split), largest / len(split)))
        factor_of = factor_of * jnp.repeat(draws, dims[position] // parts).reshape([-1 if axis == position else 1 for axis in range(len(dims))])
    return factor_of


def normal_values(rng, extent, deviation, reach, cuts=(), kind=jnp.bfloat16):
    array = deviation * jax.random.normal(rng, extent, jnp.float32)
    if cuts:
        array = array * block_scale(rng, extent, cuts, -0.22, 0.18)
    return jnp.clip(array, -reach, reach).astype(kind)


def setup_inputs(seed: int = 0) -> dict:
    keys = jax.random.split(jax.random.key(seed), 6)
    return {
        "partial_grads": draw_partial_grads(jax.random.fold_in(keys[5], 71), 0),
        "factors": draw_factors(jax.random.fold_in(keys[5], 71), 0),
        "inverse_factors": draw_inverse_factors(jax.random.fold_in(keys[5], 71), 0),
        "probes": normal_values(keys[3], (N_MP, OWN_SLOTS, BLOCK, BLOCK), 1.0, 6.0, ((0, 2), (2, 16))),
        "slot_table": draw_slot_table(jax.random.fold_in(keys[5], 71), 0),
    }


CLIP_RMS = 0.3
LEARN_RATE = 0.1
EPS_NORM = 1e-06

def product(left_op, right_op):
    return jnp.dot(left_op.astype(jnp.float32), right_op.astype(jnp.float32), precision=lax.Precision.HIGHEST)

def step_factor(factor, first_gram, second_gram):
    bound_value = jnp.max(jnp.abs(first_gram + second_gram)) + EPS_NORM
    change = jnp.triu(first_gram - second_gram).astype(jnp.bfloat16)
    moved_rows = product(change, factor)
    return (factor.astype(jnp.float32) - LEARN_RATE / bound_value * moved_rows).astype(jnp.bfloat16)

def update_block(gradient, left_q, right_q, left_inv, right_inv, probe_mat):
    left_times = product(left_q, gradient).astype(jnp.bfloat16)
    whitened = product(left_times, right_q.T).astype(jnp.bfloat16)
    half_conjugate = product(left_inv.T, probe_mat).astype(jnp.bfloat16)
    conjugate = product(half_conjugate, right_inv).astype(jnp.bfloat16)
    new_left = step_factor(left_q, product(whitened, whitened.T), product(conjugate, conjugate.T))
    new_right = step_factor(right_q, product(whitened.T, whitened), product(conjugate.T, conjugate))
    precond_left = product(new_left.T, new_left).astype(jnp.bfloat16)
    precond_right = product(new_right.T, new_right).astype(jnp.bfloat16)
    middle = product(precond_left, gradient).astype(jnp.bfloat16)
    result = product(middle, precond_right).astype(jnp.bfloat16)
    return (result, jnp.concatenate([new_left, new_right], axis=1))

def run_one(item_set):
    state = item_set[1]
    return update_block(item_set[0], state[:, :BLOCK], state[:, BLOCK:2 * BLOCK], state[:, 2 * BLOCK:3 * BLOCK], state[:, 3 * BLOCK:], item_set[2])

def reference(partial_grads, factors, inverse_factors, probes, slot_table):

    def accumulate(running, piece_dp):
        return (running + piece_dp.astype(jnp.float32), None)
    summed, _ = lax.scan(accumulate, jnp.zeros(partial_grads.shape[1:], jnp.float32), partial_grads)
    entry_count = EXPERTS * BROW * BLOCK * WCOLS
    squares = jnp.sum(summed * summed)
    clip_factor = jnp.minimum(1.0, CLIP_RMS * math.sqrt(entry_count) / jnp.sqrt(squares + EPS_NORM))
    clipped = (summed * clip_factor).astype(jnp.bfloat16)
    blocks = clipped.reshape(BLK_COL, BLOCK, N_MP, BLOCK).transpose(2, 0, 1, 3)
    results = []
    states = []
    for column in range(N_MP):
        table_row = slot_table[column].astype(jnp.int32)
        state_col = factors[column]
        combined = jnp.concatenate([state_col, inverse_factors[column]], axis=2)
        chosen = combined[table_row]
        chosen_probe = probes[column][table_row]
        block_out, factor_out = lax.map(run_one, (blocks[column], chosen, chosen_probe))
        results.append(block_out)
        states.append(state_col.at[table_row].set(factor_out))
    preconditioned = jnp.stack(results).transpose(1, 2, 0, 3).reshape(EXPERTS, BROW, BLOCK, WCOLS)
    return (preconditioned, jnp.stack(states))
```

```python
import math

import jax
import jax.numpy as jnp
from jax import lax
from jax.sharding import PartitionSpec as P

CLIP_RMS = 0.3
LEARN_RATE = 0.1
EPS_NORM = 1e-06


def product(left_op, right_op):
    return jnp.dot(left_op, right_op, preferred_element_type=jnp.float32)


def step_factor(factor, first_gram, second_gram):
    bound_value = jnp.max(jnp.abs(first_gram + second_gram)) + EPS_NORM
    change = jnp.triu(first_gram - second_gram).astype(jnp.bfloat16)
    moved_rows = product(change, factor)
    return (factor.astype(jnp.float32) - LEARN_RATE / bound_value * moved_rows).astype(jnp.bfloat16)


def flip(array, devices, mask):
    return lax.ppermute(array, "dp", [(i, i ^ mask) for i in range(devices)])


def pick(array, index, axis):
    return lax.dynamic_index_in_dim(array, index, axis, keepdims=False)


def unflip(pieces, own):
    stacked = jnp.stack(pieces)
    return jnp.stack([pick(stacked, own ^ k, 0) for k in range(len(pieces))])


def body(partial_grads, factors, inverse_factors, probes, slot_table):
    devices = lax.axis_size("dp")
    me = lax.axis_index("dp")
    experts, block_rows, block_size, columns = partial_grads.shape[1:]
    blocks = experts * block_rows
    group = devices // blocks
    rows = block_size // devices
    my_block = me // group
    my_place = me % group
    slot_row = slot_table[0]

    grads = partial_grads[0].reshape(blocks, blocks, group, rows, columns)
    sent = [flip(pick(grads, my_place ^ k, 2), devices, k) for k in range(1, group)]

    old_state = factors[0]
    wide = jnp.concatenate([old_state, inverse_factors[0], probes[0]], axis=2)
    chosen = jnp.take(wide, slot_row, axis=0)
    pieces = [pick(chosen, my_block, 0)] + [
        flip(pick(chosen, my_block ^ k, 0), devices, k * group) for k in range(1, blocks)
    ]
    quarter = unflip(pieces, my_block)

    total = pick(grads, my_place, 2).astype(jnp.float32)
    for piece in sent:
        total = total + piece.astype(jnp.float32)
    part = total.astype(jnp.bfloat16)
    mine = pick(part, my_block, 0).astype(jnp.float32)
    for k in range(1, blocks):
        mine = mine + flip(pick(part, my_block ^ k, 0), devices, k * group).astype(jnp.float32)
    grad_quarter = mine.astype(jnp.bfloat16)

    state = unflip([quarter] + [flip(quarter, devices, k) for k in range(1, group)], my_place)
    gradient = unflip(
        [grad_quarter] + [flip(grad_quarter, devices, k) for k in range(1, group)], my_place
    )
    state = state.transpose(1, 0, 2, 3).reshape(block_size, 5 * block_size)
    gradient = gradient.transpose(1, 0, 2, 3).reshape(block_size, columns)

    grad_wide = gradient.astype(jnp.float32)
    squares = jnp.full((8, 128), jnp.sum(grad_wide * grad_wide))
    for mask in range(lax.axis_size("mp").bit_length() - 1):
        squares = squares + lax.ppermute(
            squares, "mp", [(i, i ^ (1 << mask)) for i in range(lax.axis_size("mp"))]
        )
    others = [flip(squares, devices, k * group) for k in range(1, blocks)]
    for other in others:
        squares = squares + other
    entry_count = blocks * block_size * columns * lax.axis_size("mp")
    clip_factor = jnp.minimum(
        1.0, CLIP_RMS * math.sqrt(entry_count) / jnp.sqrt(squares[0, 0] + EPS_NORM)
    )

    left_q, right_q, left_inv, right_inv, probe_mat = jnp.split(state, 5, axis=1)
    half_conjugate = product(left_inv.T, probe_mat).astype(jnp.bfloat16)
    conjugate = product(half_conjugate, right_inv).astype(jnp.bfloat16)
    left_times = (clip_factor * product(left_q, gradient)).astype(jnp.bfloat16)
    whitened = product(left_times, right_q.T).astype(jnp.bfloat16)
    new_left = step_factor(left_q, product(whitened, whitened.T), product(conjugate, conjugate.T))
    new_right = step_factor(right_q, product(whitened.T, whitened), product(conjugate.T, conjugate))
    precond_right = product(new_right.T, new_right).astype(jnp.bfloat16)

    def my_rows(array):
        return pick(array.reshape(blocks, group, rows, -1), my_place, 1)

    left_columns = pick(new_left.reshape(block_size, blocks, group, rows), my_place, 2)
    left_columns = left_columns.reshape(block_size, blocks * rows)
    precond_left = product(left_columns.T, new_left).astype(jnp.bfloat16)
    middle = (clip_factor * product(precond_left, gradient)).astype(jnp.bfloat16)
    result = product(middle, precond_right).astype(jnp.bfloat16).reshape(blocks, rows, columns)

    back = jnp.concatenate([my_rows(new_left), my_rows(new_right), result], axis=2)
    back = [pick(back, my_block, 0)] + [
        flip(pick(back, my_block ^ k, 0), devices, k * group) for k in range(1, blocks)
    ]
    back = unflip(back, my_block)
    precond = back[:, :, 2 * block_size :].reshape(experts, block_rows, rows, columns)
    new_state = old_state.at[slot_row].set(back[:, :, : 2 * block_size])
    return (precond, new_state[None])


def solution(mesh):
    return jax.shard_map(
        body,
        mesh=mesh,
        in_specs=(
            P("dp", None, None, None, "mp"),
            P("mp", None, "dp", None),
            P("mp", None, "dp", None),
            P("mp", None, "dp", None),
            P("mp", None),
        ),
        out_specs=(P(None, None, "dp", "mp"), P("mp", None, "dp", None)),
        check_vma=False,
    )
```

```python
import functools
import math

import jax
import jax.numpy as jnp
from jax import lax
from jax.experimental import pallas as pl
from jax.experimental.pallas import tpu as pltpu
from jax.sharding import PartitionSpec as P

CLIP_RMS = 0.3
LEARN_RATE = 0.1
EPS_NORM = 1e-06
LANES = 128
FLOAT = jnp.float32
HALF = jnp.bfloat16


VMEM_SPEC = pl.BlockSpec(memory_space=pltpu.VMEM)
SMEM_SPEC = pl.BlockSpec(memory_space=pltpu.SMEM)


def product(left_op, right_op, left_dim=1, right_dim=0):
    return lax.dot_general(
        left_op, right_op, (((left_dim,), (right_dim,)), ((), ())), preferred_element_type=FLOAT
    )


def flip(array, devices, mask):
    return lax.ppermute(array, "dp", [(i, i ^ mask) for i in range(devices)])


def pick(array, index, axis):
    return lax.dynamic_index_in_dim(array, index, axis, keepdims=False)


def unflip(pieces, own):
    stacked = jnp.stack(pieces)
    return jnp.stack([pick(stacked, own ^ k, 0) for k in range(len(pieces))])


def call(kernel, out_shape, scratch, flops, smem, *operands):
    moved = sum(x.size * x.dtype.itemsize for x in (*operands, *jax.tree.leaves(out_shape)))
    return pl.pallas_call(
        kernel,
        out_shape=out_shape,
        in_specs=[SMEM_SPEC] * smem + [VMEM_SPEC] * (len(operands) - smem),
        out_specs=jax.tree.map(lambda _: VMEM_SPEC, out_shape),
        scratch_shapes=scratch,
        cost_estimate=pl.CostEstimate(flops=flops, bytes_accessed=moved, transcendentals=0),
    )(*operands)


class Plan:
    def __init__(self, devices, blocks, size):
        self.devices, self.blocks, self.size = devices, blocks, size
        self.group = devices // blocks
        self.rows = size // devices
        self.first = [z * (size // blocks) // LANES * LANES for z in range(blocks)]

    def spots(self):
        offset = 0
        for z in range(self.blocks):
            for what in range(5):
                first = self.first[z] if what < 4 else 0
                yield z, what, first, offset
                offset += self.size - first

    def packed(self):
        return sum(self.size - first for _, _, first, _ in self.spots())


def pack_kernel(plan, where, *refs):
    pieces, out, stack = refs[: plan.blocks], refs[-2], refs[-1]
    size = plan.size
    for k, piece in enumerate(pieces):
        stack[where[0] ^ k] = piece[...]
    for z, what, first, offset in plan.spots():
        out[:, offset : offset + size - first] = stack[z, :, what * size + first : (what + 1) * size]


def spread(plan, where, pieces, targets):
    size, rows = plan.size, plan.rows
    for z in range(1, plan.blocks):
        for target in targets[:4]:
            if target is not None and plan.first[z]:
                span = size // plan.blocks
                target[z * span : (z + 1) * span, : plan.first[z]] = jnp.zeros((span, plan.first[z]), HALF)
    for k, piece in enumerate(pieces):
        for z, what, first, offset in plan.spots():
            if targets[what] is not None:
                row = pl.multiple_of((z * plan.group + (where[1] ^ k)) * rows, rows)
                targets[what][pl.ds(row, rows), first:] = piece[:, offset : offset + size - first]


def probe_kernel(plan, where, *refs):
    pieces = refs[: plan.group]
    left, right, left_gram, right_gram, left_inv, right_inv, probe = refs[plan.group :]
    spread(plan, where, pieces, (left, right, left_inv, right_inv, probe))
    half_conjugate = product(left_inv[...], probe[...], 0, 0).astype(HALF)
    conjugate = product(half_conjugate, right_inv[...]).astype(HALF)
    left_gram[...] = product(conjugate, conjugate, 1, 1)
    right_gram[...] = product(conjugate, conjugate, 0, 0)


def sum_kernel(blocks, *refs):
    total = refs[0][...].astype(FLOAT)
    for ref in refs[1:blocks]:
        total = total + ref[...].astype(FLOAT)
    refs[blocks][...] = total.astype(HALF)
    squares = jnp.sum(total * total, axis=(0, 1))
    refs[blocks + 1][...] = jnp.full((8, LANES), jnp.sum(squares))


def bound_of(limit, squares):
    return jnp.minimum(1.0, limit / jnp.sqrt(squares + EPS_NORM))


def whiten_kernel(plan, limit, where, *refs):
    left, right, pieces = refs[0], refs[1], refs[2 : 2 + plan.group]
    grad, left_gram, right_gram, own_clip = refs[2 + plan.group :]
    for k, piece in enumerate(pieces):
        for z in range(plan.blocks):
            row = pl.multiple_of((z * plan.group + (where[1] ^ k)) * plan.rows, plan.rows)
            grad[pl.ds(row, plan.rows), :] = piece[z]
    wide = grad[...].astype(FLOAT)
    clip = bound_of(limit, jnp.sum(wide * wide, keepdims=True))
    own_clip[...] = jnp.broadcast_to(clip, own_clip.shape)
    left_times = (clip * product(left[...], grad[...])).astype(HALF)
    whitened = product(left_times, right[...], 1, 1).astype(HALF)
    left_gram[...] = product(whitened, whitened, 1, 1)
    right_gram[...] = product(whitened, whitened, 0, 0)


def step_factor(factor, ratio, first_ref, second_ref):
    first, second = ratio * first_ref[...], second_ref[...]
    bound_value = jnp.max(jnp.abs(first + second), keepdims=True) + EPS_NORM
    row = lax.broadcasted_iota(jnp.int32, first.shape, 0)
    column = lax.broadcasted_iota(jnp.int32, first.shape, 1)
    change = jnp.where(row <= column, first - second, 0.0).astype(HALF)
    moved_rows = product(change, factor)
    return (factor.astype(FLOAT) - LEARN_RATE / bound_value * moved_rows).astype(HALF)


def finish_kernel(plan, limit, where, *refs):
    sums, refs = refs[: plan.group], refs[plan.group :]
    own_clip, left, right, grad, left_p, right_p, left_q, right_q = refs[:8]
    outs, (new_left, new_right, square, result) = refs[8:-4], refs[-4:]
    squares = sums[0][0:1, 0:1]
    for ref in sums[1:]:
        squares = squares + ref[0:1, 0:1]
    clip = bound_of(limit, squares)
    ratio = clip / own_clip[0:1, 0:1]
    ratio = ratio * ratio
    size, rows = plan.size, plan.rows
    new_left[...] = step_factor(left[...], ratio, left_p, left_q)
    new_right[...] = step_factor(right[...], ratio, right_p, right_q)
    square[...] = product(new_left[...], new_left[...], 0, 0).astype(HALF)
    precond_right = product(new_right[...], new_right[...], 0, 0).astype(HALF)

    def at(z):
        return pl.ds(pl.multiple_of((z * plan.group + where[1]) * rows, rows), rows)

    precond_left = jnp.concatenate([square[at(z), :] for z in range(plan.blocks)], axis=0)
    middle = (clip * product(precond_left, grad[...])).astype(HALF)
    result[...] = product(middle, precond_right).astype(HALF).reshape(plan.blocks, rows, size)
    for k, out in enumerate(outs):
        z = where[0] ^ k
        out[:, :size] = new_left[at(z), :]
        out[:, size : 2 * size] = new_right[at(z), :]
        out[:, 2 * size :] = result[z]


def place_kernel(plan, where, slots, old_state, *refs):
    pieces, (precond, new_state) = refs[: plan.blocks], refs[plan.blocks :]
    size = plan.size
    new_state[...] = old_state[...]
    for k, piece in enumerate(pieces):
        precond[where[0] ^ k] = piece[:, 2 * size :]
        new_state[slots[where[0] ^ k]] = piece[:, : 2 * size]


def shaped(shape, dtype=HALF):
    return jax.ShapeDtypeStruct(shape, dtype)


def body(partial_grads, factors, inverse_factors, probes, slot_table):
    devices = lax.axis_size("dp")
    halves = lax.axis_size("mp")
    me = lax.axis_index("dp")
    experts, block_rows, size, columns = partial_grads.shape[1:]
    blocks = experts * block_rows
    plan = Plan(devices, blocks, size)
    group, rows = plan.group, plan.rows
    my_block = me // group
    my_place = me % group
    where = jnp.stack([my_block, my_place]).astype(jnp.int32)
    slot_row = slot_table[0]
    in_tiles = rows % 16 == 0
    limit = CLIP_RMS * math.sqrt(blocks * size * columns * halves)

    grads = partial_grads[0].reshape(blocks, blocks, group, rows, columns)
    sent = [flip(pick(grads, my_place ^ k, 2), devices, k) for k in range(1, group)]

    old_state = factors[0]
    wide = jnp.concatenate([old_state, inverse_factors[0], probes[0]], axis=2)
    chosen = jnp.take(wide, slot_row, axis=0)
    pieces = [pick(chosen, my_block, 0)] + [
        flip(pick(chosen, my_block ^ k, 0), devices, k * group) for k in range(1, blocks)
    ]
    if in_tiles:
        quarter = call(
            functools.partial(pack_kernel, plan),
            shaped((rows, plan.packed())),
            [pltpu.VMEM((blocks, rows, 5 * size), HALF)],
            0,
            1,
            where,
            *pieces,
        )
    else:
        quarter = unflip(pieces, my_block)

    total = pick(grads, my_place, 2).astype(FLOAT)
    for piece in sent:
        total = total + piece.astype(FLOAT)
    part = total.astype(HALF)
    parts = [pick(part, my_block, 0)] + [
        flip(pick(part, my_block ^ k, 0), devices, k * group) for k in range(1, blocks)
    ]
    grad_quarter, squares = call(
        functools.partial(sum_kernel, blocks),
        (shaped((blocks, rows, columns)), shaped((8, LANES), FLOAT)),
        [],
        0,
        0,
        *parts,
    )

    states = [quarter] + [flip(quarter, devices, k) for k in range(1, group)]
    quarters = [grad_quarter] + [flip(grad_quarter, devices, k) for k in range(1, group)]

    bit = 1
    while bit < halves:
        squares = squares + lax.ppermute(squares, "mp", [(i, i ^ bit) for i in range(halves)])
        bit *= 2
    bit = 1
    while bit < blocks:
        squares = squares + flip(squares, devices, bit * group)
        bit *= 2
    sums = [squares] + [flip(squares, devices, k) for k in range(1, group)]

    gram = shaped((size, size), FLOAT)
    square = shaped((size, size))
    matmul = 2 * size**3
    if in_tiles:
        left_q, right_q, left_c, right_c = call(
            functools.partial(probe_kernel, plan),
            (square, square, gram, gram),
            [pltpu.VMEM((size, size), HALF)] * 3,
            4 * matmul,
            1,
            where,
            *states,
        )
        gradient, left_w, right_w, own_clip = call(
            functools.partial(whiten_kernel, plan, limit),
            (shaped((size, columns)), gram, gram, shaped((8, LANES), FLOAT)),
            [],
            4 * matmul,
            1,
            where,
            left_q,
            right_q,
            *quarters,
        )
        back = call(
            functools.partial(finish_kernel, plan, limit),
            tuple(shaped((rows, 2 * size + columns)) for _ in range(blocks)),
            [pltpu.VMEM((size, size), HALF)] * 3 + [pltpu.VMEM((blocks, rows, columns), HALF)],
            5 * matmul,
            1,
            where,
            *sums,
            own_clip,
            left_q,
            right_q,
            gradient,
            left_w,
            right_w,
            left_c,
            right_c,
        )
    else:
        back = plain_block(plan, limit, my_block, my_place, sums, states, quarters)
    back = [back[0]] + [flip(back[k], devices, k * group) for k in range(1, blocks)]
    precond, new_state = call(
        functools.partial(place_kernel, plan),
        (shaped((blocks, rows, columns)), shaped(old_state.shape)),
        [],
        0,
        2,
        where,
        slot_row,
        old_state,
        *back,
    )
    return (precond.reshape(experts, block_rows, rows, columns), new_state[None])


def plain_block(plan, limit, my_block, my_place, sums, states, quarters):
    size, blocks, group, rows = plan.size, plan.blocks, plan.group, plan.rows
    state = unflip(states, my_place).transpose(1, 0, 2, 3).reshape(size, 5 * size)
    gradient = unflip(quarters, my_place).transpose(1, 0, 2, 3).reshape(size, -1)
    clip = bound_of(limit, functools.reduce(jnp.add, sums)[0:1, 0:1])
    left_q, right_q, left_inv, right_inv, probe_mat = jnp.split(state, 5, axis=1)
    half_conjugate = product(left_inv, probe_mat, 0, 0).astype(HALF)
    conjugate = product(half_conjugate, right_inv).astype(HALF)
    left_times = (clip * product(left_q, gradient)).astype(HALF)
    whitened = product(left_times, right_q, 1, 1).astype(HALF)
    new_left = step_factor(
        left_q, 1.0, product(whitened, whitened, 1, 1), product(conjugate, conjugate, 1, 1)
    )
    new_right = step_factor(
        right_q, 1.0, product(whitened, whitened, 0, 0), product(conjugate, conjugate, 0, 0)
    )
    precond_left = product(new_left, new_left, 0, 0).astype(HALF)
    precond_right = product(new_right, new_right, 0, 0).astype(HALF)

    def my_rows(array):
        return pick(array.reshape(blocks, group, rows, -1), my_place, 1)

    middle = (clip * product(my_rows(precond_left).reshape(blocks * rows, size), gradient)).astype(HALF)
    result = product(middle, precond_right).astype(HALF).reshape(blocks, rows, -1)
    back = jnp.concatenate([my_rows(new_left), my_rows(new_right), result], axis=2)
    return [pick(back, my_block ^ k, 0) for k in range(blocks)]


def solution(mesh):
    return jax.shard_map(
        body,
        mesh=mesh,
        in_specs=(
            P("dp", None, None, None, "mp"),
            P("mp", None, "dp", None),
            P("mp", None, "dp", None),
            P("mp", None, "dp", None),
            P("mp", None),
        ),
        out_specs=(P(None, None, "dp", "mp"), P("mp", None, "dp", None)),
        check_vma=False,
    )
```

```python
import functools
import math

import jax
import jax.numpy as jnp
from jax import lax
from jax.experimental import pallas as pl
from jax.experimental.pallas import tpu as pltpu
from jax.sharding import PartitionSpec as P

CLIP_RMS = 0.3
LEARN_RATE = 0.1
EPS_NORM = 1e-06
LANES = 128
VMEM_GRANT = 16 * 2**20
FLOAT = jnp.float32
HALF = jnp.bfloat16


VMEM_SPEC = pl.BlockSpec(memory_space=pltpu.VMEM)
SMEM_SPEC = pl.BlockSpec(memory_space=pltpu.SMEM)


def product(left_op, right_op, left_dim=1, right_dim=0):
    return lax.dot_general(
        left_op, right_op, (((left_dim,), (right_dim,)), ((), ())), preferred_element_type=FLOAT
    )


def flip(array, devices, mask):
    return lax.ppermute(array, "dp", [(i, i ^ mask) for i in range(devices)])


def pick(array, index, axis):
    return lax.dynamic_index_in_dim(array, index, axis, keepdims=False)


def unflip(pieces, own):
    stacked = jnp.stack(pieces)
    return jnp.stack([pick(stacked, own ^ k, 0) for k in range(len(pieces))])


def call(kernel, out_shape, scratch, flops, smem, *operands):
    moved = sum(x.size * x.dtype.itemsize for x in (*operands, *jax.tree.leaves(out_shape)))
    return pl.pallas_call(
        kernel,
        out_shape=out_shape,
        in_specs=[SMEM_SPEC] * smem + [VMEM_SPEC] * (len(operands) - smem),
        out_specs=jax.tree.map(lambda _: VMEM_SPEC, out_shape),
        scratch_shapes=scratch,
        cost_estimate=pl.CostEstimate(flops=flops, bytes_accessed=moved, transcendentals=0),
        compiler_params=pltpu.CompilerParams(vmem_limit_bytes=VMEM_GRANT),
    )(*operands)


class Plan:
    def __init__(self, devices, blocks, size):
        self.devices, self.blocks, self.size = devices, blocks, size
        self.group = devices // blocks
        self.rows = size // devices
        self.first = [z * (size // blocks) // LANES * LANES for z in range(blocks)]

    def spots(self):
        offset = 0
        for z in range(self.blocks):
            for what in range(5):
                first = self.first[z] if what < 4 else 0
                yield z, what, first, offset
                offset += self.size - first

    def packed(self):
        return sum(self.size - first for _, _, first, _ in self.spots())


def pack_kernel(plan, where, *refs):
    pieces, out, stack = refs[: plan.blocks], refs[-2], refs[-1]
    size = plan.size
    for k, piece in enumerate(pieces):
        stack[where[0] ^ k] = piece[...]
    for z, what, first, offset in plan.spots():
        out[:, offset : offset + size - first] = stack[z, :, what * size + first : (what + 1) * size]


def spread(plan, where, pieces, targets):
    size, rows = plan.size, plan.rows
    for z in range(1, plan.blocks):
        for target in targets[:4]:
            if target is not None and plan.first[z]:
                span = size // plan.blocks
                target[z * span : (z + 1) * span, : plan.first[z]] = jnp.zeros((span, plan.first[z]), HALF)
    for k, piece in enumerate(pieces):
        for z, what, first, offset in plan.spots():
            if targets[what] is not None:
                row = pl.multiple_of((z * plan.group + (where[1] ^ k)) * rows, rows)
                targets[what][pl.ds(row, rows), first:] = piece[:, offset : offset + size - first]


def probe_kernel(plan, where, *refs):
    pieces = refs[: plan.group]
    left, right, left_gram, right_gram, left_inv, right_inv, probe = refs[plan.group :]
    spread(plan, where, pieces, (left, right, left_inv, right_inv, probe))
    half_conjugate = product(left_inv[...], probe[...], 0, 0).astype(HALF)
    conjugate = product(half_conjugate, right_inv[...]).astype(HALF)
    left_gram[...] = product(conjugate, conjugate, 1, 1)
    right_gram[...] = product(conjugate, conjugate, 0, 0)


def sum_kernel(blocks, *refs):
    total = refs[0][...].astype(FLOAT)
    for ref in refs[1:blocks]:
        total = total + ref[...].astype(FLOAT)
    refs[blocks][...] = total.astype(HALF)
    squares = jnp.sum(total * total, axis=(0, 1))
    refs[blocks + 1][...] = jnp.full((8, LANES), jnp.sum(squares))


def bound_of(limit, squares):
    return jnp.minimum(1.0, limit / jnp.sqrt(squares + EPS_NORM))


def whiten_kernel(plan, limit, where, *refs):
    left, right, pieces = refs[0], refs[1], refs[2 : 2 + plan.group]
    grad, left_gram, right_gram, own_clip = refs[2 + plan.group :]
    for k, piece in enumerate(pieces):
        for z in range(plan.blocks):
            row = pl.multiple_of((z * plan.group + (where[1] ^ k)) * plan.rows, plan.rows)
            grad[pl.ds(row, plan.rows), :] = piece[z]
    wide = grad[...].astype(FLOAT)
    clip = bound_of(limit, jnp.sum(wide * wide, keepdims=True))
    own_clip[...] = jnp.broadcast_to(clip, own_clip.shape)
    left_times = (clip * product(left[...], grad[...])).astype(HALF)
    whitened = product(left_times, right[...], 1, 1).astype(HALF)
    left_gram[...] = product(whitened, whitened, 1, 1)
    right_gram[...] = product(whitened, whitened, 0, 0)


def step_factor(factor, ratio, first_ref, second_ref):
    first, second = ratio * first_ref[...], second_ref[...]
    bound_value = jnp.max(jnp.abs(first + second), keepdims=True) + EPS_NORM
    row = lax.broadcasted_iota(jnp.int32, first.shape, 0)
    column = lax.broadcasted_iota(jnp.int32, first.shape, 1)
    change = jnp.where(row <= column, first - second, 0.0).astype(HALF)
    moved_rows = product(change, factor)
    return (factor.astype(FLOAT) - LEARN_RATE / bound_value * moved_rows).astype(HALF)


def finish_kernel(plan, limit, where, *refs):
    sums, refs = refs[: plan.group], refs[plan.group :]
    own_clip, left, right, grad, left_p, right_p, left_q, right_q = refs[:8]
    outs, (new_left, new_right, square, result) = refs[8:-4], refs[-4:]
    squares = sums[0][0:1, 0:1]
    for ref in sums[1:]:
        squares = squares + ref[0:1, 0:1]
    clip = bound_of(limit, squares)
    ratio = clip / own_clip[0:1, 0:1]
    ratio = ratio * ratio
    size, rows = plan.size, plan.rows
    new_left[...] = step_factor(left[...], ratio, left_p, left_q)
    new_right[...] = step_factor(right[...], ratio, right_p, right_q)
    square[...] = product(new_left[...], new_left[...], 0, 0).astype(HALF)
    precond_right = product(new_right[...], new_right[...], 0, 0).astype(HALF)

    def at(z):
        return pl.ds(pl.multiple_of((z * plan.group + where[1]) * rows, rows), rows)

    precond_left = jnp.concatenate([square[at(z), :] for z in range(plan.blocks)], axis=0)
    middle = (clip * product(precond_left, grad[...])).astype(HALF)
    result[...] = product(middle, precond_right).astype(HALF).reshape(plan.blocks, rows, size)
    for k, out in enumerate(outs):
        z = where[0] ^ k
        out[:, :size] = new_left[at(z), :]
        out[:, size : 2 * size] = new_right[at(z), :]
        out[:, 2 * size :] = result[z]


def place_kernel(plan, where, slots, old_state, *refs):
    pieces, (precond, new_state) = refs[: plan.blocks], refs[plan.blocks :]
    size = plan.size
    new_state[...] = old_state[...]
    for k, piece in enumerate(pieces):
        precond[where[0] ^ k] = piece[:, 2 * size :]
        new_state[slots[where[0] ^ k]] = piece[:, : 2 * size]


def shaped(shape, dtype=HALF):
    return jax.ShapeDtypeStruct(shape, dtype)


def body(partial_grads, factors, inverse_factors, probes, slot_table):
    devices = lax.axis_size("dp")
    halves = lax.axis_size("mp")
    me = lax.axis_index("dp")
    experts, block_rows, size, columns = partial_grads.shape[1:]
    blocks = experts * block_rows
    plan = Plan(devices, blocks, size)
    group, rows = plan.group, plan.rows
    my_block = me // group
    my_place = me % group
    where = jnp.stack([my_block, my_place]).astype(jnp.int32)
    slot_row = slot_table[0]
    in_tiles = rows % 16 == 0
    limit = CLIP_RMS * math.sqrt(blocks * size * columns * halves)

    grads = partial_grads[0].reshape(blocks, blocks, group, rows, columns)
    sent = [flip(pick(grads, my_place ^ k, 2), devices, k) for k in range(1, group)]

    old_state = factors[0]
    wide = jnp.concatenate([old_state, inverse_factors[0], probes[0]], axis=2)
    chosen = jnp.take(wide, slot_row, axis=0)
    pieces = [pick(chosen, my_block, 0)] + [
        flip(pick(chosen, my_block ^ k, 0), devices, k * group) for k in range(1, blocks)
    ]
    if in_tiles:
        quarter = call(
            functools.partial(pack_kernel, plan),
            shaped((rows, plan.packed())),
            [pltpu.VMEM((blocks, rows, 5 * size), HALF)],
            0,
            1,
            where,
            *pieces,
        )
    else:
        quarter = unflip(pieces, my_block)

    total = pick(grads, my_place, 2).astype(FLOAT)
    for piece in sent:
        total = total + piece.astype(FLOAT)
    part = total.astype(HALF)
    parts = [pick(part, my_block, 0)] + [
        flip(pick(part, my_block ^ k, 0), devices, k * group) for k in range(1, blocks)
    ]
    grad_quarter, squares = call(
        functools.partial(sum_kernel, blocks),
        (shaped((blocks, rows, columns)), shaped((8, LANES), FLOAT)),
        [],
        0,
        0,
        *parts,
    )

    states = [quarter] + [flip(quarter, devices, k) for k in range(1, group)]
    quarters = [grad_quarter] + [flip(grad_quarter, devices, k) for k in range(1, group)]

    bit = 1
    while bit < halves:
        squares = squares + lax.ppermute(squares, "mp", [(i, i ^ bit) for i in range(halves)])
        bit *= 2
    bit = 1
    while bit < blocks:
        squares = squares + flip(squares, devices, bit * group)
        bit *= 2
    sums = [squares] + [flip(squares, devices, k) for k in range(1, group)]

    gram = shaped((size, size), FLOAT)
    square = shaped((size, size))
    matmul = 2 * size**3
    if in_tiles:
        left_q, right_q, left_c, right_c = call(
            functools.partial(probe_kernel, plan),
            (square, square, gram, gram),
            [pltpu.VMEM((size, size), HALF)] * 3,
            4 * matmul,
            1,
            where,
            *states,
        )
        gradient, left_w, right_w, own_clip = call(
            functools.partial(whiten_kernel, plan, limit),
            (shaped((size, columns)), gram, gram, shaped((8, LANES), FLOAT)),
            [],
            4 * matmul,
            1,
            where,
            left_q,
            right_q,
            *quarters,
        )
        back = call(
            functools.partial(finish_kernel, plan, limit),
            tuple(shaped((rows, 2 * size + columns)) for _ in range(blocks)),
            [pltpu.VMEM((size, size), HALF)] * 3 + [pltpu.VMEM((blocks, rows, columns), HALF)],
            5 * matmul,
            1,
            where,
            *sums,
            own_clip,
            left_q,
            right_q,
            gradient,
            left_w,
            right_w,
            left_c,
            right_c,
        )
    else:
        back = plain_block(plan, limit, my_block, my_place, sums, states, quarters)
    back = [back[0]] + [flip(back[k], devices, k * group) for k in range(1, blocks)]
    precond, new_state = call(
        functools.partial(place_kernel, plan),
        (shaped((blocks, rows, columns)), shaped(old_state.shape)),
        [],
        0,
        2,
        where,
        slot_row,
        old_state,
        *back,
    )
    return (precond.reshape(experts, block_rows, rows, columns), new_state[None])


def plain_block(plan, limit, my_block, my_place, sums, states, quarters):
    size, blocks, group, rows = plan.size, plan.blocks, plan.group, plan.rows
    state = unflip(states, my_place).transpose(1, 0, 2, 3).reshape(size, 5 * size)
    gradient = unflip(quarters, my_place).transpose(1, 0, 2, 3).reshape(size, -1)
    clip = bound_of(limit, functools.reduce(jnp.add, sums)[0:1, 0:1])
    left_q, right_q, left_inv, right_inv, probe_mat = jnp.split(state, 5, axis=1)
    half_conjugate = product(left_inv, probe_mat, 0, 0).astype(HALF)
    conjugate = product(half_conjugate, right_inv).astype(HALF)
    left_times = (clip * product(left_q, gradient)).astype(HALF)
    whitened = product(left_times, right_q, 1, 1).astype(HALF)
    new_left = step_factor(
        left_q, 1.0, product(whitened, whitened, 1, 1), product(conjugate, conjugate, 1, 1)
    )
    new_right = step_factor(
        right_q, 1.0, product(whitened, whitened, 0, 0), product(conjugate, conjugate, 0, 0)
    )
    precond_left = product(new_left, new_left, 0, 0).astype(HALF)
    precond_right = product(new_right, new_right, 0, 0).astype(HALF)

    def my_rows(array):
        return pick(array.reshape(blocks, group, rows, -1), my_place, 1)

    middle = (clip * product(my_rows(precond_left).reshape(blocks * rows, size), gradient)).astype(HALF)
    result = product(middle, precond_right).astype(HALF).reshape(blocks, rows, -1)
    back = jnp.concatenate([my_rows(new_left), my_rows(new_right), result], axis=2)
    return [pick(back, my_block ^ k, 0) for k in range(blocks)]


def solution(mesh):
    return jax.shard_map(
        body,
        mesh=mesh,
        in_specs=(
            P("dp", None, None, None, "mp"),
            P("mp", None, "dp", None),
            P("mp", None, "dp", None),
            P("mp", None, "dp", None),
            P("mp", None),
        ),
        out_specs=(P(None, None, "dp", "mp"), P("mp", None, "dp", None)),
        check_vma=False,
    )
```

```python
import functools
import math

import jax
import jax.numpy as jnp
from jax import lax
from jax.experimental import pallas as pl
from jax.experimental.pallas import tpu as pltpu
from jax.sharding import PartitionSpec as P

CLIP_RMS = 0.3
LEARN_RATE = 0.1
EPS_NORM = 1e-06
LANES = 128
CHUNKS = 2
VMEM_GRANT = 16 * 2**20
FLOAT = jnp.float32
HALF = jnp.bfloat16


VMEM_SPEC = pl.BlockSpec(memory_space=pltpu.VMEM)
SMEM_SPEC = pl.BlockSpec(memory_space=pltpu.SMEM)


def product(left_op, right_op, left_dim=1, right_dim=0):
    return lax.dot_general(
        left_op, right_op, (((left_dim,), (right_dim,)), ((), ())), preferred_element_type=FLOAT
    )


def pick(array, index, axis):
    return lax.dynamic_index_in_dim(array, index, axis, keepdims=False)


def unflip(pieces, own):
    stacked = jnp.stack(pieces)
    return jnp.stack([pick(stacked, own ^ k, 0) for k in range(len(pieces))])


def call(kernel, out_shape, scratch, flops, smem, *operands):
    moved = sum(x.size * x.dtype.itemsize for x in (*operands, *jax.tree.leaves(out_shape)))
    return pl.pallas_call(
        kernel,
        out_shape=out_shape,
        in_specs=[SMEM_SPEC] * smem + [VMEM_SPEC] * (len(operands) - smem),
        out_specs=jax.tree.map(lambda _: VMEM_SPEC, out_shape),
        scratch_shapes=scratch,
        cost_estimate=pl.CostEstimate(flops=flops, bytes_accessed=moved, transcendentals=0),
        compiler_params=pltpu.CompilerParams(vmem_limit_bytes=VMEM_GRANT),
    )(*operands)


class Plan:
    def __init__(self, devices, halves, blocks, size):
        self.devices, self.halves, self.blocks, self.size = devices, halves, blocks, size
        self.group = devices // blocks
        self.parts = self.group // halves
        self.rows = size // devices
        self.first = [z * (size // blocks) // LANES * LANES for z in range(blocks)]

    def owns(self, device, column):
        return device % self.halves == column

    def send(self, array, mask, source=False, target=False, column=0):
        pairs = [
            (d * self.halves + m, (d ^ mask) * self.halves + (m ^ column))
            for d in range(self.devices)
            for m in range(self.halves)
            if (not source or self.owns(d, m)) and (not target or self.owns(d ^ mask, m ^ column))
        ]
        return lax.ppermute(array, ("dp", "mp"), pairs)

    def spots(self):
        offset = 0
        for z in range(self.blocks):
            for what in range(5):
                first = self.first[z] if what < 4 else 0
                yield z, what, first, offset
                offset += self.size - first

    def packed(self):
        return sum(self.size - first for _, _, first, _ in self.spots())


def pack_kernel(plan, where, *refs):
    pieces, out, stack = refs[: plan.blocks], refs[-2], refs[-1]
    size = plan.size
    for k, piece in enumerate(pieces):
        stack[where[0] ^ k] = piece[...]
    for z, what, first, offset in plan.spots():
        out[:, offset : offset + size - first] = stack[z, :, what * size + first : (what + 1) * size]


def spread(plan, where, pieces, targets):
    size, rows = plan.size, plan.rows
    for z in range(1, plan.blocks):
        for target in targets[:4]:
            if target is not None and plan.first[z]:
                span = size // plan.blocks
                target[z * span : (z + 1) * span, : plan.first[z]] = jnp.zeros((span, plan.first[z]), HALF)
    for k, piece in enumerate(pieces):
        for z, what, first, offset in plan.spots():
            if targets[what] is not None:
                row = pl.multiple_of((z * plan.group + (where[1] ^ k)) * rows, rows)
                targets[what][pl.ds(row, rows), first:] = piece[:, offset : offset + size - first]


def probe_kernel(plan, where, *refs):
    pieces = refs[: plan.group]
    left, right, left_gram, right_gram, left_inv, right_inv, probe = refs[plan.group :]
    spread(plan, where, pieces, (left, right, left_inv, right_inv, probe))
    half_conjugate = product(left_inv[...], probe[...], 0, 0).astype(HALF)
    conjugate = product(half_conjugate, right_inv[...]).astype(HALF)
    left_gram[...] = product(conjugate, conjugate, 1, 1)
    right_gram[...] = product(conjugate, conjugate, 0, 0)


def gather_kernel(plan, where, *refs):
    terms, outs = refs[: plan.group], refs[plan.group :]
    for k, out in enumerate(outs):
        block = where[0] ^ k
        total = terms[0][block].astype(FLOAT)
        for term in terms[1:]:
            total = total + term[block].astype(FLOAT)
        out[...] = total.astype(HALF)


def sum_kernel(blocks, *refs):
    terms, (out, squares) = refs[:-2], refs[-2:]
    found, start = 0.0, 0
    for i in range(0, len(terms), blocks):
        total = terms[i][...].astype(FLOAT)
        for term in terms[i + 1 : i + blocks]:
            total = total + term[...].astype(FLOAT)
        out[start : start + total.shape[0]] = total.astype(HALF)
        start += total.shape[0]
        found = found + jnp.sum(jnp.sum(total * total, axis=(0, 1)))
    squares[...] = jnp.full(squares.shape, found)


def bound_of(limit, squares):
    return jnp.minimum(1.0, limit / jnp.sqrt(squares + EPS_NORM))


def whiten_kernel(plan, limit, where, *refs):
    left, right, pieces = refs[0], refs[1], refs[2 : 2 + plan.parts]
    grad, left_gram, right_gram, own_clip = refs[2 + plan.parts :]
    span = plan.halves * plan.rows
    for k, piece in enumerate(pieces):
        for z in range(plan.blocks):
            row = pl.multiple_of((z * plan.parts + (where[2] ^ k)) * span, span)
            grad[pl.ds(row, span), :] = piece[z]
    wide = grad[...].astype(FLOAT)
    clip = bound_of(limit, jnp.sum(wide * wide, keepdims=True))
    own_clip[...] = jnp.broadcast_to(clip, own_clip.shape)
    left_times = (clip * product(left[...], grad[...])).astype(HALF)
    whitened = product(left_times, right[...], 1, 1).astype(HALF)
    left_gram[...] = product(whitened, whitened, 1, 1)
    right_gram[...] = product(whitened, whitened, 0, 0)


def step_factor(factor, ratio, first_ref, second_ref):
    first, second = ratio * first_ref[...], second_ref[...]
    bound_value = jnp.max(jnp.abs(first + second), keepdims=True) + EPS_NORM
    row = lax.broadcasted_iota(jnp.int32, first.shape, 0)
    column = lax.broadcasted_iota(jnp.int32, first.shape, 1)
    change = jnp.where(row <= column, first - second, 0.0).astype(HALF)
    moved_rows = product(change, factor)
    return (factor.astype(FLOAT) - LEARN_RATE / bound_value * moved_rows).astype(HALF)


def finish_kernel(plan, limit, where, *refs):
    sums, refs = refs[: plan.blocks], refs[plan.blocks :]
    own_clip, left, right, grad, left_p, right_p, left_q, right_q = refs[:8]
    outs, (new_left, new_right, square, result) = refs[8:-4], refs[-4:]
    squares = sums[0][0:1, 0:1]
    for ref in sums[1:]:
        squares = squares + ref[0:1, 0:1]
    clip = bound_of(limit, squares)
    ratio = clip / own_clip[0:1, 0:1]
    ratio = ratio * ratio
    size, rows = plan.size, plan.rows
    span = plan.halves * rows
    new_left[...] = step_factor(left[...], ratio, left_p, left_q)
    new_right[...] = step_factor(right[...], ratio, right_p, right_q)
    square[...] = product(new_left[...], new_left[...], 0, 0).astype(HALF)
    precond_right = product(new_right[...], new_right[...], 0, 0).astype(HALF)

    def part(z):
        return pl.ds(pl.multiple_of((z * plan.parts + where[2]) * span, span), span)

    precond_left = jnp.concatenate([square[part(z), :] for z in range(plan.blocks)], axis=0)
    middle = (clip * product(precond_left, grad[...])).astype(HALF)
    done = product(middle, precond_right).astype(HALF)
    result[...] = done.reshape(plan.blocks * plan.halves, rows, size)
    for i, out in enumerate(outs):
        z, low = where[0] ^ (i // plan.halves), where[3] ^ (i % plan.halves)
        row = pl.ds(pl.multiple_of((z * plan.group + where[2] * plan.halves + low) * rows, rows), rows)
        out[:, :size] = new_left[row, :]
        out[:, size : 2 * size] = new_right[row, :]
        out[:, 2 * size :] = result[z * plan.halves + low]


def place_kernel(plan, where, slots, old_state, *refs):
    pieces, (precond, new_state) = refs[:-2], refs[-2:]
    size = plan.size
    new_state[...] = old_state[...]
    for i, piece in enumerate(pieces):

        @pl.when(where[4] == i % plan.halves)
        def _(i=i, piece=piece):
            block = where[0] ^ (i // plan.halves)
            precond[block] = piece[:, 2 * size :]
            new_state[slots[block]] = piece[:, : 2 * size]


def shaped(shape, dtype=HALF):
    return jax.ShapeDtypeStruct(shape, dtype)


def body(partial_grads, factors, inverse_factors, probes, slot_table):
    devices = lax.axis_size("dp")
    halves = lax.axis_size("mp")
    me = lax.axis_index("dp")
    column = lax.axis_index("mp")
    experts, block_rows, size, columns = partial_grads.shape[1:]
    blocks = experts * block_rows
    plan = Plan(devices, halves, blocks, size)
    group, rows, parts = plan.group, plan.rows, plan.parts
    span = halves * rows
    my_block = me // group
    my_place = me % group
    my_part = my_place // halves
    my_low = my_place % halves
    where = jnp.stack([my_block, my_place, my_part, my_low, my_low ^ column]).astype(jnp.int32)
    slot_row = slot_table[0]
    in_tiles = rows % 16 == 0
    limit = CLIP_RMS * math.sqrt(blocks * size * columns * halves)

    grads = partial_grads[0].reshape(blocks, blocks, parts, span, columns)
    chunks = []
    step = blocks // CHUNKS
    for start in range(0, blocks, step):
        chunk = grads[:, start : start + step]
        rows_of = [pick(chunk, my_part ^ k, 2) for k in range(parts)]
        chunks.append(
            [rows_of[0]]
            + [plan.send(rows_of[k // halves], k, target=True) for k in range(1, group)]
        )

    old_state = factors[0]
    wide = jnp.concatenate([old_state, inverse_factors[0], probes[0]], axis=2)
    chosen = jnp.take(wide, slot_row, axis=0)
    pieces = [pick(chosen, my_block, 0)] + [
        plan.send(pick(chosen, my_block ^ k, 0), k * group) for k in range(1, blocks)
    ]
    if in_tiles:
        quarter = call(
            functools.partial(pack_kernel, plan),
            shaped((rows, plan.packed())),
            [pltpu.VMEM((blocks, rows, 5 * size), HALF)],
            0,
            1,
            where,
            *pieces,
        )
    else:
        quarter = unflip(pieces, my_block)

    terms = []
    for chunk in chunks:
        mine = call(
            functools.partial(gather_kernel, plan),
            tuple(shaped((step, span, columns)) for _ in range(blocks)),
            [],
            0,
            1,
            where,
            *chunk,
        )
        terms += [mine[0]] + [plan.send(mine[k], k * group, source=True) for k in range(1, blocks)]
    grad_part, squares = call(
        functools.partial(sum_kernel, blocks),
        (shaped((blocks, span, columns)), shaped((8, LANES), FLOAT)),
        [],
        0,
        0,
        *terms,
    )

    states = [quarter] + [plan.send(quarter, k, target=True) for k in range(1, group)]
    grad_parts = [grad_part] + [
        plan.send(grad_part, k * halves, source=True) for k in range(1, parts)
    ]
    near = [squares] + [
        plan.send(squares, k, source=True, column=k % halves) for k in range(1, group)
    ]
    squares = functools.reduce(jnp.add, near)
    sums = [squares] + [plan.send(squares, k * group, source=True) for k in range(1, blocks)]

    gram = shaped((size, size), FLOAT)
    square = shaped((size, size))
    matmul = 2 * size**3
    if in_tiles:
        left_q, right_q, left_c, right_c = call(
            functools.partial(probe_kernel, plan),
            (square, square, gram, gram),
            [pltpu.VMEM((size, size), HALF)] * 3,
            4 * matmul,
            1,
            where,
            *states,
        )
        gradient, left_w, right_w, own_clip = call(
            functools.partial(whiten_kernel, plan, limit),
            (shaped((size, columns)), gram, gram, shaped((8, LANES), FLOAT)),
            [],
            4 * matmul,
            1,
            where,
            left_q,
            right_q,
            *grad_parts,
        )
        back = call(
            functools.partial(finish_kernel, plan, limit),
            tuple(shaped((rows, 2 * size + columns)) for _ in range(blocks * halves)),
            [pltpu.VMEM((size, size), HALF)] * 3
            + [pltpu.VMEM((blocks * halves, rows, columns), HALF)],
            5 * matmul,
            1,
            where,
            *sums,
            own_clip,
            left_q,
            right_q,
            gradient,
            left_w,
            right_w,
            left_c,
            right_c,
        )
    else:
        back = plain_block(plan, limit, my_block, my_place, sums, states, grad_parts)
    back = [back[0]] + [
        plan.send(back[i], i // halves * group + i % halves, source=True)
        for i in range(1, blocks * halves)
    ]
    precond, new_state = call(
        functools.partial(place_kernel, plan),
        (shaped((blocks, rows, columns)), shaped(old_state.shape)),
        [],
        0,
        2,
        where,
        slot_row,
        old_state,
        *back,
    )
    return (precond.reshape(experts, block_rows, rows, columns), new_state[None])


def plain_block(plan, limit, my_block, my_place, sums, states, grad_parts):
    size, blocks, group, rows, halves = plan.size, plan.blocks, plan.group, plan.rows, plan.halves
    state = unflip(states, my_place).transpose(1, 0, 2, 3).reshape(size, 5 * size)
    gradient = unflip(grad_parts, my_place // halves).transpose(1, 0, 2, 3).reshape(size, -1)
    clip = bound_of(limit, functools.reduce(jnp.add, sums)[0:1, 0:1])
    left_q, right_q, left_inv, right_inv, probe_mat = jnp.split(state, 5, axis=1)
    half_conjugate = product(left_inv, probe_mat, 0, 0).astype(HALF)
    conjugate = product(half_conjugate, right_inv).astype(HALF)
    left_times = (clip * product(left_q, gradient)).astype(HALF)
    whitened = product(left_times, right_q, 1, 1).astype(HALF)
    new_left = step_factor(
        left_q, 1.0, product(whitened, whitened, 1, 1), product(conjugate, conjugate, 1, 1)
    )
    new_right = step_factor(
        right_q, 1.0, product(whitened, whitened, 0, 0), product(conjugate, conjugate, 0, 0)
    )
    precond_left = product(new_left, new_left, 0, 0).astype(HALF)
    precond_right = product(new_right, new_right, 0, 0).astype(HALF)
    middle = (clip * product(precond_left, gradient)).astype(HALF)
    result = product(middle, precond_right).astype(HALF)
    back = jnp.concatenate([new_left, new_right, result], axis=1)
    back = back.reshape(blocks, group, rows, -1)
    return [
        pick(pick(back, my_block ^ (i // halves), 0), my_place ^ (i % halves), 0)
        for i in range(blocks * halves)
    ]


def solution(mesh):
    return jax.shard_map(
        body,
        mesh=mesh,
        in_specs=(
            P("dp", None, None, None, "mp"),
            P("mp", None, "dp", None),
            P("mp", None, "dp", None),
            P("mp", None, "dp", None),
            P("mp", None),
        ),
        out_specs=(P(None, None, "dp", "mp"), P("mp", None, "dp", None)),
        check_vma=False,
    )
```

```python
import functools
import math

import jax
import jax.numpy as jnp
from jax import lax
from jax.experimental import pallas as pl
from jax.experimental.pallas import tpu as pltpu
from jax.sharding import PartitionSpec as P

CLIP_RMS = 0.3
LEARN_RATE = 0.1
EPS_NORM = 1e-06
LANES = 128
CHUNKS = 1
VMEM_GRANT = 16 * 2**20
FLOAT = jnp.float32
HALF = jnp.bfloat16


VMEM_SPEC = pl.BlockSpec(memory_space=pltpu.VMEM)
SMEM_SPEC = pl.BlockSpec(memory_space=pltpu.SMEM)


def product(left_op, right_op, left_dim=1, right_dim=0):
    return lax.dot_general(
        left_op, right_op, (((left_dim,), (right_dim,)), ((), ())), preferred_element_type=FLOAT
    )


def pick(array, index, axis):
    return lax.dynamic_index_in_dim(array, index, axis, keepdims=False)


def unflip(pieces, own):
    stacked = jnp.stack(pieces)
    return jnp.stack([pick(stacked, own ^ k, 0) for k in range(len(pieces))])


def call(kernel, out_shape, scratch, flops, smem, *operands):
    moved = sum(x.size * x.dtype.itemsize for x in (*operands, *jax.tree.leaves(out_shape)))
    return pl.pallas_call(
        kernel,
        out_shape=out_shape,
        in_specs=[SMEM_SPEC] * smem + [VMEM_SPEC] * (len(operands) - smem),
        out_specs=jax.tree.map(lambda _: VMEM_SPEC, out_shape),
        scratch_shapes=scratch,
        cost_estimate=pl.CostEstimate(flops=flops, bytes_accessed=moved, transcendentals=0),
        compiler_params=pltpu.CompilerParams(vmem_limit_bytes=VMEM_GRANT),
    )(*operands)


class Plan:
    def __init__(self, devices, halves, blocks, size):
        self.devices, self.halves, self.blocks, self.size = devices, halves, blocks, size
        self.group = devices // blocks
        self.parts = self.group // halves
        self.rows = size // devices
        self.first = [z * (size // blocks) // LANES * LANES for z in range(blocks)]

    def route(self, array, block=0, high=0, low=0, column=0, swap=False):
        pairs = []
        for d in range(self.devices):
            for m in range(self.halves):
                b, h, l = d // self.group, d % self.group // self.halves, d % self.halves
                l2, m2 = (m, l) if swap else (l, m)
                to = ((b ^ block) * self.parts + (h ^ high)) * self.halves + (l2 ^ low)
                pairs.append((d * self.halves + m, to * self.halves + (m2 ^ column)))
        return lax.ppermute(array, ("dp", "mp"), pairs)

    def spots(self):
        offset = 0
        for z in range(self.blocks):
            for what in range(5):
                first = self.first[z] if what < 4 else 0
                yield z, what, first, offset
                offset += self.size - first

    def packed(self):
        return sum(self.size - first for _, _, first, _ in self.spots())


def pack_kernel(plan, where, *refs):
    pieces, out, stack = refs[: plan.blocks], refs[-2], refs[-1]
    size = plan.size
    for k, piece in enumerate(pieces):
        stack[where[0] ^ k] = piece[...]
    for z, what, first, offset in plan.spots():
        out[:, offset : offset + size - first] = stack[z, :, what * size + first : (what + 1) * size]


def spread(plan, where, pieces, targets):
    size, rows = plan.size, plan.rows
    for z in range(1, plan.blocks):
        for target in targets[:4]:
            if target is not None and plan.first[z]:
                span = size // plan.blocks
                target[z * span : (z + 1) * span, : plan.first[z]] = jnp.zeros((span, plan.first[z]), HALF)
    for k, piece in enumerate(pieces):
        for z, what, first, offset in plan.spots():
            if targets[what] is not None:
                row = pl.multiple_of((z * plan.group + (where[1] ^ k)) * rows, rows)
                targets[what][pl.ds(row, rows), first:] = piece[:, offset : offset + size - first]


def probe_kernel(plan, where, *refs):
    pieces = refs[: plan.group]
    left, right, left_gram, right_gram, left_inv, right_inv, probe = refs[plan.group :]
    spread(plan, where, pieces, (left, right, left_inv, right_inv, probe))
    half_conjugate = product(left_inv[...], probe[...], 0, 0).astype(HALF)
    conjugate = product(half_conjugate, right_inv[...]).astype(HALF)
    left_gram[...] = product(conjugate, conjugate, 1, 1)
    right_gram[...] = product(conjugate, conjugate, 0, 0)


def gather_kernel(plan, where, *refs):
    terms, outs = refs[: plan.group], refs[plan.group :]
    for k, out in enumerate(outs):
        block = where[0] ^ k
        total = terms[0][block].astype(FLOAT)
        for term in terms[1:]:
            total = total + term[block].astype(FLOAT)
        out[...] = total.astype(HALF)


def sum_kernel(blocks, *refs):
    terms, (out, squares) = refs[:-2], refs[-2:]
    found, start = 0.0, 0
    for i in range(0, len(terms), blocks):
        total = terms[i][...].astype(FLOAT)
        for term in terms[i + 1 : i + blocks]:
            total = total + term[...].astype(FLOAT)
        out[start : start + total.shape[0]] = total.astype(HALF)
        start += total.shape[0]
        found = found + jnp.sum(jnp.sum(total * total, axis=(0, 1)))
    squares[...] = jnp.full(squares.shape, found)


def bound_of(limit, squares):
    return jnp.minimum(1.0, limit / jnp.sqrt(squares + EPS_NORM))


def whiten_kernel(plan, limit, where, *refs):
    left, right, pieces = refs[0], refs[1], refs[2 : 2 + plan.group]
    grad, left_gram, right_gram, own_clip = refs[2 + plan.group :]
    for k, piece in enumerate(pieces):
        for z in range(plan.blocks):
            row = pl.multiple_of((z * plan.group + (where[1] ^ k)) * plan.rows, plan.rows)
            grad[pl.ds(row, plan.rows), :] = piece[z]
    wide = grad[...].astype(FLOAT)
    clip = bound_of(limit, jnp.sum(wide * wide, keepdims=True))
    own_clip[...] = jnp.broadcast_to(clip, own_clip.shape)
    left_times = (clip * product(left[...], grad[...])).astype(HALF)
    whitened = product(left_times, right[...], 1, 1).astype(HALF)
    left_gram[...] = product(whitened, whitened, 1, 1)
    right_gram[...] = product(whitened, whitened, 0, 0)


def step_factor(factor, ratio, first_ref, second_ref):
    first, second = ratio * first_ref[...], second_ref[...]
    bound_value = jnp.max(jnp.abs(first + second), keepdims=True) + EPS_NORM
    row = lax.broadcasted_iota(jnp.int32, first.shape, 0)
    column = lax.broadcasted_iota(jnp.int32, first.shape, 1)
    change = jnp.where(row <= column, first - second, 0.0).astype(HALF)
    moved_rows = product(change, factor)
    return (factor.astype(FLOAT) - LEARN_RATE / bound_value * moved_rows).astype(HALF)


def finish_kernel(plan, limit, where, *refs):
    sums, refs = refs[: plan.group], refs[plan.group :]
    own_clip, left, right, grad, left_p, right_p, left_q, right_q = refs[:8]
    outs, (new_left, new_right, square, result) = refs[8:-4], refs[-4:]
    squares = sums[0][0:1, 0:1]
    for ref in sums[1:]:
        squares = squares + ref[0:1, 0:1]
    clip = bound_of(limit, squares)
    ratio = clip / own_clip[0:1, 0:1]
    ratio = ratio * ratio
    size, rows = plan.size, plan.rows
    new_left[...] = step_factor(left[...], ratio, left_p, left_q)
    new_right[...] = step_factor(right[...], ratio, right_p, right_q)
    square[...] = product(new_left[...], new_left[...], 0, 0).astype(HALF)
    precond_right = product(new_right[...], new_right[...], 0, 0).astype(HALF)

    def at(z):
        return pl.ds(pl.multiple_of((z * plan.group + where[1]) * rows, rows), rows)

    precond_left = jnp.concatenate([square[at(z), :] for z in range(plan.blocks)], axis=0)
    middle = (clip * product(precond_left, grad[...])).astype(HALF)
    result[...] = product(middle, precond_right).astype(HALF).reshape(plan.blocks, rows, size)
    for k, out in enumerate(outs):
        z = where[0] ^ k
        out[:, :size] = new_left[at(z), :]
        out[:, size : 2 * size] = new_right[at(z), :]
        out[:, 2 * size :] = result[z]


def place_kernel(plan, where, slots, old_state, *refs):
    pieces, (precond, new_state) = refs[: plan.blocks], refs[plan.blocks :]
    size = plan.size
    new_state[...] = old_state[...]
    for k, piece in enumerate(pieces):
        precond[where[0] ^ k] = piece[:, 2 * size :]
        new_state[slots[where[0] ^ k]] = piece[:, : 2 * size]


def shaped(shape, dtype=HALF):
    return jax.ShapeDtypeStruct(shape, dtype)


def body(partial_grads, factors, inverse_factors, probes, slot_table):
    devices = lax.axis_size("dp")
    halves = lax.axis_size("mp")
    me = lax.axis_index("dp")
    column = lax.axis_index("mp")
    experts, block_rows, size, columns = partial_grads.shape[1:]
    blocks = experts * block_rows
    plan = Plan(devices, halves, blocks, size)
    group, rows, parts = plan.group, plan.rows, plan.parts
    my_block = me // group
    my_place = me % group
    work_place = my_place // halves * halves + column
    where = jnp.stack([my_block, work_place]).astype(jnp.int32)
    slot_row = slot_table[0]
    in_tiles = rows % 16 == 0
    limit = CLIP_RMS * math.sqrt(blocks * size * columns * halves)

    grads = partial_grads[0].reshape(blocks, blocks, group, rows, columns)
    step = blocks // CHUNKS
    chunks = [
        [
            plan.route(
                pick(grads[:, start : start + step], my_place ^ k, 2),
                high=k // halves,
                column=k % halves,
                swap=True,
            )
            for k in range(group)
        ]
        for start in range(0, blocks, step)
    ]

    old_state = factors[0]
    wide = jnp.concatenate([old_state, inverse_factors[0], probes[0]], axis=2)
    chosen = jnp.take(wide, slot_row, axis=0)
    pieces = [pick(chosen, my_block, 0)] + [
        plan.route(pick(chosen, my_block ^ k, 0), block=k) for k in range(1, blocks)
    ]
    if in_tiles:
        quarter = call(
            functools.partial(pack_kernel, plan),
            shaped((rows, plan.packed())),
            [pltpu.VMEM((blocks, rows, 5 * size), HALF)],
            0,
            1,
            where,
            *pieces,
        )
    else:
        quarter = unflip(pieces, my_block)

    terms = []
    for chunk in chunks:
        mine = call(
            functools.partial(gather_kernel, plan),
            tuple(shaped((step, rows, columns)) for _ in range(blocks)),
            [],
            0,
            1,
            where,
            *chunk,
        )
        terms += [mine[0]] + [plan.route(mine[k], block=k) for k in range(1, blocks)]
    grad_quarter, squares = call(
        functools.partial(sum_kernel, blocks),
        (shaped((blocks, rows, columns)), shaped((8, LANES), FLOAT)),
        [],
        0,
        0,
        *terms,
    )

    near = [plan.route(quarter, high=k, swap=True) for k in range(parts)]
    states = [
        near[k // halves] if k % halves == 0 else plan.route(near[k // halves], column=k % halves)
        for k in range(group)
    ]
    quarters = [grad_quarter] + [
        plan.route(grad_quarter, high=k // halves, column=k % halves) for k in range(1, group)
    ]

    squares = functools.reduce(
        jnp.add, [squares] + [plan.route(squares, block=k) for k in range(1, blocks)]
    )
    bit = 1
    while bit < halves:
        squares = squares + plan.route(squares, column=bit)
        bit *= 2
    sums = [squares] + [
        plan.route(squares, high=k // halves, low=k % halves) for k in range(1, group)
    ]

    gram = shaped((size, size), FLOAT)
    square = shaped((size, size))
    matmul = 2 * size**3
    if in_tiles:
        left_q, right_q, left_c, right_c = call(
            functools.partial(probe_kernel, plan),
            (square, square, gram, gram),
            [pltpu.VMEM((size, size), HALF)] * 3,
            4 * matmul,
            1,
            where,
            *states,
        )
        gradient, left_w, right_w, own_clip = call(
            functools.partial(whiten_kernel, plan, limit),
            (shaped((size, columns)), gram, gram, shaped((8, LANES), FLOAT)),
            [],
            4 * matmul,
            1,
            where,
            left_q,
            right_q,
            *quarters,
        )
        back = call(
            functools.partial(finish_kernel, plan, limit),
            tuple(shaped((rows, 2 * size + columns)) for _ in range(blocks)),
            [pltpu.VMEM((size, size), HALF)] * 3 + [pltpu.VMEM((blocks, rows, columns), HALF)],
            5 * matmul,
            1,
            where,
            *sums,
            own_clip,
            left_q,
            right_q,
            gradient,
            left_w,
            right_w,
            left_c,
            right_c,
        )
    else:
        back = plain_block(plan, limit, my_block, work_place, sums, states, quarters)
    back = [plan.route(back[k], block=k, swap=True) for k in range(blocks)]
    precond, new_state = call(
        functools.partial(place_kernel, plan),
        (shaped((blocks, rows, columns)), shaped(old_state.shape)),
        [],
        0,
        2,
        where,
        slot_row,
        old_state,
        *back,
    )
    return (precond.reshape(experts, block_rows, rows, columns), new_state[None])


def plain_block(plan, limit, my_block, my_place, sums, states, quarters):
    size, blocks, group, rows = plan.size, plan.blocks, plan.group, plan.rows
    state = unflip(states, my_place).transpose(1, 0, 2, 3).reshape(size, 5 * size)
    gradient = unflip(quarters, my_place).transpose(1, 0, 2, 3).reshape(size, -1)
    clip = bound_of(limit, functools.reduce(jnp.add, sums)[0:1, 0:1])
    left_q, right_q, left_inv, right_inv, probe_mat = jnp.split(state, 5, axis=1)
    half_conjugate = product(left_inv, probe_mat, 0, 0).astype(HALF)
    conjugate = product(half_conjugate, right_inv).astype(HALF)
    left_times = (clip * product(left_q, gradient)).astype(HALF)
    whitened = product(left_times, right_q, 1, 1).astype(HALF)
    new_left = step_factor(
        left_q, 1.0, product(whitened, whitened, 1, 1), product(conjugate, conjugate, 1, 1)
    )
    new_right = step_factor(
        right_q, 1.0, product(whitened, whitened, 0, 0), product(conjugate, conjugate, 0, 0)
    )
    precond_left = product(new_left, new_left, 0, 0).astype(HALF)
    precond_right = product(new_right, new_right, 0, 0).astype(HALF)

    def my_rows(array):
        return pick(array.reshape(blocks, group, rows, -1), my_place, 1)

    middle = (clip * product(my_rows(precond_left).reshape(blocks * rows, size), gradient)).astype(HALF)
    result = product(middle, precond_right).astype(HALF).reshape(blocks, rows, -1)
    back = jnp.concatenate([my_rows(new_left), my_rows(new_right), result], axis=2)
    return [pick(back, my_block ^ k, 0) for k in range(blocks)]


def solution(mesh):
    return jax.shard_map(
        body,
        mesh=mesh,
        in_specs=(
            P("dp", None, None, None, "mp"),
            P("mp", None, "dp", None),
            P("mp", None, "dp", None),
            P("mp", None, "dp", None),
            P("mp", None),
        ),
        out_specs=(P(None, None, "dp", "mp"), P("mp", None, "dp", None)),
        check_vma=False,
    )
```

```python
import functools
import math

import jax
import jax.numpy as jnp
from jax import lax
from jax.experimental import pallas as pl
from jax.experimental.pallas import tpu as pltpu
from jax.sharding import PartitionSpec as P

CLIP_RMS = 0.3
LEARN_RATE = 0.1
EPS_NORM = 1e-06
LANES = 128
CHUNKS = 2
VMEM_GRANT = 16 * 2**20
FLOAT = jnp.float32
HALF = jnp.bfloat16


VMEM_SPEC = pl.BlockSpec(memory_space=pltpu.VMEM)
SMEM_SPEC = pl.BlockSpec(memory_space=pltpu.SMEM)


def product(left_op, right_op, left_dim=1, right_dim=0):
    return lax.dot_general(
        left_op, right_op, (((left_dim,), (right_dim,)), ((), ())), preferred_element_type=FLOAT
    )


def flip(array, devices, mask):
    return lax.ppermute(array, "dp", [(i, i ^ mask) for i in range(devices)])


def pick(array, index, axis):
    return lax.dynamic_index_in_dim(array, index, axis, keepdims=False)


def unflip(pieces, own):
    stacked = jnp.stack(pieces)
    return jnp.stack([pick(stacked, own ^ k, 0) for k in range(len(pieces))])


def call(kernel, out_shape, scratch, flops, smem, *operands):
    moved = sum(x.size * x.dtype.itemsize for x in (*operands, *jax.tree.leaves(out_shape)))
    return pl.pallas_call(
        kernel,
        out_shape=out_shape,
        in_specs=[SMEM_SPEC] * smem + [VMEM_SPEC] * (len(operands) - smem),
        out_specs=jax.tree.map(lambda _: VMEM_SPEC, out_shape),
        scratch_shapes=scratch,
        cost_estimate=pl.CostEstimate(flops=flops, bytes_accessed=moved, transcendentals=0),
        compiler_params=pltpu.CompilerParams(vmem_limit_bytes=VMEM_GRANT),
    )(*operands)


class Plan:
    def __init__(self, devices, blocks, size):
        self.devices, self.blocks, self.size = devices, blocks, size
        self.group = devices // blocks
        self.rows = size // devices
        self.first = [z * (size // blocks) // LANES * LANES for z in range(blocks)]

    def spots(self):
        offset = 0
        for z in range(self.blocks):
            for what in range(5):
                first = self.first[z] if what < 4 else 0
                yield z, what, first, offset
                offset += self.size - first

    def packed(self):
        return sum(self.size - first for _, _, first, _ in self.spots())


def pack_kernel(plan, where, *refs):
    pieces, out, stack = refs[: plan.blocks], refs[-2], refs[-1]
    size = plan.size
    for k, piece in enumerate(pieces):
        stack[where[0] ^ k] = piece[...]
    for z, what, first, offset in plan.spots():
        out[:, offset : offset + size - first] = stack[z, :, what * size + first : (what + 1) * size]


def spread(plan, where, pieces, targets):
    size, rows = plan.size, plan.rows
    for z in range(1, plan.blocks):
        for target in targets[:4]:
            if target is not None and plan.first[z]:
                span = size // plan.blocks
                target[z * span : (z + 1) * span, : plan.first[z]] = jnp.zeros((span, plan.first[z]), HALF)
    for k, piece in enumerate(pieces):
        for z, what, first, offset in plan.spots():
            if targets[what] is not None:
                row = pl.multiple_of((z * plan.group + (where[1] ^ k)) * rows, rows)
                targets[what][pl.ds(row, rows), first:] = piece[:, offset : offset + size - first]


def probe_kernel(plan, where, *refs):
    pieces = refs[: plan.group]
    left, right, left_gram, right_gram, left_inv, right_inv, probe = refs[plan.group :]
    spread(plan, where, pieces, (left, right, left_inv, right_inv, probe))
    half_conjugate = product(left_inv[...], probe[...], 0, 0).astype(HALF)
    conjugate = product(half_conjugate, right_inv[...]).astype(HALF)
    left_gram[...] = product(conjugate, conjugate, 1, 1)
    right_gram[...] = product(conjugate, conjugate, 0, 0)


def gather_kernel(plan, where, *refs):
    terms, outs = refs[: plan.group], refs[plan.group :]
    for k, out in enumerate(outs):
        block = where[0] ^ k
        total = terms[0][block].astype(FLOAT)
        for term in terms[1:]:
            total = total + term[block].astype(FLOAT)
        out[...] = total.astype(HALF)


def sum_kernel(blocks, *refs):
    terms, (out, squares) = refs[:-2], refs[-2:]
    found, start = 0.0, 0
    for i in range(0, len(terms), blocks):
        total = terms[i][...].astype(FLOAT)
        for term in terms[i + 1 : i + blocks]:
            total = total + term[...].astype(FLOAT)
        out[start : start + total.shape[0]] = total.astype(HALF)
        start += total.shape[0]
        found = found + jnp.sum(jnp.sum(total * total, axis=(0, 1)))
    squares[...] = jnp.full(squares.shape, found)


def bound_of(limit, squares):
    return jnp.minimum(1.0, limit / jnp.sqrt(squares + EPS_NORM))


def whiten_kernel(plan, limit, where, *refs):
    left, right, pieces = refs[0], refs[1], refs[2 : 2 + plan.group]
    grad, left_gram, right_gram, own_clip = refs[2 + plan.group :]
    for k, piece in enumerate(pieces):
        for z in range(plan.blocks):
            row = pl.multiple_of((z * plan.group + (where[1] ^ k)) * plan.rows, plan.rows)
            grad[pl.ds(row, plan.rows), :] = piece[z]
    wide = grad[...].astype(FLOAT)
    clip = bound_of(limit, jnp.sum(wide * wide, keepdims=True))
    own_clip[...] = jnp.broadcast_to(clip, own_clip.shape)
    left_times = (clip * product(left[...], grad[...])).astype(HALF)
    whitened = product(left_times, right[...], 1, 1).astype(HALF)
    left_gram[...] = product(whitened, whitened, 1, 1)
    right_gram[...] = product(whitened, whitened, 0, 0)


def step_factor(factor, ratio, first_ref, second_ref):
    first, second = ratio * first_ref[...], second_ref[...]
    bound_value = jnp.max(jnp.abs(first + second), keepdims=True) + EPS_NORM
    row = lax.broadcasted_iota(jnp.int32, first.shape, 0)
    column = lax.broadcasted_iota(jnp.int32, first.shape, 1)
    change = jnp.where(row <= column, first - second, 0.0).astype(HALF)
    moved_rows = product(change, factor)
    return (factor.astype(FLOAT) - LEARN_RATE / bound_value * moved_rows).astype(HALF)


def finish_kernel(plan, limit, where, *refs):
    sums, refs = refs[: plan.group], refs[plan.group :]
    own_clip, left, right, grad, left_p, right_p, left_q, right_q = refs[:8]
    outs, (new_left, new_right, square, result) = refs[8:-4], refs[-4:]
    squares = sums[0][0:1, 0:1]
    for ref in sums[1:]:
        squares = squares + ref[0:1, 0:1]
    clip = bound_of(limit, squares)
    ratio = clip / own_clip[0:1, 0:1]
    ratio = ratio * ratio
    size, rows = plan.size, plan.rows
    new_left[...] = step_factor(left[...], ratio, left_p, left_q)
    new_right[...] = step_factor(right[...], ratio, right_p, right_q)
    square[...] = product(new_left[...], new_left[...], 0, 0).astype(HALF)
    precond_right = product(new_right[...], new_right[...], 0, 0).astype(HALF)

    def at(z):
        return pl.ds(pl.multiple_of((z * plan.group + where[1]) * rows, rows), rows)

    precond_left = jnp.concatenate([square[at(z), :] for z in range(plan.blocks)], axis=0)
    middle = (clip * product(precond_left, grad[...])).astype(HALF)
    result[...] = product(middle, precond_right).astype(HALF).reshape(plan.blocks, rows, size)
    for k, out in enumerate(outs):
        z = where[0] ^ k
        out[:, :size] = new_left[at(z), :]
        out[:, size : 2 * size] = new_right[at(z), :]
        out[:, 2 * size :] = result[z]


def place_kernel(plan, where, slots, old_state, *refs):
    pieces, (precond, new_state) = refs[: plan.blocks], refs[plan.blocks :]
    size = plan.size
    new_state[...] = old_state[...]
    for k, piece in enumerate(pieces):
        precond[where[0] ^ k] = piece[:, 2 * size :]
        new_state[slots[where[0] ^ k]] = piece[:, : 2 * size]


def shaped(shape, dtype=HALF):
    return jax.ShapeDtypeStruct(shape, dtype)


def body(partial_grads, factors, inverse_factors, probes, slot_table):
    devices = lax.axis_size("dp")
    halves = lax.axis_size("mp")
    me = lax.axis_index("dp")
    experts, block_rows, size, columns = partial_grads.shape[1:]
    blocks = experts * block_rows
    plan = Plan(devices, blocks, size)
    group, rows = plan.group, plan.rows
    my_block = me // group
    my_place = me % group
    where = jnp.stack([my_block, my_place]).astype(jnp.int32)
    slot_row = slot_table[0]
    in_tiles = rows % 16 == 0
    limit = CLIP_RMS * math.sqrt(blocks * size * columns * halves)

    grads = partial_grads[0].reshape(blocks, blocks, group, rows, columns)
    step = blocks // CHUNKS
    chunks = []
    for i in range(CHUNKS):
        chunk = grads[:, i * step : (i + 1) * step]
        chunks.append(
            [pick(chunk, my_place, 2)]
            + [flip(pick(chunk, my_place ^ k, 2), devices, k) for k in range(1, group)]
        )

    old_state = factors[0]
    wide = jnp.concatenate([old_state, inverse_factors[0], probes[0]], axis=2)
    chosen = jnp.take(wide, slot_row, axis=0)
    pieces = [pick(chosen, my_block, 0)] + [
        flip(pick(chosen, my_block ^ k, 0), devices, k * group) for k in range(1, blocks)
    ]
    if in_tiles:
        quarter = call(
            functools.partial(pack_kernel, plan),
            shaped((rows, plan.packed())),
            [pltpu.VMEM((blocks, rows, 5 * size), HALF)],
            0,
            1,
            where,
            *pieces,
        )
    else:
        quarter = unflip(pieces, my_block)

    terms = []
    for chunk in chunks:
        mine = call(
            functools.partial(gather_kernel, plan),
            tuple(shaped((step, rows, columns)) for _ in range(blocks)),
            [],
            0,
            1,
            where,
            *chunk,
        )
        terms += [mine[0]] + [flip(mine[k], devices, k * group) for k in range(1, blocks)]
    grad_quarter, squares = call(
        functools.partial(sum_kernel, blocks),
        (shaped((blocks, rows, columns)), shaped((8, LANES), FLOAT)),
        [],
        0,
        0,
        *terms,
    )

    states = [quarter] + [flip(quarter, devices, k) for k in range(1, group)]
    quarters = [grad_quarter] + [flip(grad_quarter, devices, k) for k in range(1, group)]

    bit = 1
    while bit < halves:
        other = lax.ppermute(squares, "mp", [(i, i ^ bit) for i in range(halves)])
        squares = squares + other
        bit *= 2
    bit = 1
    while bit < blocks:
        squares = squares + flip(squares, devices, bit * group)
        bit *= 2
    sums = [squares] + [flip(squares, devices, k) for k in range(1, group)]

    gram = shaped((size, size), FLOAT)
    square = shaped((size, size))
    matmul = 2 * size**3
    if in_tiles:
        left_q, right_q, left_c, right_c = call(
            functools.partial(probe_kernel, plan),
            (square, square, gram, gram),
            [pltpu.VMEM((size, size), HALF)] * 3,
            4 * matmul,
            1,
            where,
            *states,
        )
        gradient, left_w, right_w, own_clip = call(
            functools.partial(whiten_kernel, plan, limit),
            (shaped((size, columns)), gram, gram, shaped((8, LANES), FLOAT)),
            [],
            4 * matmul,
            1,
            where,
            left_q,
            right_q,
            *quarters,
        )
        back = call(
            functools.partial(finish_kernel, plan, limit),
            tuple(shaped((rows, 2 * size + columns)) for _ in range(blocks)),
            [pltpu.VMEM((size, size), HALF)] * 3 + [pltpu.VMEM((blocks, rows, columns), HALF)],
            5 * matmul,
            1,
            where,
            *sums,
            own_clip,
            left_q,
            right_q,
            gradient,
            left_w,
            right_w,
            left_c,
            right_c,
        )
    else:
        back = plain_block(plan, limit, my_block, my_place, sums, states, quarters)
    back = [back[0]] + [flip(back[k], devices, k * group) for k in range(1, blocks)]
    precond, new_state = call(
        functools.partial(place_kernel, plan),
        (shaped((blocks, rows, columns)), shaped(old_state.shape)),
        [],
        0,
        2,
        where,
        slot_row,
        old_state,
        *back,
    )
    return (precond.reshape(experts, block_rows, rows, columns), new_state[None])


def plain_block(plan, limit, my_block, my_place, sums, states, quarters):
    size, blocks, group, rows = plan.size, plan.blocks, plan.group, plan.rows
    state = unflip(states, my_place).transpose(1, 0, 2, 3).reshape(size, 5 * size)
    gradient = unflip(quarters, my_place).transpose(1, 0, 2, 3).reshape(size, -1)
    clip = bound_of(limit, functools.reduce(jnp.add, sums)[0:1, 0:1])
    left_q, right_q, left_inv, right_inv, probe_mat = jnp.split(state, 5, axis=1)
    half_conjugate = product(left_inv, probe_mat, 0, 0).astype(HALF)
    conjugate = product(half_conjugate, right_inv).astype(HALF)
    left_times = (clip * product(left_q, gradient)).astype(HALF)
    whitened = product(left_times, right_q, 1, 1).astype(HALF)
    new_left = step_factor(
        left_q, 1.0, product(whitened, whitened, 1, 1), product(conjugate, conjugate, 1, 1)
    )
    new_right = step_factor(
        right_q, 1.0, product(whitened, whitened, 0, 0), product(conjugate, conjugate, 0, 0)
    )
    precond_left = product(new_left, new_left, 0, 0).astype(HALF)
    precond_right = product(new_right, new_right, 0, 0).astype(HALF)

    def my_rows(array):
        return pick(array.reshape(blocks, group, rows, -1), my_place, 1)

    middle = (clip * product(my_rows(precond_left).reshape(blocks * rows, size), gradient)).astype(HALF)
    result = product(middle, precond_right).astype(HALF).reshape(blocks, rows, -1)
    back = jnp.concatenate([my_rows(new_left), my_rows(new_right), result], axis=2)
    return [pick(back, my_block ^ k, 0) for k in range(blocks)]


def solution(mesh):
    return jax.shard_map(
        body,
        mesh=mesh,
        in_specs=(
            P("dp", None, None, None, "mp"),
            P("mp", None, "dp", None),
            P("mp", None, "dp", None),
            P("mp", None, "dp", None),
            P("mp", None),
        ),
        out_specs=(P(None, None, "dp", "mp"), P("mp", None, "dp", None)),
        check_vma=False,
    )
```

```python
import functools
import math

import jax
import jax.numpy as jnp
from jax import lax
from jax.experimental import pallas as pl
from jax.experimental.pallas import tpu as pltpu
from jax.sharding import PartitionSpec as P

CLIP_RMS = 0.3
LEARN_RATE = 0.1
EPS_NORM = 1e-06
LANES = 128
CHUNKS = 2
VMEM_GRANT = 16 * 2**20
FLOAT = jnp.float32
HALF = jnp.bfloat16


VMEM_SPEC = pl.BlockSpec(memory_space=pltpu.VMEM)
SMEM_SPEC = pl.BlockSpec(memory_space=pltpu.SMEM)


def product(left_op, right_op, left_dim=1, right_dim=0):
    return lax.dot_general(
        left_op, right_op, (((left_dim,), (right_dim,)), ((), ())), preferred_element_type=FLOAT
    )


def flip(array, devices, mask):
    return lax.ppermute(array, "dp", [(i, i ^ mask) for i in range(devices)])


def pick(array, index, axis):
    return lax.dynamic_index_in_dim(array, index, axis, keepdims=False)


def unflip(pieces, own):
    stacked = jnp.stack(pieces)
    return jnp.stack([pick(stacked, own ^ k, 0) for k in range(len(pieces))])


def call(kernel, out_shape, scratch, flops, smem, *operands):
    moved = sum(x.size * x.dtype.itemsize for x in (*operands, *jax.tree.leaves(out_shape)))
    return pl.pallas_call(
        kernel,
        out_shape=out_shape,
        in_specs=[SMEM_SPEC] * smem + [VMEM_SPEC] * (len(operands) - smem),
        out_specs=jax.tree.map(lambda _: VMEM_SPEC, out_shape),
        scratch_shapes=scratch,
        cost_estimate=pl.CostEstimate(flops=flops, bytes_accessed=moved, transcendentals=0),
        compiler_params=pltpu.CompilerParams(vmem_limit_bytes=VMEM_GRANT),
    )(*operands)


class Plan:
    def __init__(self, devices, blocks, size):
        self.devices, self.blocks, self.size = devices, blocks, size
        self.group = devices // blocks
        self.rows = size // devices
        self.first = [z * (size // blocks) // LANES * LANES for z in range(blocks)]

    def spots(self):
        offset = 0
        for z in range(self.blocks):
            for what in range(5):
                first = self.first[z] if what < 4 else 0
                yield z, what, first, offset
                offset += self.size - first

    def packed(self):
        return sum(self.size - first for _, _, first, _ in self.spots())


def choose_kernel(plan, where, slots, factors, inverses, probes, *outs):
    size = plan.size
    for k, out in enumerate(outs):
        slot = slots[where[0] ^ k]
        out[:, : 2 * size] = factors[slot]
        out[:, 2 * size : 4 * size] = inverses[slot]
        out[:, 4 * size :] = probes[slot]


def pack_kernel(plan, where, *refs):
    pieces, out, stack = refs[: plan.blocks], refs[-2], refs[-1]
    size = plan.size
    for k, piece in enumerate(pieces):
        stack[where[0] ^ k] = piece[...]
    for z, what, first, offset in plan.spots():
        out[:, offset : offset + size - first] = stack[z, :, what * size + first : (what + 1) * size]


def spread(plan, where, pieces, targets):
    size, rows = plan.size, plan.rows
    for z in range(1, plan.blocks):
        for target in targets[:4]:
            if target is not None and plan.first[z]:
                span = size // plan.blocks
                target[z * span : (z + 1) * span, : plan.first[z]] = jnp.zeros((span, plan.first[z]), HALF)
    for k, piece in enumerate(pieces):
        for z, what, first, offset in plan.spots():
            if targets[what] is not None:
                row = pl.multiple_of((z * plan.group + (where[1] ^ k)) * rows, rows)
                targets[what][pl.ds(row, rows), first:] = piece[:, offset : offset + size - first]


def probe_kernel(plan, where, *refs):
    pieces = refs[: plan.group]
    left, right, left_gram, right_gram, left_inv, right_inv, probe = refs[plan.group :]
    spread(plan, where, pieces, (left, right, left_inv, right_inv, probe))
    half_conjugate = product(left_inv[...], probe[...], 0, 0).astype(HALF)
    conjugate = product(half_conjugate, right_inv[...]).astype(HALF)
    left_gram[...] = product(conjugate, conjugate, 1, 1)
    right_gram[...] = product(conjugate, conjugate, 0, 0)


def gather_kernel(plan, where, *refs):
    terms, outs = refs[: plan.group], refs[plan.group :]
    for k, out in enumerate(outs):
        block = where[0] ^ k
        total = terms[0][block].astype(FLOAT)
        for term in terms[1:]:
            total = total + term[block].astype(FLOAT)
        out[...] = total.astype(HALF)


def sum_kernel(blocks, *refs):
    terms, (out, squares) = refs[:-2], refs[-2:]
    found, start = 0.0, 0
    for i in range(0, len(terms), blocks):
        total = terms[i][...].astype(FLOAT)
        for term in terms[i + 1 : i + blocks]:
            total = total + term[...].astype(FLOAT)
        out[start : start + total.shape[0]] = total.astype(HALF)
        start += total.shape[0]
        found = found + jnp.sum(jnp.sum(total * total, axis=(0, 1)))
    squares[...] = jnp.full(squares.shape, found)


def bound_of(limit, squares):
    return jnp.minimum(1.0, limit / jnp.sqrt(squares + EPS_NORM))


def whiten_kernel(plan, limit, where, *refs):
    left, right, pieces = refs[0], refs[1], refs[2 : 2 + plan.group]
    grad, left_gram, right_gram, own_clip = refs[2 + plan.group :]
    for k, piece in enumerate(pieces):
        for z in range(plan.blocks):
            row = pl.multiple_of((z * plan.group + (where[1] ^ k)) * plan.rows, plan.rows)
            grad[pl.ds(row, plan.rows), :] = piece[z]
    wide = grad[...].astype(FLOAT)
    clip = bound_of(limit, jnp.sum(wide * wide, keepdims=True))
    own_clip[...] = jnp.broadcast_to(clip, own_clip.shape)
    left_times = (clip * product(left[...], grad[...])).astype(HALF)
    whitened = product(left_times, right[...], 1, 1).astype(HALF)
    left_gram[...] = product(whitened, whitened, 1, 1)
    right_gram[...] = product(whitened, whitened, 0, 0)


def step_factor(factor, ratio, first_ref, second_ref):
    first, second = ratio * first_ref[...], second_ref[...]
    bound_value = jnp.max(jnp.abs(first + second), keepdims=True) + EPS_NORM
    row = lax.broadcasted_iota(jnp.int32, first.shape, 0)
    column = lax.broadcasted_iota(jnp.int32, first.shape, 1)
    change = jnp.where(row <= column, first - second, 0.0).astype(HALF)
    moved_rows = product(change, factor)
    return (factor.astype(FLOAT) - LEARN_RATE / bound_value * moved_rows).astype(HALF)


def finish_kernel(plan, limit, where, *refs):
    sums, refs = refs[: plan.group], refs[plan.group :]
    own_clip, left, right, grad, left_p, right_p, left_q, right_q = refs[:8]
    outs, (new_left, new_right, square, result) = refs[8:-4], refs[-4:]
    squares = sums[0][0:1, 0:1]
    for ref in sums[1:]:
        squares = squares + ref[0:1, 0:1]
    clip = bound_of(limit, squares)
    ratio = clip / own_clip[0:1, 0:1]
    ratio = ratio * ratio
    size, rows = plan.size, plan.rows
    new_left[...] = step_factor(left[...], ratio, left_p, left_q)
    new_right[...] = step_factor(right[...], ratio, right_p, right_q)
    square[...] = product(new_left[...], new_left[...], 0, 0).astype(HALF)
    precond_right = product(new_right[...], new_right[...], 0, 0).astype(HALF)

    def at(z):
        return pl.ds(pl.multiple_of((z * plan.group + where[1]) * rows, rows), rows)

    precond_left = jnp.concatenate([square[at(z), :] for z in range(plan.blocks)], axis=0)
    middle = (clip * product(precond_left, grad[...])).astype(HALF)
    result[...] = product(middle, precond_right).astype(HALF).reshape(plan.blocks, rows, size)
    for k, out in enumerate(outs):
        z = where[0] ^ k
        out[:, :size] = new_left[at(z), :]
        out[:, size : 2 * size] = new_right[at(z), :]
        out[:, 2 * size :] = result[z]


def place_kernel(plan, where, slots, old_state, *refs):
    pieces, (precond, new_state) = refs[: plan.blocks], refs[plan.blocks :]
    size = plan.size
    new_state[...] = old_state[...]
    for k, piece in enumerate(pieces):
        precond[where[0] ^ k] = piece[:, 2 * size :]
        new_state[slots[where[0] ^ k]] = piece[:, : 2 * size]


def shaped(shape, dtype=HALF):
    return jax.ShapeDtypeStruct(shape, dtype)


def body(partial_grads, factors, inverse_factors, probes, slot_table):
    devices = lax.axis_size("dp")
    halves = lax.axis_size("mp")
    me = lax.axis_index("dp")
    experts, block_rows, size, columns = partial_grads.shape[1:]
    blocks = experts * block_rows
    plan = Plan(devices, blocks, size)
    group, rows = plan.group, plan.rows
    my_block = me // group
    my_place = me % group
    where = jnp.stack([my_block, my_place]).astype(jnp.int32)
    slot_row = slot_table[0]
    in_tiles = rows % 16 == 0
    limit = CLIP_RMS * math.sqrt(blocks * size * columns * halves)

    grads = partial_grads[0].reshape(blocks, blocks, group, rows, columns)
    step = blocks // CHUNKS
    later = lax.optimization_barrier(grads)
    chunks = []
    for i in range(CHUNKS):
        cut = [
            lax.dynamic_slice(
                grads if i == 0 and k > 0 else later,
                (0, i * step, my_place ^ k, 0, 0),
                (blocks, step, 1, rows, columns),
            ).reshape(blocks, step, rows, columns)
            for k in range(group)
        ]
        chunks.append([cut[0]] + [flip(cut[k], devices, k) for k in range(1, group)])

    old_state = factors[0]
    if in_tiles:
        pieces = call(
            functools.partial(choose_kernel, plan),
            tuple(shaped((rows, 5 * size)) for _ in range(blocks)),
            [],
            0,
            2,
            where,
            slot_row,
            old_state,
            inverse_factors[0],
            probes[0],
        )
    else:
        wide = jnp.concatenate([old_state, inverse_factors[0], probes[0]], axis=2)
        pieces = [pick(wide, slot_row[my_block ^ k], 0) for k in range(blocks)]
    pieces = [pieces[0]] + [flip(pieces[k], devices, k * group) for k in range(1, blocks)]
    if in_tiles:
        quarter = call(
            functools.partial(pack_kernel, plan),
            shaped((rows, plan.packed())),
            [pltpu.VMEM((blocks, rows, 5 * size), HALF)],
            0,
            1,
            where,
            *pieces,
        )
    else:
        quarter = unflip(pieces, my_block)

    terms = []
    for chunk in chunks:
        mine = call(
            functools.partial(gather_kernel, plan),
            tuple(shaped((step, rows, columns)) for _ in range(blocks)),
            [],
            0,
            1,
            where,
            *chunk,
        )
        terms += [mine[0]] + [flip(mine[k], devices, k * group) for k in range(1, blocks)]
    grad_quarter, squares = call(
        functools.partial(sum_kernel, blocks),
        (shaped((blocks, rows, columns)), shaped((8, LANES), FLOAT)),
        [],
        0,
        0,
        *terms,
    )

    states = [quarter] + [flip(quarter, devices, k) for k in range(1, group)]
    quarters = [grad_quarter] + [flip(grad_quarter, devices, k) for k in range(1, group)]

    squares = functools.reduce(
        jnp.add,
        [squares] + [flip(squares, devices, k * group) for k in range(1, blocks)],
    )
    bit = 1
    while bit < halves:
        other = lax.ppermute(squares, "mp", [(i, i ^ bit) for i in range(halves)])
        squares = squares + other
        bit *= 2
    sums = [squares] + [flip(squares, devices, k) for k in range(1, group)]

    gram = shaped((size, size), FLOAT)
    square = shaped((size, size))
    matmul = 2 * size**3
    if in_tiles:
        left_q, right_q, left_c, right_c = call(
            functools.partial(probe_kernel, plan),
            (square, square, gram, gram),
            [pltpu.VMEM((size, size), HALF)] * 3,
            4 * matmul,
            1,
            where,
            *states,
        )
        gradient, left_w, right_w, own_clip = call(
            functools.partial(whiten_kernel, plan, limit),
            (shaped((size, columns)), gram, gram, shaped((8, LANES), FLOAT)),
            [],
            4 * matmul,
            1,
            where,
            left_q,
            right_q,
            *quarters,
        )
        back = call(
            functools.partial(finish_kernel, plan, limit),
            tuple(shaped((rows, 2 * size + columns)) for _ in range(blocks)),
            [pltpu.VMEM((size, size), HALF)] * 3 + [pltpu.VMEM((blocks, rows, columns), HALF)],
            5 * matmul,
            1,
            where,
            *sums,
            own_clip,
            left_q,
            right_q,
            gradient,
            left_w,
            right_w,
            left_c,
            right_c,
        )
    else:
        back = plain_block(plan, limit, my_block, my_place, sums, states, quarters)
    back = [back[0]] + [flip(back[k], devices, k * group) for k in range(1, blocks)]
    precond, new_state = call(
        functools.partial(place_kernel, plan),
        (shaped((blocks, rows, columns)), shaped(old_state.shape)),
        [],
        0,
        2,
        where,
        slot_row,
        old_state,
        *back,
    )
    return (precond.reshape(experts, block_rows, rows, columns), new_state[None])


def plain_block(plan, limit, my_block, my_place, sums, states, quarters):
    size, blocks, group, rows = plan.size, plan.blocks, plan.group, plan.rows
    state = unflip(states, my_place).transpose(1, 0, 2, 3).reshape(size, 5 * size)
    gradient = unflip(quarters, my_place).transpose(1, 0, 2, 3).reshape(size, -1)
    clip = bound_of(limit, functools.reduce(jnp.add, sums)[0:1, 0:1])
    left_q, right_q, left_inv, right_inv, probe_mat = jnp.split(state, 5, axis=1)
    half_conjugate = product(left_inv, probe_mat, 0, 0).astype(HALF)
    conjugate = product(half_conjugate, right_inv).astype(HALF)
    left_times = (clip * product(left_q, gradient)).astype(HALF)
    whitened = product(left_times, right_q, 1, 1).astype(HALF)
    new_left = step_factor(
        left_q, 1.0, product(whitened, whitened, 1, 1), product(conjugate, conjugate, 1, 1)
    )
    new_right = step_factor(
        right_q, 1.0, product(whitened, whitened, 0, 0), product(conjugate, conjugate, 0, 0)
    )
    precond_left = product(new_left, new_left, 0, 0).astype(HALF)
    precond_right = product(new_right, new_right, 0, 0).astype(HALF)

    def my_rows(array):
        return pick(array.reshape(blocks, group, rows, -1), my_place, 1)

    middle = (clip * product(my_rows(precond_left).reshape(blocks * rows, size), gradient)).astype(HALF)
    result = product(middle, precond_right).astype(HALF).reshape(blocks, rows, -1)
    back = jnp.concatenate([my_rows(new_left), my_rows(new_right), result], axis=2)
    return [pick(back, my_block ^ k, 0) for k in range(blocks)]


def solution(mesh):
    return jax.shard_map(
        body,
        mesh=mesh,
        in_specs=(
            P("dp", None, None, None, "mp"),
            P("mp", None, "dp", None),
            P("mp", None, "dp", None),
            P("mp", None, "dp", None),
            P("mp", None),
        ),
        out_specs=(P(None, None, "dp", "mp"), P("mp", None, "dp", None)),
        check_vma=False,
    )
```

```python
import functools
import math

import jax
import jax.numpy as jnp
from jax import lax
from jax.experimental import pallas as pl
from jax.experimental.pallas import tpu as pltpu
from jax.sharding import PartitionSpec as P

CLIP_RMS = 0.3
LEARN_RATE = 0.1
EPS_NORM = 1e-06
LANES = 128
CHUNKS = 1
VMEM_GRANT = 16 * 2**20
FLOAT = jnp.float32
HALF = jnp.bfloat16


VMEM_SPEC = pl.BlockSpec(memory_space=pltpu.VMEM)
SMEM_SPEC = pl.BlockSpec(memory_space=pltpu.SMEM)


def product(left_op, right_op, left_dim=1, right_dim=0):
    return lax.dot_general(
        left_op, right_op, (((left_dim,), (right_dim,)), ((), ())), preferred_element_type=FLOAT
    )


def flip(array, devices, mask):
    return lax.ppermute(array, "dp", [(i, i ^ mask) for i in range(devices)])


def pick(array, index, axis):
    return lax.dynamic_index_in_dim(array, index, axis, keepdims=False)


def unflip(pieces, own):
    stacked = jnp.stack(pieces)
    return jnp.stack([pick(stacked, own ^ k, 0) for k in range(len(pieces))])


def call(kernel, out_shape, scratch, flops, smem, *operands, space=pltpu.VMEM):
    moved = sum(x.size * x.dtype.itemsize for x in (*operands, *jax.tree.leaves(out_shape)))
    return pl.pallas_call(
        kernel,
        out_shape=out_shape,
        in_specs=[SMEM_SPEC] * smem + [pl.BlockSpec(memory_space=space)] * (len(operands) - smem),
        out_specs=jax.tree.map(lambda _: VMEM_SPEC, out_shape),
        scratch_shapes=scratch,
        cost_estimate=pl.CostEstimate(flops=flops, bytes_accessed=moved, transcendentals=0),
        compiler_params=pltpu.CompilerParams(vmem_limit_bytes=VMEM_GRANT),
    )(*operands)


class Plan:
    def __init__(self, devices, blocks, size):
        self.devices, self.blocks, self.size = devices, blocks, size
        self.group = devices // blocks
        self.rows = size // devices
        self.first = [z * (size // blocks) // LANES * LANES for z in range(blocks)]

    def spots(self):
        offset = 0
        for z in range(self.blocks):
            for what in range(5):
                first = self.first[z] if what < 4 else 0
                yield z, what, first, offset
                offset += self.size - first

    def packed(self):
        return sum(self.size - first for _, _, first, _ in self.spots())


def choose_kernel(plan, where, slots, factors, inverses, probes, *refs):
    outs, done = refs[:-1], refs[-1]
    size, copies = plan.size, []
    for k, out in enumerate(outs):
        slot = slots[where[0] ^ k]
        parts = (
            (factors, out.at[:, : 2 * size]),
            (inverses, out.at[:, 2 * size : 4 * size]),
            (probes, out.at[:, 4 * size :]),
        )
        for i, (source, target) in enumerate(parts):
            copies.append(pltpu.make_async_copy(source.at[slot], target, done.at[3 * k + i]))
    for copy in copies:
        copy.start()
    for copy in copies:
        copy.wait()


def pack_kernel(plan, where, *refs):
    pieces, out, stack = refs[: plan.blocks], refs[-2], refs[-1]
    size = plan.size
    for k, piece in enumerate(pieces):
        stack[where[0] ^ k] = piece[...]
    for z, what, first, offset in plan.spots():
        out[:, offset : offset + size - first] = stack[z, :, what * size + first : (what + 1) * size]


def spread(plan, where, pieces, targets):
    size, rows = plan.size, plan.rows
    for z in range(1, plan.blocks):
        for target in targets[:4]:
            if target is not None and plan.first[z]:
                span = size // plan.blocks
                target[z * span : (z + 1) * span, : plan.first[z]] = jnp.zeros((span, plan.first[z]), HALF)
    for k, piece in enumerate(pieces):
        for z, what, first, offset in plan.spots():
            if targets[what] is not None:
                row = pl.multiple_of((z * plan.group + (where[1] ^ k)) * rows, rows)
                targets[what][pl.ds(row, rows), first:] = piece[:, offset : offset + size - first]


def probe_kernel(plan, where, *refs):
    pieces = refs[: plan.group]
    left, right, left_gram, right_gram, left_inv, right_inv, probe = refs[plan.group :]
    spread(plan, where, pieces, (left, right, left_inv, right_inv, probe))
    half_conjugate = product(left_inv[...], probe[...], 0, 0).astype(HALF)
    conjugate = product(half_conjugate, right_inv[...]).astype(HALF)
    left_gram[...] = product(conjugate, conjugate, 1, 1)
    right_gram[...] = product(conjugate, conjugate, 0, 0)


def gather_kernel(plan, where, *refs):
    terms, outs = refs[: plan.group], refs[plan.group :]
    for k, out in enumerate(outs):
        block = where[0] ^ k
        total = terms[0][block].astype(FLOAT)
        for term in terms[1:]:
            total = total + term[block].astype(FLOAT)
        out[...] = total.astype(HALF)


def sum_kernel(blocks, *refs):
    terms, (out, squares) = refs[:-2], refs[-2:]
    found, start = 0.0, 0
    for i in range(0, len(terms), blocks):
        total = terms[i][...].astype(FLOAT)
        for term in terms[i + 1 : i + blocks]:
            total = total + term[...].astype(FLOAT)
        out[start : start + total.shape[0]] = total.astype(HALF)
        start += total.shape[0]
        found = found + jnp.sum(jnp.sum(total * total, axis=(0, 1)))
    squares[...] = jnp.full(squares.shape, found)


def bound_of(limit, squares):
    return jnp.minimum(1.0, limit / jnp.sqrt(squares + EPS_NORM))


def whiten_kernel(plan, limit, where, *refs):
    left, right, pieces = refs[0], refs[1], refs[2 : 2 + plan.group]
    grad, left_gram, right_gram, own_clip = refs[2 + plan.group :]
    for k, piece in enumerate(pieces):
        for z in range(plan.blocks):
            row = pl.multiple_of((z * plan.group + (where[1] ^ k)) * plan.rows, plan.rows)
            grad[pl.ds(row, plan.rows), :] = piece[z]
    wide = grad[...].astype(FLOAT)
    clip = bound_of(limit, jnp.sum(wide * wide, keepdims=True))
    own_clip[...] = jnp.broadcast_to(clip, own_clip.shape)
    left_times = (clip * product(left[...], grad[...])).astype(HALF)
    whitened = product(left_times, right[...], 1, 1).astype(HALF)
    left_gram[...] = product(whitened, whitened, 1, 1)
    right_gram[...] = product(whitened, whitened, 0, 0)


def step_factor(factor, ratio, first_ref, second_ref):
    first, second = ratio * first_ref[...], second_ref[...]
    bound_value = jnp.max(jnp.abs(first + second), keepdims=True) + EPS_NORM
    row = lax.broadcasted_iota(jnp.int32, first.shape, 0)
    column = lax.broadcasted_iota(jnp.int32, first.shape, 1)
    change = jnp.where(row <= column, first - second, 0.0).astype(HALF)
    moved_rows = product(change, factor)
    return (factor.astype(FLOAT) - LEARN_RATE / bound_value * moved_rows).astype(HALF)


def finish_kernel(plan, limit, where, *refs):
    sums, refs = refs[: plan.group], refs[plan.group :]
    own_clip, left, right, grad, left_p, right_p, left_q, right_q = refs[:8]
    outs, (new_left, new_right, square, result) = refs[8:-4], refs[-4:]
    squares = sums[0][0:1, 0:1]
    for ref in sums[1:]:
        squares = squares + ref[0:1, 0:1]
    clip = bound_of(limit, squares)
    ratio = clip / own_clip[0:1, 0:1]
    ratio = ratio * ratio
    size, rows = plan.size, plan.rows
    new_left[...] = step_factor(left[...], ratio, left_p, left_q)
    new_right[...] = step_factor(right[...], ratio, right_p, right_q)
    square[...] = product(new_left[...], new_left[...], 0, 0).astype(HALF)
    precond_right = product(new_right[...], new_right[...], 0, 0).astype(HALF)

    def at(z):
        return pl.ds(pl.multiple_of((z * plan.group + where[1]) * rows, rows), rows)

    precond_left = jnp.concatenate([square[at(z), :] for z in range(plan.blocks)], axis=0)
    middle = (clip * product(precond_left, grad[...])).astype(HALF)
    result[...] = product(middle, precond_right).astype(HALF).reshape(plan.blocks, rows, size)
    for k, out in enumerate(outs):
        z = where[0] ^ k
        out[:, :size] = new_left[at(z), :]
        out[:, size : 2 * size] = new_right[at(z), :]
        out[:, 2 * size :] = result[z]


def place_kernel(plan, where, slots, old_state, *refs):
    pieces, (precond, new_state) = refs[: plan.blocks], refs[plan.blocks :]
    size = plan.size
    new_state[...] = old_state[...]
    for k, piece in enumerate(pieces):
        precond[where[0] ^ k] = piece[:, 2 * size :]
        new_state[slots[where[0] ^ k]] = piece[:, : 2 * size]


def shaped(shape, dtype=HALF):
    return jax.ShapeDtypeStruct(shape, dtype)


def body(partial_grads, factors, inverse_factors, probes, slot_table):
    devices = lax.axis_size("dp")
    halves = lax.axis_size("mp")
    me = lax.axis_index("dp")
    experts, block_rows, size, columns = partial_grads.shape[1:]
    blocks = experts * block_rows
    plan = Plan(devices, blocks, size)
    group, rows = plan.group, plan.rows
    my_block = me // group
    my_place = me % group
    where = jnp.stack([my_block, my_place]).astype(jnp.int32)
    slot_row = slot_table[0]
    in_tiles = rows % 16 == 0
    limit = CLIP_RMS * math.sqrt(blocks * size * columns * halves)

    grads = partial_grads[0].reshape(blocks, blocks, group, rows, columns)
    step = blocks // CHUNKS
    later = lax.optimization_barrier(grads)
    chunks = []
    for i in range(CHUNKS):
        cut = [
            lax.dynamic_slice(
                grads if i == 0 and k > 0 else later,
                (0, i * step, my_place ^ k, 0, 0),
                (blocks, step, 1, rows, columns),
            ).reshape(blocks, step, rows, columns)
            for k in range(group)
        ]
        chunks.append([cut[0]] + [flip(cut[k], devices, k) for k in range(1, group)])

    old_state = factors[0]
    if in_tiles:
        pieces = call(
            functools.partial(choose_kernel, plan),
            tuple(shaped((rows, 5 * size)) for _ in range(blocks)),
            [pltpu.SemaphoreType.DMA((3 * blocks,))],
            0,
            2,
            where,
            slot_row,
            old_state,
            inverse_factors[0],
            probes[0],
            space=pl.ANY,
        )
    else:
        wide = jnp.concatenate([old_state, inverse_factors[0], probes[0]], axis=2)
        pieces = [pick(wide, slot_row[my_block ^ k], 0) for k in range(blocks)]
    pieces = [pieces[0]] + [flip(pieces[k], devices, k * group) for k in range(1, blocks)]
    if in_tiles:
        quarter = call(
            functools.partial(pack_kernel, plan),
            shaped((rows, plan.packed())),
            [pltpu.VMEM((blocks, rows, 5 * size), HALF)],
            0,
            1,
            where,
            *pieces,
        )
    else:
        quarter = unflip(pieces, my_block)

    terms = []
    for chunk in chunks:
        mine = call(
            functools.partial(gather_kernel, plan),
            tuple(shaped((step, rows, columns)) for _ in range(blocks)),
            [],
            0,
            1,
            where,
            *chunk,
        )
        terms += [mine[0]] + [flip(mine[k], devices, k * group) for k in range(1, blocks)]
    grad_quarter, squares = call(
        functools.partial(sum_kernel, blocks),
        (shaped((blocks, rows, columns)), shaped((8, LANES), FLOAT)),
        [],
        0,
        0,
        *terms,
    )

    states = [quarter] + [flip(quarter, devices, k) for k in range(1, group)]
    quarters = [grad_quarter] + [flip(grad_quarter, devices, k) for k in range(1, group)]

    squares = functools.reduce(
        jnp.add,
        [squares] + [flip(squares, devices, k * group) for k in range(1, blocks)],
    )
    bit = 1
    while bit < halves:
        other = lax.ppermute(squares, "mp", [(i, i ^ bit) for i in range(halves)])
        squares = squares + other
        bit *= 2
    sums = [squares] + [flip(squares, devices, k) for k in range(1, group)]

    gram = shaped((size, size), FLOAT)
    square = shaped((size, size))
    matmul = 2 * size**3
    if in_tiles:
        left_q, right_q, left_c, right_c = call(
            functools.partial(probe_kernel, plan),
            (square, square, gram, gram),
            [pltpu.VMEM((size, size), HALF)] * 3,
            4 * matmul,
            1,
            where,
            *states,
        )
        gradient, left_w, right_w, own_clip = call(
            functools.partial(whiten_kernel, plan, limit),
            (shaped((size, columns)), gram, gram, shaped((8, LANES), FLOAT)),
            [],
            4 * matmul,
            1,
            where,
            left_q,
            right_q,
            *quarters,
        )
        back = call(
            functools.partial(finish_kernel, plan, limit),
            tuple(shaped((rows, 2 * size + columns)) for _ in range(blocks)),
            [pltpu.VMEM((size, size), HALF)] * 3 + [pltpu.VMEM((blocks, rows, columns), HALF)],
            5 * matmul,
            1,
            where,
            *sums,
            own_clip,
            left_q,
            right_q,
            gradient,
            left_w,
            right_w,
            left_c,
            right_c,
        )
    else:
        back = plain_block(plan, limit, my_block, my_place, sums, states, quarters)
    back = [back[0]] + [flip(back[k], devices, k * group) for k in range(1, blocks)]
    precond, new_state = call(
        functools.partial(place_kernel, plan),
        (shaped((blocks, rows, columns)), shaped(old_state.shape)),
        [],
        0,
        2,
        where,
        slot_row,
        old_state,
        *back,
    )
    return (precond.reshape(experts, block_rows, rows, columns), new_state[None])


def plain_block(plan, limit, my_block, my_place, sums, states, quarters):
    size, blocks, group, rows = plan.size, plan.blocks, plan.group, plan.rows
    state = unflip(states, my_place).transpose(1, 0, 2, 3).reshape(size, 5 * size)
    gradient = unflip(quarters, my_place).transpose(1, 0, 2, 3).reshape(size, -1)
    clip = bound_of(limit, functools.reduce(jnp.add, sums)[0:1, 0:1])
    left_q, right_q, left_inv, right_inv, probe_mat = jnp.split(state, 5, axis=1)
    half_conjugate = product(left_inv, probe_mat, 0, 0).astype(HALF)
    conjugate = product(half_conjugate, right_inv).astype(HALF)
    left_times = (clip * product(left_q, gradient)).astype(HALF)
    whitened = product(left_times, right_q, 1, 1).astype(HALF)
    new_left = step_factor(
        left_q, 1.0, product(whitened, whitened, 1, 1), product(conjugate, conjugate, 1, 1)
    )
    new_right = step_factor(
        right_q, 1.0, product(whitened, whitened, 0, 0), product(conjugate, conjugate, 0, 0)
    )
    precond_left = product(new_left, new_left, 0, 0).astype(HALF)
    precond_right = product(new_right, new_right, 0, 0).astype(HALF)

    def my_rows(array):
        return pick(array.reshape(blocks, group, rows, -1), my_place, 1)

    middle = (clip * product(my_rows(precond_left).reshape(blocks * rows, size), gradient)).astype(HALF)
    result = product(middle, precond_right).astype(HALF).reshape(blocks, rows, -1)
    back = jnp.concatenate([my_rows(new_left), my_rows(new_right), result], axis=2)
    return [pick(back, my_block ^ k, 0) for k in range(blocks)]


def solution(mesh):
    return jax.shard_map(
        body,
        mesh=mesh,
        in_specs=(
            P("dp", None, None, None, "mp"),
            P("mp", None, "dp", None),
            P("mp", None, "dp", None),
            P("mp", None, "dp", None),
            P("mp", None),
        ),
        out_specs=(P(None, None, "dp", "mp"), P("mp", None, "dp", None)),
        check_vma=False,
    )
```

```python
import functools
import math

import jax
import jax.numpy as jnp
from jax import lax
from jax.experimental import pallas as pl
from jax.experimental.pallas import tpu as pltpu
from jax.sharding import PartitionSpec as P

CLIP_RMS = 0.3
LEARN_RATE = 0.1
EPS_NORM = 1e-06
LANES = 128
VMEM_GRANT = 16 * 2**20
FLOAT = jnp.float32
HALF = jnp.bfloat16


VMEM_SPEC = pl.BlockSpec(memory_space=pltpu.VMEM)
SMEM_SPEC = pl.BlockSpec(memory_space=pltpu.SMEM)


def product(left_op, right_op, left_dim=1, right_dim=0):
    return lax.dot_general(
        left_op, right_op, (((left_dim,), (right_dim,)), ((), ())), preferred_element_type=FLOAT
    )


def flip(array, devices, mask):
    return lax.ppermute(array, "dp", [(i, i ^ mask) for i in range(devices)])


def pick(array, index, axis):
    return lax.dynamic_index_in_dim(array, index, axis, keepdims=False)


def unflip(pieces, own):
    stacked = jnp.stack(pieces)
    return jnp.stack([pick(stacked, own ^ k, 0) for k in range(len(pieces))])


def call(kernel, out_shape, scratch, flops, smem, *operands, space=pltpu.VMEM):
    moved = sum(x.size * x.dtype.itemsize for x in (*operands, *jax.tree.leaves(out_shape)))
    return pl.pallas_call(
        kernel,
        out_shape=out_shape,
        in_specs=[SMEM_SPEC] * smem + [pl.BlockSpec(memory_space=space)] * (len(operands) - smem),
        out_specs=jax.tree.map(lambda _: VMEM_SPEC, out_shape),
        scratch_shapes=scratch,
        cost_estimate=pl.CostEstimate(flops=flops, bytes_accessed=moved, transcendentals=0),
        compiler_params=pltpu.CompilerParams(vmem_limit_bytes=VMEM_GRANT),
    )(*operands)


class Plan:
    def __init__(self, devices, blocks, size):
        self.devices, self.blocks, self.size = devices, blocks, size
        self.group = devices // blocks
        self.rows = size // devices
        self.first = [z * (size // blocks) // LANES * LANES for z in range(blocks)]

    def spots(self):
        offset = 0
        for z in range(self.blocks):
            for what in range(5):
                first = self.first[z] if what < 4 else 0
                yield z, what, first, offset
                offset += self.size - first

    def packed(self):
        return sum(self.size - first for _, _, first, _ in self.spots())


def choose_kernel(plan, where, slots, factors, inverses, probes, *refs):
    outs, done = refs[:-1], refs[-1]
    size, copies = plan.size, []
    for k, out in enumerate(outs):
        slot = slots[where[0] ^ k]
        parts = (
            (factors, out.at[:, : 2 * size]),
            (inverses, out.at[:, 2 * size : 4 * size]),
            (probes, out.at[:, 4 * size :]),
        )
        for i, (source, target) in enumerate(parts):
            copies.append(pltpu.make_async_copy(source.at[slot], target, done.at[3 * k + i]))
    for copy in copies:
        copy.start()
    for copy in copies:
        copy.wait()


def pack_kernel(plan, where, *refs):
    pieces, out, stack = refs[: plan.blocks], refs[-2], refs[-1]
    size = plan.size
    for k, piece in enumerate(pieces):
        stack[where[0] ^ k] = piece[...]
    for z, what, first, offset in plan.spots():
        out[:, offset : offset + size - first] = stack[z, :, what * size + first : (what + 1) * size]


def spread(plan, where, pieces, targets):
    size, rows = plan.size, plan.rows
    for z in range(1, plan.blocks):
        for target in targets[:4]:
            if target is not None and plan.first[z]:
                span = size // plan.blocks
                target[z * span : (z + 1) * span, : plan.first[z]] = jnp.zeros((span, plan.first[z]), HALF)
    for k, piece in enumerate(pieces):
        for z, what, first, offset in plan.spots():
            if targets[what] is not None:
                row = pl.multiple_of((z * plan.group + (where[1] ^ k)) * rows, rows)
                targets[what][pl.ds(row, rows), first:] = piece[:, offset : offset + size - first]


def probe_kernel(plan, where, *refs):
    pieces = refs[: plan.group]
    left, right, left_gram, right_gram, left_inv, right_inv, probe = refs[plan.group :]
    spread(plan, where, pieces, (left, right, left_inv, right_inv, probe))
    half_conjugate = product(left_inv[...], probe[...], 0, 0).astype(HALF)
    conjugate = product(half_conjugate, right_inv[...]).astype(HALF)
    left_gram[...] = product(conjugate, conjugate, 1, 1)
    right_gram[...] = product(conjugate, conjugate, 0, 0)


def relay_kernel(where, low_own, low_seen, high_own, high_seen, low_out, high_out):
    seen = low_seen[:, :, 1 - where[3]].astype(FLOAT)
    low_out[...] = (low_own[...].astype(FLOAT) + seen).astype(HALF)
    seen = high_seen[:, :, 1 - where[2]].astype(FLOAT)
    high_out[...] = (high_own[...].astype(FLOAT) + seen).astype(HALF)


def gather_kernel(where, own, low_seen, low_last, high_seen, high_last, *outs):
    middle = own.shape[1] // 2
    for k, out in enumerate(outs):
        block = where[0] ^ k
        low = own[block, :middle].astype(FLOAT) + low_seen[block, :, where[3]].astype(FLOAT)
        out[:middle] = (low + low_last[block].astype(FLOAT)).astype(HALF)
        high = own[block, middle:].astype(FLOAT) + high_seen[block, :, where[2]].astype(FLOAT)
        out[middle:] = (high + high_last[block].astype(FLOAT)).astype(HALF)


def sum_kernel(blocks, *refs):
    terms, (out, squares) = refs[:-2], refs[-2:]
    found, start = 0.0, 0
    for i in range(0, len(terms), blocks):
        total = terms[i][...].astype(FLOAT)
        for term in terms[i + 1 : i + blocks]:
            total = total + term[...].astype(FLOAT)
        out[start : start + total.shape[0]] = total.astype(HALF)
        start += total.shape[0]
        found = found + jnp.sum(jnp.sum(total * total, axis=(0, 1)))
    squares[...] = jnp.full(squares.shape, found)


def bound_of(limit, squares):
    return jnp.minimum(1.0, limit / jnp.sqrt(squares + EPS_NORM))


def whiten_kernel(plan, limit, where, *refs):
    left, right, pieces = refs[0], refs[1], refs[2 : 2 + plan.group]
    grad, left_gram, right_gram, own_clip = refs[2 + plan.group :]
    for k, piece in enumerate(pieces):
        for z in range(plan.blocks):
            row = pl.multiple_of((z * plan.group + (where[1] ^ k)) * plan.rows, plan.rows)
            grad[pl.ds(row, plan.rows), :] = piece[z]
    wide = grad[...].astype(FLOAT)
    clip = bound_of(limit, jnp.sum(wide * wide, keepdims=True))
    own_clip[...] = jnp.broadcast_to(clip, own_clip.shape)
    left_times = (clip * product(left[...], grad[...])).astype(HALF)
    whitened = product(left_times, right[...], 1, 1).astype(HALF)
    left_gram[...] = product(whitened, whitened, 1, 1)
    right_gram[...] = product(whitened, whitened, 0, 0)


def step_factor(factor, ratio, first_ref, second_ref):
    first, second = ratio * first_ref[...], second_ref[...]
    bound_value = jnp.max(jnp.abs(first + second), keepdims=True) + EPS_NORM
    row = lax.broadcasted_iota(jnp.int32, first.shape, 0)
    column = lax.broadcasted_iota(jnp.int32, first.shape, 1)
    change = jnp.where(row <= column, first - second, 0.0).astype(HALF)
    moved_rows = product(change, factor)
    return (factor.astype(FLOAT) - LEARN_RATE / bound_value * moved_rows).astype(HALF)


def finish_kernel(plan, limit, where, *refs):
    sums, refs = refs[: plan.group], refs[plan.group :]
    own_clip, left, right, grad, left_p, right_p, left_q, right_q = refs[:8]
    outs, (new_left, new_right, square, result) = refs[8:-4], refs[-4:]
    squares = sums[0][0:1, 0:1]
    for ref in sums[1:]:
        squares = squares + ref[0:1, 0:1]
    clip = bound_of(limit, squares)
    ratio = clip / own_clip[0:1, 0:1]
    ratio = ratio * ratio
    size, rows = plan.size, plan.rows
    new_left[...] = step_factor(left[...], ratio, left_p, left_q)
    new_right[...] = step_factor(right[...], ratio, right_p, right_q)
    square[...] = product(new_left[...], new_left[...], 0, 0).astype(HALF)
    precond_right = product(new_right[...], new_right[...], 0, 0).astype(HALF)

    def at(z):
        return pl.ds(pl.multiple_of((z * plan.group + where[1]) * rows, rows), rows)

    precond_left = jnp.concatenate([square[at(z), :] for z in range(plan.blocks)], axis=0)
    middle = (clip * product(precond_left, grad[...])).astype(HALF)
    result[...] = product(middle, precond_right).astype(HALF).reshape(plan.blocks, rows, size)
    for k, out in enumerate(outs):
        z = where[0] ^ k
        out[:, :size] = new_left[at(z), :]
        out[:, size : 2 * size] = new_right[at(z), :]
        out[:, 2 * size :] = result[z]


def place_kernel(plan, where, slots, old_state, *refs):
    pieces, (precond, new_state) = refs[: plan.blocks], refs[plan.blocks :]
    size = plan.size
    new_state[...] = old_state[...]
    for k, piece in enumerate(pieces):
        precond[where[0] ^ k] = piece[:, 2 * size :]
        new_state[slots[where[0] ^ k]] = piece[:, : 2 * size]


def shaped(shape, dtype=HALF):
    return jax.ShapeDtypeStruct(shape, dtype)


def body(partial_grads, factors, inverse_factors, probes, slot_table):
    devices = lax.axis_size("dp")
    halves = lax.axis_size("mp")
    me = lax.axis_index("dp")
    experts, block_rows, size, columns = partial_grads.shape[1:]
    blocks = experts * block_rows
    plan = Plan(devices, blocks, size)
    group, rows = plan.group, plan.rows
    my_block = me // group
    my_place = me % group
    my_low, my_high = my_place % 2, my_place // 2
    where = jnp.stack([my_block, my_place, my_low, my_high]).astype(jnp.int32)
    slot_row = slot_table[0]
    in_tiles = rows % 16 == 0
    limit = CLIP_RMS * math.sqrt(blocks * size * columns * halves)

    grads = partial_grads[0].reshape(blocks, blocks, group, rows, columns)
    middle = blocks // 2
    if in_tiles and group == 4:

        def part(array, half, high, low):
            start = (0, (half or 0) * middle, high, low, 0, 0)
            extent = (
                blocks,
                blocks if half is None else middle,
                2 if high is None else 1,
                2 if low is None else 1,
                rows,
                columns,
            )
            array = array.reshape(blocks, blocks, 2, 2, rows, columns)
            cut = lax.dynamic_slice(array, [0 if i is None else i for i in start], extent)
            return cut.reshape([n for i, n in enumerate(extent) if n > 1 or i not in (2, 3)])

        low_seen = flip(part(grads, 0, None, 1 - my_low), devices, 1)
        high_seen = flip(part(grads, 1, 1 - my_high, None), devices, 2)
        low_sent, high_sent = call(
            relay_kernel,
            (shaped((blocks, middle, rows, columns)),) * 2,
            [],
            0,
            1,
            where,
            part(grads, 0, 1 - my_high, my_low),
            low_seen,
            part(grads, 1, my_high, 1 - my_low),
            high_seen,
        )
        parts = call(
            gather_kernel,
            tuple(shaped((blocks, rows, columns)) for _ in range(blocks)),
            [],
            0,
            1,
            where,
            part(grads, None, my_high, my_low),
            low_seen,
            flip(low_sent, devices, 2),
            high_seen,
            flip(high_sent, devices, 1),
        )
    else:
        halves_of = []
        masks = [1 << i for i in range(group.bit_length() - 1)]
        for half, order in enumerate((masks, masks[::-1])):
            kept = grads[:, half * middle : (half + 1) * middle].astype(FLOAT)
            kept = kept.reshape(blocks, middle, *[2] * len(masks), rows, columns)
            left = sorted(masks, reverse=True)
            for mask in order:
                axis, bit = 2 + left.index(mask), my_place // mask % 2
                sent = pick(kept, 1 - bit, axis).astype(HALF)
                left.remove(mask)
                kept = pick(kept, bit, axis) + flip(sent, devices, mask)
            halves_of.append(kept)
        total = jnp.concatenate(halves_of, axis=1).astype(HALF)
        parts = [pick(total, my_block ^ k, 0) for k in range(blocks)]

    old_state = factors[0]
    if in_tiles:
        pieces = call(
            functools.partial(choose_kernel, plan),
            tuple(shaped((rows, 5 * size)) for _ in range(blocks)),
            [pltpu.SemaphoreType.DMA((3 * blocks,))],
            0,
            2,
            where,
            slot_row,
            old_state,
            inverse_factors[0],
            probes[0],
            space=pltpu.HBM,
        )
    else:
        wide = jnp.concatenate([old_state, inverse_factors[0], probes[0]], axis=2)
        pieces = [pick(wide, slot_row[my_block ^ k], 0) for k in range(blocks)]
    pieces = [pieces[0]] + [flip(pieces[k], devices, k * group) for k in range(1, blocks)]
    if in_tiles:
        quarter = call(
            functools.partial(pack_kernel, plan),
            shaped((rows, plan.packed())),
            [pltpu.VMEM((blocks, rows, 5 * size), HALF)],
            0,
            1,
            where,
            *pieces,
        )
    else:
        quarter = unflip(pieces, my_block)

    terms = [parts[0]] + [flip(parts[k], devices, k * group) for k in range(1, blocks)]
    grad_quarter, squares = call(
        functools.partial(sum_kernel, blocks),
        (shaped((blocks, rows, columns)), shaped((8, LANES), FLOAT)),
        [],
        0,
        0,
        *terms,
    )

    states = [quarter] + [flip(quarter, devices, k) for k in range(1, group)]
    quarters = [grad_quarter] + [flip(grad_quarter, devices, k) for k in range(1, group)]

    squares = functools.reduce(
        jnp.add,
        [squares] + [flip(squares, devices, k * group) for k in range(1, blocks)],
    )
    bit = 1
    while bit < halves:
        other = lax.ppermute(squares, "mp", [(i, i ^ bit) for i in range(halves)])
        squares = squares + other
        bit *= 2
    sums = [squares] + [flip(squares, devices, k) for k in range(1, group)]

    gram = shaped((size, size), FLOAT)
    square = shaped((size, size))
    matmul = 2 * size**3
    if in_tiles:
        left_q, right_q, left_c, right_c = call(
            functools.partial(probe_kernel, plan),
            (square, square, gram, gram),
            [pltpu.VMEM((size, size), HALF)] * 3,
            4 * matmul,
            1,
            where,
            *states,
        )
        gradient, left_w, right_w, own_clip = call(
            functools.partial(whiten_kernel, plan, limit),
            (shaped((size, columns)), gram, gram, shaped((8, LANES), FLOAT)),
            [],
            4 * matmul,
            1,
            where,
            left_q,
            right_q,
            *quarters,
        )
        back = call(
            functools.partial(finish_kernel, plan, limit),
            tuple(shaped((rows, 2 * size + columns)) for _ in range(blocks)),
            [pltpu.VMEM((size, size), HALF)] * 3 + [pltpu.VMEM((blocks, rows, columns), HALF)],
            5 * matmul,
            1,
            where,
            *sums,
            own_clip,
            left_q,
            right_q,
            gradient,
            left_w,
            right_w,
            left_c,
            right_c,
        )
    else:
        back = plain_block(plan, limit, my_block, my_place, sums, states, quarters)
    back = [back[0]] + [flip(back[k], devices, k * group) for k in range(1, blocks)]
    precond, new_state = call(
        functools.partial(place_kernel, plan),
        (shaped((blocks, rows, columns)), shaped(old_state.shape)),
        [],
        0,
        2,
        where,
        slot_row,
        old_state,
        *back,
    )
    return (precond.reshape(experts, block_rows, rows, columns), new_state[None])


def plain_block(plan, limit, my_block, my_place, sums, states, quarters):
    size, blocks, group, rows = plan.size, plan.blocks, plan.group, plan.rows
    state = unflip(states, my_place).transpose(1, 0, 2, 3).reshape(size, 5 * size)
    gradient = unflip(quarters, my_place).transpose(1, 0, 2, 3).reshape(size, -1)
    clip = bound_of(limit, functools.reduce(jnp.add, sums)[0:1, 0:1])
    left_q, right_q, left_inv, right_inv, probe_mat = jnp.split(state, 5, axis=1)
    half_conjugate = product(left_inv, probe_mat, 0, 0).astype(HALF)
    conjugate = product(half_conjugate, right_inv).astype(HALF)
    left_times = (clip * product(left_q, gradient)).astype(HALF)
    whitened = product(left_times, right_q, 1, 1).astype(HALF)
    new_left = step_factor(
        left_q, 1.0, product(whitened, whitened, 1, 1), product(conjugate, conjugate, 1, 1)
    )
    new_right = step_factor(
        right_q, 1.0, product(whitened, whitened, 0, 0), product(conjugate, conjugate, 0, 0)
    )
    precond_left = product(new_left, new_left, 0, 0).astype(HALF)
    precond_right = product(new_right, new_right, 0, 0).astype(HALF)

    def my_rows(array):
        return pick(array.reshape(blocks, group, rows, -1), my_place, 1)

    middle = (clip * product(my_rows(precond_left).reshape(blocks * rows, size), gradient)).astype(HALF)
    result = product(middle, precond_right).astype(HALF).reshape(blocks, rows, -1)
    back = jnp.concatenate([my_rows(new_left), my_rows(new_right), result], axis=2)
    return [pick(back, my_block ^ k, 0) for k in range(blocks)]


def solution(mesh):
    return jax.shard_map(
        body,
        mesh=mesh,
        in_specs=(
            P("dp", None, None, None, "mp"),
            P("mp", None, "dp", None),
            P("mp", None, "dp", None),
            P("mp", None, "dp", None),
            P("mp", None),
        ),
        out_specs=(P(None, None, "dp", "mp"), P("mp", None, "dp", None)),
        check_vma=False,
    )
```

```python
import functools
import math

import jax
import jax.numpy as jnp
from jax import lax
from jax.experimental import pallas as pl
from jax.experimental.pallas import tpu as pltpu
from jax.sharding import PartitionSpec as P

CLIP_RMS = 0.3
LEARN_RATE = 0.1
EPS_NORM = 1e-06
LANES = 128
VMEM_GRANT = 16 * 2**20
FLOAT = jnp.float32
HALF = jnp.bfloat16


VMEM_SPEC = pl.BlockSpec(memory_space=pltpu.VMEM)
SMEM_SPEC = pl.BlockSpec(memory_space=pltpu.SMEM)


def product(left_op, right_op, left_dim=1, right_dim=0):
    return lax.dot_general(
        left_op, right_op, (((left_dim,), (right_dim,)), ((), ())), preferred_element_type=FLOAT
    )


def flip(array, devices, mask):
    return lax.ppermute(array, "dp", [(i, i ^ mask) for i in range(devices)])


def pick(array, index, axis):
    return lax.dynamic_index_in_dim(array, index, axis, keepdims=False)


def unflip(pieces, own):
    stacked = jnp.stack(pieces)
    return jnp.stack([pick(stacked, own ^ k, 0) for k in range(len(pieces))])


def call(kernel, out_shape, scratch, flops, smem, *operands, space=pltpu.VMEM):
    moved = sum(x.size * x.dtype.itemsize for x in (*operands, *jax.tree.leaves(out_shape)))
    return pl.pallas_call(
        kernel,
        out_shape=out_shape,
        in_specs=[SMEM_SPEC] * smem + [pl.BlockSpec(memory_space=space)] * (len(operands) - smem),
        out_specs=jax.tree.map(lambda _: VMEM_SPEC, out_shape),
        scratch_shapes=scratch,
        cost_estimate=pl.CostEstimate(flops=flops, bytes_accessed=moved, transcendentals=0),
        compiler_params=pltpu.CompilerParams(vmem_limit_bytes=VMEM_GRANT),
    )(*operands)


class Plan:
    def __init__(self, devices, blocks, size):
        self.devices, self.blocks, self.size = devices, blocks, size
        self.group = devices // blocks
        self.rows = size // devices
        self.first = [z * (size // blocks) // LANES * LANES for z in range(blocks)]

    def spots(self):
        offset = 0
        for z in range(self.blocks):
            for what in range(5):
                first = self.first[z] if what < 4 else 0
                yield z, what, first, offset
                offset += self.size - first

    def split(self):
        half = self.packed() // 2
        return min((offset for _, _, _, offset in self.spots()), key=lambda x: abs(x - half))

    def packed(self):
        return sum(self.size - first for _, _, first, _ in self.spots())


def choose_kernel(plan, where, slots, factors, inverses, probes, *refs):
    outs, done = refs[:-1], refs[-1]
    size, copies = plan.size, []
    for k, out in enumerate(outs):
        slot = slots[where[0] ^ k]
        parts = (
            (factors, out.at[:, : 2 * size]),
            (inverses, out.at[:, 2 * size : 4 * size]),
            (probes, out.at[:, 4 * size :]),
        )
        for i, (source, target) in enumerate(parts):
            copies.append(pltpu.make_async_copy(source.at[slot], target, done.at[3 * k + i]))
    for copy in copies:
        copy.start()
    for copy in copies:
        copy.wait()


def pack_kernel(plan, where, *refs):
    pieces, out, stack = refs[: plan.blocks], refs[-2], refs[-1]
    size = plan.size
    for k, piece in enumerate(pieces):
        stack[where[0] ^ k] = piece[...]
    for z, what, first, offset in plan.spots():
        out[:, offset : offset + size - first] = stack[z, :, what * size + first : (what + 1) * size]


def spread(plan, where, pieces, targets):
    size, rows = plan.size, plan.rows
    for z in range(1, plan.blocks):
        for target in targets[:4]:
            if plan.first[z]:
                span = size // plan.blocks
                target[z * span : (z + 1) * span, : plan.first[z]] = jnp.zeros((span, plan.first[z]), HALF)
    for k in range(plan.group):
        for z, what, first, offset in plan.spots():
            piece, start = pieces[k], offset
            if len(pieces) > plan.group and k == plan.group - 1 and offset >= plan.split():
                piece, start = pieces[k + 1], offset - plan.split()
            row = pl.multiple_of((z * plan.group + (where[1] ^ k)) * rows, rows)
            targets[what][pl.ds(row, rows), first:] = piece[:, start : start + size - first]


def probe_kernel(plan, where, *refs):
    pieces = refs[:-7]
    left, right, left_gram, right_gram, left_inv, right_inv, probe = refs[-7:]
    spread(plan, where, pieces, (left, right, left_inv, right_inv, probe))
    half_conjugate = product(left_inv[...], probe[...], 0, 0).astype(HALF)
    conjugate = product(half_conjugate, right_inv[...]).astype(HALF)
    left_gram[...] = product(conjugate, conjugate, 1, 1)
    right_gram[...] = product(conjugate, conjugate, 0, 0)


def relay_kernel(where, own, low_own, low_seen, high_own, high_seen, kept, low_out, high_out):
    middle = own.shape[1] // 2

    def add(mine, seen):
        return mine.astype(FLOAT) + seen.astype(FLOAT)

    kept[:, :middle] = add(own[:, :middle], low_seen[:, :, where[3]])
    kept[:, middle:] = add(own[:, middle:], high_seen[:, :, where[2]])
    low_out[...] = add(low_own[...], low_seen[:, :, 1 - where[3]]).astype(HALF)
    high_out[...] = add(high_own[...], high_seen[:, :, 1 - where[2]]).astype(HALF)


def gather_kernel(where, kept, low_last, high_last, *outs):
    middle = kept.shape[1] // 2
    for k, out in enumerate(outs):
        block = where[0] ^ k
        out[:middle] = (kept[block, :middle] + low_last[block].astype(FLOAT)).astype(HALF)
        out[middle:] = (kept[block, middle:] + high_last[block].astype(FLOAT)).astype(HALF)


def sum_kernel(blocks, *refs):
    terms, (out, squares) = refs[:-2], refs[-2:]
    found, start = 0.0, 0
    for i in range(0, len(terms), blocks):
        total = terms[i][...].astype(FLOAT)
        for term in terms[i + 1 : i + blocks]:
            total = total + term[...].astype(FLOAT)
        out[start : start + total.shape[0]] = total.astype(HALF)
        start += total.shape[0]
        found = found + jnp.sum(jnp.sum(total * total, axis=(0, 1)))
    squares[...] = jnp.full(squares.shape, found)


def bound_of(limit, squares):
    return jnp.minimum(1.0, limit / jnp.sqrt(squares + EPS_NORM))


def whiten_kernel(plan, limit, where, *refs):
    left, right, pieces = refs[0], refs[1], refs[2 : 2 + plan.group]
    grad, left_gram, right_gram, own_clip = refs[2 + plan.group :]
    for k, piece in enumerate(pieces):
        for z in range(plan.blocks):
            row = pl.multiple_of((z * plan.group + (where[1] ^ k)) * plan.rows, plan.rows)
            grad[pl.ds(row, plan.rows), :] = piece[z]
    wide = grad[...].astype(FLOAT)
    clip = bound_of(limit, jnp.sum(wide * wide, keepdims=True))
    own_clip[...] = jnp.broadcast_to(clip, own_clip.shape)
    left_times = (clip * product(left[...], grad[...])).astype(HALF)
    whitened = product(left_times, right[...], 1, 1).astype(HALF)
    left_gram[...] = product(whitened, whitened, 1, 1)
    right_gram[...] = product(whitened, whitened, 0, 0)


def step_factor(factor, ratio, first_ref, second_ref):
    first, second = ratio * first_ref[...], second_ref[...]
    bound_value = jnp.max(jnp.abs(first + second), keepdims=True) + EPS_NORM
    row = lax.broadcasted_iota(jnp.int32, first.shape, 0)
    column = lax.broadcasted_iota(jnp.int32, first.shape, 1)
    change = jnp.where(row <= column, first - second, 0.0).astype(HALF)
    moved_rows = product(change, factor)
    return (factor.astype(FLOAT) - LEARN_RATE / bound_value * moved_rows).astype(HALF)


def clip_of(limit, squares):
    return bound_of(limit, squares[0:1, 0:1])


def factor_kernel(plan, limit, where, *refs):
    squares, own_clip, left, right, left_p, right_p, left_q, right_q = refs[:8]
    new_left, new_right, outs = refs[8], refs[9], refs[10:]
    ratio = clip_of(limit, squares) / own_clip[0:1, 0:1]
    ratio = ratio * ratio
    size, rows = plan.size, plan.rows
    new_left[...] = step_factor(left[...], ratio, left_p, left_q)
    new_right[...] = step_factor(right[...], ratio, right_p, right_q)
    for k, out in enumerate(outs):
        row = pl.multiple_of(((where[0] ^ k) * plan.group + where[1]) * rows, rows)
        out[:, :size] = new_left[pl.ds(row, rows), :]
        out[:, size:] = new_right[pl.ds(row, rows), :]


def result_kernel(plan, limit, where, squares, new_left, new_right, grad, *refs):
    outs, (square, result) = refs[:-2], refs[-2:]
    size, rows = plan.size, plan.rows
    square[...] = product(new_left[...], new_left[...], 0, 0).astype(HALF)
    precond_right = product(new_right[...], new_right[...], 0, 0).astype(HALF)
    starts = [pl.multiple_of((z * plan.group + where[1]) * rows, rows) for z in range(plan.blocks)]
    precond_left = jnp.concatenate([square[pl.ds(row, rows), :] for row in starts], axis=0)
    middle = (clip_of(limit, squares) * product(precond_left, grad[...])).astype(HALF)
    result[...] = product(middle, precond_right).astype(HALF).reshape(plan.blocks, rows, size)
    for k, out in enumerate(outs):
        out[...] = result[where[0] ^ k]


def place_kernel(plan, where, slots, old_state, *refs):
    pieces, (precond, new_state) = refs[:-2], refs[-2:]
    new_state[...] = old_state[...]
    for k in range(plan.blocks):
        new_state[slots[where[0] ^ k]] = pieces[k][...]
        precond[where[0] ^ k] = pieces[plan.blocks + k][...]


def shaped(shape, dtype=HALF):
    return jax.ShapeDtypeStruct(shape, dtype)


def body(partial_grads, factors, inverse_factors, probes, slot_table):
    devices = lax.axis_size("dp")
    halves = lax.axis_size("mp")
    me = lax.axis_index("dp")
    experts, block_rows, size, columns = partial_grads.shape[1:]
    blocks = experts * block_rows
    plan = Plan(devices, blocks, size)
    group, rows = plan.group, plan.rows
    my_block = me // group
    my_place = me % group
    my_low, my_high = my_place % 2, my_place // 2
    where = jnp.stack([my_block, my_place, my_low, my_high]).astype(jnp.int32)
    slot_row = slot_table[0]
    in_tiles = rows % 16 == 0
    limit = CLIP_RMS * math.sqrt(blocks * size * columns * halves)

    grads = partial_grads[0].reshape(blocks, blocks, group, rows, columns)
    middle = blocks // 2
    if in_tiles and group == 4:

        def part(array, half, high, low):
            start = (0, (half or 0) * middle, high, low, 0, 0)
            extent = (
                blocks,
                blocks if half is None else middle,
                2 if high is None else 1,
                2 if low is None else 1,
                rows,
                columns,
            )
            array = array.reshape(blocks, blocks, 2, 2, rows, columns)
            cut = lax.dynamic_slice(array, [0 if i is None else i for i in start], extent)
            return cut.reshape([n for i, n in enumerate(extent) if n > 1 or i not in (2, 3)])

        low_seen = flip(part(grads, 0, None, 1 - my_low), devices, 1)
        high_seen = flip(part(grads, 1, 1 - my_high, None), devices, 2)
        kept, low_sent, high_sent = call(
            relay_kernel,
            (shaped((blocks, blocks, rows, columns), FLOAT),)
            + (shaped((blocks, middle, rows, columns)),) * 2,
            [],
            0,
            1,
            where,
            part(grads, None, my_high, my_low),
            part(grads, 0, 1 - my_high, my_low),
            low_seen,
            part(grads, 1, my_high, 1 - my_low),
            high_seen,
        )
        parts = call(
            gather_kernel,
            tuple(shaped((blocks, rows, columns)) for _ in range(blocks)),
            [],
            0,
            1,
            where,
            kept,
            flip(low_sent, devices, 2),
            flip(high_sent, devices, 1),
        )
    else:
        halves_of = []
        masks = [1 << i for i in range(group.bit_length() - 1)]
        for half, order in enumerate((masks, masks[::-1])):
            kept = grads[:, half * middle : (half + 1) * middle].astype(FLOAT)
            kept = kept.reshape(blocks, middle, *[2] * len(masks), rows, columns)
            left = sorted(masks, reverse=True)
            for mask in order:
                axis, bit = 2 + left.index(mask), my_place // mask % 2
                sent = pick(kept, 1 - bit, axis).astype(HALF)
                left.remove(mask)
                kept = pick(kept, bit, axis) + flip(sent, devices, mask)
            halves_of.append(kept)
        total = jnp.concatenate(halves_of, axis=1).astype(HALF)
        parts = [pick(total, my_block ^ k, 0) for k in range(blocks)]

    old_state = factors[0]
    if in_tiles:
        pieces = call(
            functools.partial(choose_kernel, plan),
            tuple(shaped((rows, 5 * size)) for _ in range(blocks)),
            [pltpu.SemaphoreType.DMA((3 * blocks,))],
            0,
            2,
            where,
            slot_row,
            old_state,
            inverse_factors[0],
            probes[0],
            space=pltpu.HBM,
        )
    else:
        wide = jnp.concatenate([old_state, inverse_factors[0], probes[0]], axis=2)
        pieces = [pick(wide, slot_row[my_block ^ k], 0) for k in range(blocks)]
    pieces = [pieces[0]] + [flip(pieces[k], devices, k * group) for k in range(1, blocks)]
    if in_tiles:
        quarter = call(
            functools.partial(pack_kernel, plan),
            shaped((rows, plan.packed())),
            [pltpu.VMEM((blocks, rows, 5 * size), HALF)],
            0,
            1,
            where,
            *pieces,
        )
    else:
        quarter = unflip(pieces, my_block)

    terms = [parts[0]] + [flip(parts[k], devices, k * group) for k in range(1, blocks)]
    grad_quarter, squares = call(
        functools.partial(sum_kernel, blocks),
        (shaped((blocks, rows, columns)), shaped((8, LANES), FLOAT)),
        [],
        0,
        0,
        *terms,
    )

    if in_tiles and group == 4:
        states = [quarter] + [flip(quarter, devices, k) for k in (1, 2)]
        cut = states[1][:, : plan.split()], states[2][:, plan.split() :]
        states += [flip(cut[i], devices, 2 - i) for i in range(2)]
    else:
        states = [quarter] + [flip(quarter, devices, k) for k in range(1, group)]
    quarters = [grad_quarter] + [flip(grad_quarter, devices, k) for k in range(1, group)]

    squares = functools.reduce(
        jnp.add,
        [squares] + [flip(squares, devices, k * group) for k in range(1, blocks)],
    )
    bit = 1
    while bit < halves:
        other = lax.ppermute(squares, "mp", [(i, i ^ bit) for i in range(halves)])
        squares = squares + other
        bit *= 2
    bit = 1
    while bit < group:
        squares = squares + flip(squares, devices, bit)
        bit *= 2

    gram = shaped((size, size), FLOAT)
    square = shaped((size, size))
    matmul = 2 * size**3
    if in_tiles:
        left_q, right_q, left_c, right_c = call(
            functools.partial(probe_kernel, plan),
            (square, square, gram, gram),
            [pltpu.VMEM((size, size), HALF)] * 3,
            4 * matmul,
            1,
            where,
            *states,
        )
        gradient, left_w, right_w, own_clip = call(
            functools.partial(whiten_kernel, plan, limit),
            (shaped((size, columns)), gram, gram, shaped((8, LANES), FLOAT)),
            [],
            4 * matmul,
            1,
            where,
            left_q,
            right_q,
            *quarters,
        )
        new_left, new_right, *back = call(
            functools.partial(factor_kernel, plan, limit),
            (square, square) + tuple(shaped((rows, 2 * size)) for _ in range(blocks)),
            [],
            2 * matmul,
            1,
            where,
            squares,
            own_clip,
            left_q,
            right_q,
            left_w,
            right_w,
            left_c,
            right_c,
        )
        last = call(
            functools.partial(result_kernel, plan, limit),
            tuple(shaped((rows, columns)) for _ in range(blocks)),
            [pltpu.VMEM((size, size), HALF), pltpu.VMEM((blocks, rows, columns), HALF)],
            3 * matmul,
            1,
            where,
            squares,
            new_left,
            new_right,
            gradient,
        )
    else:
        back, last = plain_block(plan, limit, my_block, my_place, squares, states, quarters)
    back = [back[0]] + [flip(back[k], devices, k * group) for k in range(1, blocks)]
    last = [last[0]] + [flip(last[k], devices, k * group) for k in range(1, blocks)]
    precond, new_state = call(
        functools.partial(place_kernel, plan),
        (shaped((blocks, rows, columns)), shaped(old_state.shape)),
        [],
        0,
        2,
        where,
        slot_row,
        old_state,
        *back,
        *last,
    )
    return (precond.reshape(experts, block_rows, rows, columns), new_state[None])


def plain_block(plan, limit, my_block, my_place, squares, states, quarters):
    size, blocks, group, rows = plan.size, plan.blocks, plan.group, plan.rows
    state = unflip(states, my_place).transpose(1, 0, 2, 3).reshape(size, 5 * size)
    gradient = unflip(quarters, my_place).transpose(1, 0, 2, 3).reshape(size, -1)
    clip = clip_of(limit, squares)
    left_q, right_q, left_inv, right_inv, probe_mat = jnp.split(state, 5, axis=1)
    half_conjugate = product(left_inv, probe_mat, 0, 0).astype(HALF)
    conjugate = product(half_conjugate, right_inv).astype(HALF)
    left_times = (clip * product(left_q, gradient)).astype(HALF)
    whitened = product(left_times, right_q, 1, 1).astype(HALF)
    new_left = step_factor(
        left_q, 1.0, product(whitened, whitened, 1, 1), product(conjugate, conjugate, 1, 1)
    )
    new_right = step_factor(
        right_q, 1.0, product(whitened, whitened, 0, 0), product(conjugate, conjugate, 0, 0)
    )
    precond_left = product(new_left, new_left, 0, 0).astype(HALF)
    precond_right = product(new_right, new_right, 0, 0).astype(HALF)

    def my_rows(array):
        return pick(array.reshape(blocks, group, rows, -1), my_place, 1)

    middle = (clip * product(my_rows(precond_left).reshape(blocks * rows, size), gradient)).astype(HALF)
    result = product(middle, precond_right).astype(HALF).reshape(blocks, rows, -1)
    back = jnp.concatenate([my_rows(new_left), my_rows(new_right)], axis=2)
    order = [my_block ^ k for k in range(blocks)]
    return [pick(back, b, 0) for b in order], [pick(result, b, 0) for b in order]


def solution(mesh):
    return jax.shard_map(
        body,
        mesh=mesh,
        in_specs=(
            P("dp", None, None, None, "mp"),
            P("mp", None, "dp", None),
            P("mp", None, "dp", None),
            P("mp", None, "dp", None),
            P("mp", None),
        ),
        out_specs=(P(None, None, "dp", "mp"), P("mp", None, "dp", None)),
        check_vma=False,
    )
```

```python
import functools
import math

import jax
import jax.numpy as jnp
from jax import lax
from jax.experimental import pallas as pl
from jax.experimental.pallas import tpu as pltpu
from jax.sharding import PartitionSpec as P

CLIP_RMS = 0.3
LEARN_RATE = 0.1
EPS_NORM = 1e-06
LANES = 128
VMEM_GRANT = 16 * 2**20
FLOAT = jnp.float32
HALF = jnp.bfloat16


VMEM_SPEC = pl.BlockSpec(memory_space=pltpu.VMEM)
SMEM_SPEC = pl.BlockSpec(memory_space=pltpu.SMEM)


def product(left_op, right_op, left_dim=1, right_dim=0):
    return lax.dot_general(
        left_op, right_op, (((left_dim,), (right_dim,)), ((), ())), preferred_element_type=FLOAT
    )


def flip(array, devices, mask):
    return lax.ppermute(array, "dp", [(i, i ^ mask) for i in range(devices)])


def pick(array, index, axis):
    return lax.dynamic_index_in_dim(array, index, axis, keepdims=False)


def unflip(pieces, own):
    stacked = jnp.stack(pieces)
    return jnp.stack([pick(stacked, own ^ k, 0) for k in range(len(pieces))])


def call(kernel, out_shape, scratch, flops, smem, *operands, space=pltpu.VMEM):
    moved = sum(x.size * x.dtype.itemsize for x in (*operands, *jax.tree.leaves(out_shape)))
    return pl.pallas_call(
        kernel,
        out_shape=out_shape,
        in_specs=[SMEM_SPEC] * smem + [pl.BlockSpec(memory_space=space)] * (len(operands) - smem),
        out_specs=jax.tree.map(lambda _: VMEM_SPEC, out_shape),
        scratch_shapes=scratch,
        cost_estimate=pl.CostEstimate(flops=flops, bytes_accessed=moved, transcendentals=0),
        compiler_params=pltpu.CompilerParams(vmem_limit_bytes=VMEM_GRANT),
    )(*operands)


class Plan:
    def __init__(self, devices, blocks, size):
        self.devices, self.blocks, self.size = devices, blocks, size
        self.group = devices // blocks
        self.rows = size // devices
        self.first = [z * (size // blocks) // LANES * LANES for z in range(blocks)]

    def spots(self):
        offset = 0
        for z in range(self.blocks):
            for what in range(5):
                first = self.first[z] if what < 4 else 0
                yield z, what, first, offset
                offset += self.size - first

    def split(self):
        half = self.packed() // 2
        return min((offset for _, _, _, offset in self.spots()), key=lambda x: abs(x - half))

    def packed(self):
        return sum(self.size - first for _, _, first, _ in self.spots())


def choose_kernel(plan, where, slots, factors, inverses, probes, *refs):
    outs, done = refs[:-1], refs[-1]
    size, copies = plan.size, []
    for k, out in enumerate(outs):
        slot = slots[where[0] ^ k]
        parts = (
            (factors, out.at[:, : 2 * size]),
            (inverses, out.at[:, 2 * size : 4 * size]),
            (probes, out.at[:, 4 * size :]),
        )
        for i, (source, target) in enumerate(parts):
            copies.append(pltpu.make_async_copy(source.at[slot], target, done.at[3 * k + i]))
    for copy in copies:
        copy.start()
    for copy in copies:
        copy.wait()


def pack_kernel(plan, where, *refs):
    pieces, out, stack = refs[: plan.blocks], refs[-2], refs[-1]
    size = plan.size
    for k, piece in enumerate(pieces):
        stack[where[0] ^ k] = piece[...]
    for z, what, first, offset in plan.spots():
        out[:, offset : offset + size - first] = stack[z, :, what * size + first : (what + 1) * size]


def spread(plan, where, pieces, targets):
    size, rows = plan.size, plan.rows
    for z in range(1, plan.blocks):
        for target in targets[:4]:
            if plan.first[z]:
                span = size // plan.blocks
                target[z * span : (z + 1) * span, : plan.first[z]] = jnp.zeros((span, plan.first[z]), HALF)
    for k in range(plan.group):
        for z, what, first, offset in plan.spots():
            piece, start = pieces[k], offset
            if len(pieces) > plan.group and k == plan.group - 1 and offset >= plan.split():
                piece, start = pieces[k + 1], offset - plan.split()
            row = pl.multiple_of((z * plan.group + (where[1] ^ k)) * rows, rows)
            targets[what][pl.ds(row, rows), first:] = piece[:, start : start + size - first]


def probe_kernel(plan, where, *refs):
    pieces = refs[:-7]
    left, right, left_gram, right_gram, left_inv, right_inv, probe = refs[-7:]
    spread(plan, where, pieces, (left, right, left_inv, right_inv, probe))
    h = plan.size // 2
    half_conjugate = jnp.concatenate(
        [product(left_inv[:h, :h], probe[:h, :], 0, 0), product(left_inv[:, h:], probe[...], 0, 0)],
        axis=0,
    ).astype(HALF)
    conjugate = jnp.concatenate(
        [product(half_conjugate[:, :h], right_inv[:h, :h]), product(half_conjugate, right_inv[:, h:])],
        axis=1,
    ).astype(HALF)
    gram_rows(left_gram, conjugate)
    gram_columns(right_gram, conjugate)


def relay_kernel(where, own, low_own, low_seen, high_own, high_seen, kept, low_out, high_out):
    middle = own.shape[1] // 2

    def add(mine, seen):
        return mine.astype(FLOAT) + seen.astype(FLOAT)

    kept[:, :middle] = add(own[:, :middle], low_seen[:, :, where[3]])
    kept[:, middle:] = add(own[:, middle:], high_seen[:, :, where[2]])
    low_out[...] = add(low_own[...], low_seen[:, :, 1 - where[3]]).astype(HALF)
    high_out[...] = add(high_own[...], high_seen[:, :, 1 - where[2]]).astype(HALF)


def gather_kernel(where, kept, low_last, high_last, *outs):
    middle = kept.shape[1] // 2
    for k, out in enumerate(outs):
        block = where[0] ^ k
        out[:middle] = (kept[block, :middle] + low_last[block].astype(FLOAT)).astype(HALF)
        out[middle:] = (kept[block, middle:] + high_last[block].astype(FLOAT)).astype(HALF)


def sum_kernel(blocks, *refs):
    terms, (out, squares) = refs[:-2], refs[-2:]
    found, start = 0.0, 0
    for i in range(0, len(terms), blocks):
        total = terms[i][...].astype(FLOAT)
        for term in terms[i + 1 : i + blocks]:
            total = total + term[...].astype(FLOAT)
        out[start : start + total.shape[0]] = total.astype(HALF)
        start += total.shape[0]
        found = found + jnp.sum(jnp.sum(total * total, axis=(0, 1)))
    squares[...] = jnp.full(squares.shape, found)


def bound_of(limit, squares):
    return jnp.minimum(1.0, limit / jnp.sqrt(squares + EPS_NORM))


def whiten_kernel(plan, limit, where, *refs):
    left, right, pieces = refs[0], refs[1], refs[2 : 2 + plan.group]
    grad, left_gram, right_gram, own_clip = refs[2 + plan.group :]
    for k, piece in enumerate(pieces):
        for z in range(plan.blocks):
            row = pl.multiple_of((z * plan.group + (where[1] ^ k)) * plan.rows, plan.rows)
            grad[pl.ds(row, plan.rows), :] = piece[z]
    wide = grad[...].astype(FLOAT)
    clip = bound_of(limit, jnp.sum(wide * wide, keepdims=True))
    own_clip[...] = jnp.broadcast_to(clip, own_clip.shape)
    h = plan.size // 2
    left_times = jnp.concatenate(
        [product(left[:h, :], grad[...]), product(left[h:, h:], grad[h:, :])], axis=0
    )
    left_times = (clip * left_times).astype(HALF)
    whitened = jnp.concatenate(
        [product(left_times, right[:h, :], 1, 1), product(left_times[:, h:], right[h:, h:], 1, 1)],
        axis=1,
    ).astype(HALF)
    gram_rows(left_gram, whitened)
    gram_columns(right_gram, whitened)


def step_factor(factor, ratio, first_ref, second_ref):
    first, second = ratio * first_ref[...], second_ref[...]
    bound_value = jnp.max(jnp.abs(first + second), keepdims=True) + EPS_NORM
    row = lax.broadcasted_iota(jnp.int32, first.shape, 0)
    column = lax.broadcasted_iota(jnp.int32, first.shape, 1)
    change = jnp.where(row <= column, first - second, 0.0).astype(HALF)
    moved_rows = product(change, factor)
    return (factor.astype(FLOAT) - LEARN_RATE / bound_value * moved_rows).astype(HALF)


def clip_of(limit, squares):
    return bound_of(limit, squares[0:1, 0:1])


def gram_rows(out, matrix):
    h = out.shape[0] // 2
    out[:h, :] = product(matrix[:h, :], matrix, 1, 1)
    out[h:, h:] = product(matrix[h:, :], matrix[h:, :], 1, 1)


def gram_columns(out, matrix):
    h = out.shape[0] // 2
    out[:h, :] = product(matrix[:, :h], matrix, 0, 0)
    out[h:, h:] = product(matrix[:, h:], matrix[:, h:], 0, 0)


def move_factor(out, factor, ratio, first, second):
    h = out.shape[0] // 2
    firsts = ratio * first[:h, :], ratio * first[h:, h:]
    seconds = second[:h, :], second[h:, h:]
    peaks = [jnp.max(jnp.abs(p + q), keepdims=True) for p, q in zip(firsts, seconds)]
    scale = LEARN_RATE / (jnp.maximum(*peaks) + EPS_NORM)
    top, end = [
        jnp.where(
            lax.broadcasted_iota(jnp.int32, p.shape, 0) <= lax.broadcasted_iota(jnp.int32, p.shape, 1),
            p - q,
            0.0,
        ).astype(HALF)
        for p, q in zip(firsts, seconds)
    ]

    def moved(old, moved_rows):
        return (old.astype(FLOAT) - scale * moved_rows).astype(HALF)

    out[:h, :h] = moved(factor[:h, :h], product(top[:, :h], factor[:h, :h]))
    out[:h, h:] = moved(factor[:h, h:], product(top, factor[:, h:]))
    out[h:, :h] = jnp.zeros((h, h), HALF)
    out[h:, h:] = moved(factor[h:, h:], product(end, factor[h:, h:]))


def square_of(out, factor):
    h = out.shape[0] // 2
    out[:h, :] = product(factor[:h, :h], factor[:h, :], 0, 0).astype(HALF)
    out[h:, :h] = product(factor[:h, h:], factor[:h, :h], 0, 0).astype(HALF)
    out[h:, h:] = product(factor[:, h:], factor[:, h:], 0, 0).astype(HALF)


def finish_kernel(plan, limit, where, *refs):
    squares, own_clip, left, right, grad, left_p, right_p, left_q, right_q = refs[:9]
    outs, (new_left, new_right, left_square, right_square, result) = refs[9:-5], refs[-5:]
    clip = clip_of(limit, squares)
    ratio = clip / own_clip[0:1, 0:1]
    ratio = ratio * ratio
    size, rows = plan.size, plan.rows
    move_factor(new_left, left, ratio, left_p, left_q)
    move_factor(new_right, right, ratio, right_p, right_q)
    square_of(left_square, new_left)
    square_of(right_square, new_right)

    def at(z):
        return pl.ds(pl.multiple_of((z * plan.group + where[1]) * rows, rows), rows)

    precond_left = jnp.concatenate([left_square[at(z), :] for z in range(plan.blocks)], axis=0)
    middle = (clip * product(precond_left, grad[...])).astype(HALF)
    done = product(middle, right_square[...]).astype(HALF)
    result[...] = done.reshape(plan.blocks, rows, size)
    for k, out in enumerate(outs):
        z = where[0] ^ k
        out[:, :size] = new_left[at(z), :]
        out[:, size : 2 * size] = new_right[at(z), :]
        out[:, 2 * size :] = result[z]


def place_kernel(plan, where, slots, old_state, *refs):
    pieces, (precond, new_state) = refs[: plan.blocks], refs[plan.blocks :]
    size = plan.size
    new_state[...] = old_state[...]
    for k, piece in enumerate(pieces):
        precond[where[0] ^ k] = piece[:, 2 * size :]
        new_state[slots[where[0] ^ k]] = piece[:, : 2 * size]


def shaped(shape, dtype=HALF):
    return jax.ShapeDtypeStruct(shape, dtype)


def body(partial_grads, factors, inverse_factors, probes, slot_table):
    devices = lax.axis_size("dp")
    halves = lax.axis_size("mp")
    me = lax.axis_index("dp")
    experts, block_rows, size, columns = partial_grads.shape[1:]
    blocks = experts * block_rows
    plan = Plan(devices, blocks, size)
    group, rows = plan.group, plan.rows
    my_block = me // group
    my_place = me % group
    my_low, my_high = my_place % 2, my_place // 2
    where = jnp.stack([my_block, my_place, my_low, my_high]).astype(jnp.int32)
    slot_row = slot_table[0]
    in_tiles = rows % 16 == 0 and size % (2 * LANES) == 0
    limit = CLIP_RMS * math.sqrt(blocks * size * columns * halves)

    grads = partial_grads[0].reshape(blocks, blocks, group, rows, columns)
    middle = blocks // 2
    if in_tiles and group == 4:

        def part(array, half, high, low):
            start = (0, (half or 0) * middle, high, low, 0, 0)
            extent = (
                blocks,
                blocks if half is None else middle,
                2 if high is None else 1,
                2 if low is None else 1,
                rows,
                columns,
            )
            array = array.reshape(blocks, blocks, 2, 2, rows, columns)
            cut = lax.dynamic_slice(array, [0 if i is None else i for i in start], extent)
            return cut.reshape([n for i, n in enumerate(extent) if n > 1 or i not in (2, 3)])

        low_seen = flip(part(grads, 0, None, 1 - my_low), devices, 1)
        high_seen = flip(part(grads, 1, 1 - my_high, None), devices, 2)
        kept, low_sent, high_sent = call(
            relay_kernel,
            (shaped((blocks, blocks, rows, columns), FLOAT),)
            + (shaped((blocks, middle, rows, columns)),) * 2,
            [],
            0,
            1,
            where,
            part(grads, None, my_high, my_low),
            part(grads, 0, 1 - my_high, my_low),
            low_seen,
            part(grads, 1, my_high, 1 - my_low),
            high_seen,
        )
        parts = call(
            gather_kernel,
            tuple(shaped((blocks, rows, columns)) for _ in range(blocks)),
            [],
            0,
            1,
            where,
            kept,
            flip(low_sent, devices, 2),
            flip(high_sent, devices, 1),
        )
    else:
        halves_of = []
        masks = [1 << i for i in range(group.bit_length() - 1)]
        for half, order in enumerate((masks, masks[::-1])):
            kept = grads[:, half * middle : (half + 1) * middle].astype(FLOAT)
            kept = kept.reshape(blocks, middle, *[2] * len(masks), rows, columns)
            left = sorted(masks, reverse=True)
            for mask in order:
                axis, bit = 2 + left.index(mask), my_place // mask % 2
                sent = pick(kept, 1 - bit, axis).astype(HALF)
                left.remove(mask)
                kept = pick(kept, bit, axis) + flip(sent, devices, mask)
            halves_of.append(kept)
        total = jnp.concatenate(halves_of, axis=1).astype(HALF)
        parts = [pick(total, my_block ^ k, 0) for k in range(blocks)]

    old_state = factors[0]
    if in_tiles:
        pieces = call(
            functools.partial(choose_kernel, plan),
            tuple(shaped((rows, 5 * size)) for _ in range(blocks)),
            [pltpu.SemaphoreType.DMA((3 * blocks,))],
            0,
            2,
            where,
            slot_row,
            old_state,
            inverse_factors[0],
            probes[0],
            space=pltpu.HBM,
        )
    else:
        wide = jnp.concatenate([old_state, inverse_factors[0], probes[0]], axis=2)
        pieces = [pick(wide, slot_row[my_block ^ k], 0) for k in range(blocks)]
    pieces = [pieces[0]] + [flip(pieces[k], devices, k * group) for k in range(1, blocks)]
    if in_tiles:
        quarter = call(
            functools.partial(pack_kernel, plan),
            shaped((rows, plan.packed())),
            [pltpu.VMEM((blocks, rows, 5 * size), HALF)],
            0,
            1,
            where,
            *pieces,
        )
    else:
        quarter = unflip(pieces, my_block)

    terms = [parts[0]] + [flip(parts[k], devices, k * group) for k in range(1, blocks)]
    grad_quarter, squares = call(
        functools.partial(sum_kernel, blocks),
        (shaped((blocks, rows, columns)), shaped((8, LANES), FLOAT)),
        [],
        0,
        0,
        *terms,
    )

    if in_tiles and group == 4:
        states = [quarter] + [flip(quarter, devices, k) for k in (1, 2)]
        cut = states[1][:, : plan.split()], states[2][:, plan.split() :]
        states += [flip(cut[i], devices, 2 - i) for i in range(2)]
    else:
        states = [quarter] + [flip(quarter, devices, k) for k in range(1, group)]
    quarters = [grad_quarter] + [flip(grad_quarter, devices, k) for k in range(1, group)]

    squares = functools.reduce(
        jnp.add,
        [squares] + [flip(squares, devices, k * group) for k in range(1, blocks)],
    )
    bit = 1
    while bit < halves:
        other = lax.ppermute(squares, "mp", [(i, i ^ bit) for i in range(halves)])
        squares = squares + other
        bit *= 2
    bit = 1
    while bit < group:
        squares = squares + flip(squares, devices, bit)
        bit *= 2

    gram = shaped((size, size), FLOAT)
    square = shaped((size, size))
    matmul = 2 * size**3
    if in_tiles:
        left_q, right_q, left_c, right_c = call(
            functools.partial(probe_kernel, plan),
            (square, square, gram, gram),
            [pltpu.VMEM((size, size), HALF)] * 3,
            4 * matmul,
            1,
            where,
            *states,
        )
        gradient, left_w, right_w, own_clip = call(
            functools.partial(whiten_kernel, plan, limit),
            (shaped((size, columns)), gram, gram, shaped((8, LANES), FLOAT)),
            [],
            4 * matmul,
            1,
            where,
            left_q,
            right_q,
            *quarters,
        )
        back = call(
            functools.partial(finish_kernel, plan, limit),
            tuple(shaped((rows, 2 * size + columns)) for _ in range(blocks)),
            [pltpu.VMEM((size, size), HALF)] * 4 + [pltpu.VMEM((blocks, rows, columns), HALF)],
            5 * matmul,
            1,
            where,
            squares,
            own_clip,
            left_q,
            right_q,
            gradient,
            left_w,
            right_w,
            left_c,
            right_c,
        )
    else:
        back = plain_block(plan, limit, my_block, my_place, squares, states, quarters)
    back = [back[0]] + [flip(back[k], devices, k * group) for k in range(1, blocks)]
    precond, new_state = call(
        functools.partial(place_kernel, plan),
        (shaped((blocks, rows, columns)), shaped(old_state.shape)),
        [],
        0,
        2,
        where,
        slot_row,
        old_state,
        *back,
    )
    return (precond.reshape(experts, block_rows, rows, columns), new_state[None])


def plain_block(plan, limit, my_block, my_place, squares, states, quarters):
    size, blocks, group, rows = plan.size, plan.blocks, plan.group, plan.rows
    state = unflip(states, my_place).transpose(1, 0, 2, 3).reshape(size, 5 * size)
    gradient = unflip(quarters, my_place).transpose(1, 0, 2, 3).reshape(size, -1)
    clip = clip_of(limit, squares)
    left_q, right_q, left_inv, right_inv, probe_mat = jnp.split(state, 5, axis=1)
    half_conjugate = product(left_inv, probe_mat, 0, 0).astype(HALF)
    conjugate = product(half_conjugate, right_inv).astype(HALF)
    left_times = (clip * product(left_q, gradient)).astype(HALF)
    whitened = product(left_times, right_q, 1, 1).astype(HALF)
    new_left = step_factor(
        left_q, 1.0, product(whitened, whitened, 1, 1), product(conjugate, conjugate, 1, 1)
    )
    new_right = step_factor(
        right_q, 1.0, product(whitened, whitened, 0, 0), product(conjugate, conjugate, 0, 0)
    )
    precond_left = product(new_left, new_left, 0, 0).astype(HALF)
    precond_right = product(new_right, new_right, 0, 0).astype(HALF)

    def my_rows(array):
        return pick(array.reshape(blocks, group, rows, -1), my_place, 1)

    middle = (clip * product(my_rows(precond_left).reshape(blocks * rows, size), gradient)).astype(HALF)
    result = product(middle, precond_right).astype(HALF).reshape(blocks, rows, -1)
    back = jnp.concatenate([my_rows(new_left), my_rows(new_right), result], axis=2)
    return [pick(back, my_block ^ k, 0) for k in range(blocks)]


def solution(mesh):
    return jax.shard_map(
        body,
        mesh=mesh,
        in_specs=(
            P("dp", None, None, None, "mp"),
            P("mp", None, "dp", None),
            P("mp", None, "dp", None),
            P("mp", None, "dp", None),
            P("mp", None),
        ),
        out_specs=(P(None, None, "dp", "mp"), P("mp", None, "dp", None)),
        check_vma=False,
    )
```

```python
import functools
import math

import jax
import jax.numpy as jnp
from jax import lax
from jax.experimental import pallas as pl
from jax.experimental.pallas import tpu as pltpu
from jax.sharding import PartitionSpec as P

CLIP_RMS = 0.3
LEARN_RATE = 0.1
EPS_NORM = 1e-06
LANES = 128
VMEM_GRANT = 16 * 2**20
FLOAT = jnp.float32
HALF = jnp.bfloat16


VMEM_SPEC = pl.BlockSpec(memory_space=pltpu.VMEM)
SMEM_SPEC = pl.BlockSpec(memory_space=pltpu.SMEM)


def product(left_op, right_op, left_dim=1, right_dim=0):
    return lax.dot_general(
        left_op, right_op, (((left_dim,), (right_dim,)), ((), ())), preferred_element_type=FLOAT
    )


def flip(array, devices, mask):
    return lax.ppermute(array, "dp", [(i, i ^ mask) for i in range(devices)])


def pick(array, index, axis):
    return lax.dynamic_index_in_dim(array, index, axis, keepdims=False)


def unflip(pieces, own):
    stacked = jnp.stack(pieces)
    return jnp.stack([pick(stacked, own ^ k, 0) for k in range(len(pieces))])


def call(kernel, out_shape, scratch, flops, smem, *operands, space=pltpu.VMEM, grant=VMEM_GRANT):
    moved = sum(x.size * x.dtype.itemsize for x in (*operands, *jax.tree.leaves(out_shape)))
    return pl.pallas_call(
        kernel,
        out_shape=out_shape,
        in_specs=[SMEM_SPEC] * smem + [pl.BlockSpec(memory_space=space)] * (len(operands) - smem),
        out_specs=jax.tree.map(lambda _: VMEM_SPEC, out_shape),
        scratch_shapes=scratch,
        cost_estimate=pl.CostEstimate(flops=flops, bytes_accessed=moved, transcendentals=0),
        compiler_params=pltpu.CompilerParams(vmem_limit_bytes=grant),
    )(*operands)


class Plan:
    def __init__(self, devices, blocks, size):
        self.devices, self.blocks, self.size = devices, blocks, size
        self.group = devices // blocks
        self.rows = size // devices
        self.first = [z * (size // blocks) // LANES * LANES for z in range(blocks)]

    def spots(self):
        offset = 0
        for z in range(self.blocks):
            for what in range(5):
                first = self.first[z] if what < 4 else 0
                yield z, what, first, offset
                offset += self.size - first

    def split(self):
        half = self.packed() // 2
        return min((offset for _, _, _, offset in self.spots()), key=lambda x: abs(x - half))

    def packed(self):
        return sum(self.size - first for _, _, first, _ in self.spots())


def choose_kernel(plan, where, slots, factors, inverses, probes, *refs):
    outs, done = refs[:-1], refs[-1]
    size, copies = plan.size, []
    for k, out in enumerate(outs):
        slot = slots[where[0] ^ k]
        parts = (
            (factors, out.at[:, : 2 * size]),
            (inverses, out.at[:, 2 * size : 4 * size]),
            (probes, out.at[:, 4 * size :]),
        )
        for i, (source, target) in enumerate(parts):
            copies.append(pltpu.make_async_copy(source.at[slot], target, done.at[3 * k + i]))
    for copy in copies:
        copy.start()
    for copy in copies:
        copy.wait()


def pack_kernel(plan, where, *refs):
    pieces, out, stack = refs[: plan.blocks], refs[-2], refs[-1]
    size = plan.size
    for k, piece in enumerate(pieces):
        stack[where[0] ^ k] = piece[...]
    for z, what, first, offset in plan.spots():
        out[:, offset : offset + size - first] = stack[z, :, what * size + first : (what + 1) * size]


def spread(plan, where, pieces, targets):
    size, rows = plan.size, plan.rows
    for z in range(1, plan.blocks):
        for target in targets[:4]:
            if plan.first[z]:
                span = size // plan.blocks
                target[z * span : (z + 1) * span, : plan.first[z]] = jnp.zeros((span, plan.first[z]), HALF)
    for k in range(plan.group):
        for z, what, first, offset in plan.spots():
            piece, start = pieces[k], offset
            if len(pieces) > plan.group and k == plan.group - 1 and offset >= plan.split():
                piece, start = pieces[k + 1], offset - plan.split()
            row = pl.multiple_of((z * plan.group + (where[1] ^ k)) * rows, rows)
            targets[what][pl.ds(row, rows), first:] = piece[:, start : start + size - first]


def probe_kernel(plan, where, *refs):
    pieces = refs[:-7]
    left, right, left_gram, right_gram, left_inv, right_inv, probe = refs[-7:]
    spread(plan, where, pieces, (left, right, left_inv, right_inv, probe))
    h = plan.size // 2
    half_conjugate = jnp.concatenate(
        [product(left_inv[:h, :h], probe[:h, :], 0, 0), product(left_inv[:, h:], probe[...], 0, 0)],
        axis=0,
    ).astype(HALF)
    conjugate = jnp.concatenate(
        [product(half_conjugate[:, :h], right_inv[:h, :h]), product(half_conjugate, right_inv[:, h:])],
        axis=1,
    ).astype(HALF)
    gram_rows(left_gram, conjugate)
    gram_columns(right_gram, conjugate)


def cut_kernel(where, grads, low_out, high_out, done):
    blocks, middle = low_out.shape[:2]
    copies = []
    for block in range(blocks):
        for z in range(middle):
            for high in range(2):
                source = grads.at[block, z, high, 1 - where[2]]
                copies.append((source, low_out.at[block, z, high]))
            source = grads.at[block, middle + z, 1 - where[3]]
            copies.append((source, high_out.at[block, z]))
    copies = [pltpu.make_async_copy(*pair, done.at[i]) for i, pair in enumerate(copies)]
    for copy in copies:
        copy.start()
    for copy in copies:
        copy.wait()


def relay_kernel(where, own, low_own, low_seen, high_own, high_seen, kept, low_out, high_out):
    middle = own.shape[1] // 2

    def add(mine, seen):
        return mine.astype(FLOAT) + seen.astype(FLOAT)

    kept[:, :middle] = add(own[:, :middle], low_seen[:, :, where[3]])
    kept[:, middle:] = add(own[:, middle:], high_seen[:, :, where[2]])
    low_out[...] = add(low_own[...], low_seen[:, :, 1 - where[3]]).astype(HALF)
    high_out[...] = add(high_own[...], high_seen[:, :, 1 - where[2]]).astype(HALF)


def gather_kernel(where, kept, low_last, high_last, *outs):
    middle = kept.shape[1] // 2
    for k, out in enumerate(outs):
        block = where[0] ^ k
        out[:middle] = (kept[block, :middle] + low_last[block].astype(FLOAT)).astype(HALF)
        out[middle:] = (kept[block, middle:] + high_last[block].astype(FLOAT)).astype(HALF)


def sum_kernel(blocks, *refs):
    terms, (out, squares) = refs[:-2], refs[-2:]
    found, start = 0.0, 0
    for i in range(0, len(terms), blocks):
        total = terms[i][...].astype(FLOAT)
        for term in terms[i + 1 : i + blocks]:
            total = total + term[...].astype(FLOAT)
        out[start : start + total.shape[0]] = total.astype(HALF)
        start += total.shape[0]
        found = found + jnp.sum(jnp.sum(total * total, axis=(0, 1)))
    squares[...] = jnp.full(squares.shape, found)


def bound_of(limit, squares):
    return jnp.minimum(1.0, limit / jnp.sqrt(squares + EPS_NORM))


def whiten_kernel(plan, limit, where, *refs):
    left, right, pieces = refs[0], refs[1], refs[2 : 2 + plan.group]
    grad, left_gram, right_gram, own_clip = refs[2 + plan.group :]
    for k, piece in enumerate(pieces):
        for z in range(plan.blocks):
            row = pl.multiple_of((z * plan.group + (where[1] ^ k)) * plan.rows, plan.rows)
            grad[pl.ds(row, plan.rows), :] = piece[z]
    wide = grad[...].astype(FLOAT)
    clip = bound_of(limit, jnp.sum(wide * wide, keepdims=True))
    own_clip[...] = jnp.broadcast_to(clip, own_clip.shape)
    h = plan.size // 2
    left_times = jnp.concatenate(
        [product(left[:h, :], grad[...]), product(left[h:, h:], grad[h:, :])], axis=0
    )
    left_times = (clip * left_times).astype(HALF)
    whitened = jnp.concatenate(
        [product(left_times, right[:h, :], 1, 1), product(left_times[:, h:], right[h:, h:], 1, 1)],
        axis=1,
    ).astype(HALF)
    gram_rows(left_gram, whitened)
    gram_columns(right_gram, whitened)


def step_factor(factor, ratio, first_ref, second_ref):
    first, second = ratio * first_ref[...], second_ref[...]
    bound_value = jnp.max(jnp.abs(first + second), keepdims=True) + EPS_NORM
    row = lax.broadcasted_iota(jnp.int32, first.shape, 0)
    column = lax.broadcasted_iota(jnp.int32, first.shape, 1)
    change = jnp.where(row <= column, first - second, 0.0).astype(HALF)
    moved_rows = product(change, factor)
    return (factor.astype(FLOAT) - LEARN_RATE / bound_value * moved_rows).astype(HALF)


def clip_of(limit, squares):
    return bound_of(limit, squares[0:1, 0:1])


def gram_rows(out, matrix):
    h = out.shape[0] // 2
    out[:h, :] = product(matrix[:h, :], matrix, 1, 1)
    out[h:, h:] = product(matrix[h:, :], matrix[h:, :], 1, 1)


def gram_columns(out, matrix):
    h = out.shape[0] // 2
    out[:h, :] = product(matrix[:, :h], matrix, 0, 0)
    out[h:, h:] = product(matrix[:, h:], matrix[:, h:], 0, 0)


def move_factor(out, factor, ratio, first, second):
    h = out.shape[0] // 2
    firsts = ratio * first[:h, :], ratio * first[h:, h:]
    seconds = second[:h, :], second[h:, h:]
    peaks = [jnp.max(jnp.abs(p + q), keepdims=True) for p, q in zip(firsts, seconds)]
    scale = LEARN_RATE / (jnp.maximum(*peaks) + EPS_NORM)
    top, end = [
        jnp.where(
            lax.broadcasted_iota(jnp.int32, p.shape, 0) <= lax.broadcasted_iota(jnp.int32, p.shape, 1),
            p - q,
            0.0,
        ).astype(HALF)
        for p, q in zip(firsts, seconds)
    ]

    def moved(old, moved_rows):
        return (old.astype(FLOAT) - scale * moved_rows).astype(HALF)

    out[:h, :h] = moved(factor[:h, :h], product(top[:, :h], factor[:h, :h]))
    out[:h, h:] = moved(factor[:h, h:], product(top, factor[:, h:]))
    out[h:, :h] = jnp.zeros((h, h), HALF)
    out[h:, h:] = moved(factor[h:, h:], product(end, factor[h:, h:]))


def square_of(out, factor):
    h = out.shape[0] // 2
    out[:h, :] = product(factor[:h, :h], factor[:h, :], 0, 0).astype(HALF)
    out[h:, :h] = product(factor[:h, h:], factor[:h, :h], 0, 0).astype(HALF)
    out[h:, h:] = product(factor[:, h:], factor[:, h:], 0, 0).astype(HALF)


def finish_kernel(plan, limit, where, *refs):
    squares, own_clip, left, right, grad, left_p, right_p, left_q, right_q = refs[:9]
    outs, (new_left, new_right, left_square, right_square, result) = refs[9:-5], refs[-5:]
    clip = clip_of(limit, squares)
    ratio = clip / own_clip[0:1, 0:1]
    ratio = ratio * ratio
    size, rows = plan.size, plan.rows
    move_factor(new_left, left, ratio, left_p, left_q)
    move_factor(new_right, right, ratio, right_p, right_q)
    square_of(left_square, new_left)
    square_of(right_square, new_right)

    def at(z):
        return pl.ds(pl.multiple_of((z * plan.group + where[1]) * rows, rows), rows)

    precond_left = jnp.concatenate([left_square[at(z), :] for z in range(plan.blocks)], axis=0)
    middle = (clip * product(precond_left, grad[...])).astype(HALF)
    done = product(middle, right_square[...]).astype(HALF)
    result[...] = done.reshape(plan.blocks, rows, size)
    for k, out in enumerate(outs):
        z = where[0] ^ k
        out[:, :size] = new_left[at(z), :]
        out[:, size : 2 * size] = new_right[at(z), :]
        out[:, 2 * size :] = result[z]


def place_kernel(plan, where, slots, old_state, *refs):
    pieces, (precond, new_state) = refs[: plan.blocks], refs[plan.blocks :]
    size = plan.size
    if new_state.shape[0] > plan.blocks:
        new_state[...] = old_state[...]
    for k, piece in enumerate(pieces):
        precond[where[0] ^ k] = piece[:, 2 * size :]
        new_state[slots[where[0] ^ k]] = piece[:, : 2 * size]


def shaped(shape, dtype=HALF):
    return jax.ShapeDtypeStruct(shape, dtype)


def body(partial_grads, factors, inverse_factors, probes, slot_table):
    devices = lax.axis_size("dp")
    halves = lax.axis_size("mp")
    me = lax.axis_index("dp")
    experts, block_rows, size, columns = partial_grads.shape[1:]
    blocks = experts * block_rows
    plan = Plan(devices, blocks, size)
    group, rows = plan.group, plan.rows
    my_block = me // group
    my_place = me % group
    my_low, my_high = my_place % 2, my_place // 2
    where = jnp.stack([my_block, my_place, my_low, my_high]).astype(jnp.int32)
    slot_row = slot_table[0]
    in_tiles = rows % 16 == 0 and size % (2 * LANES) == 0
    limit = CLIP_RMS * math.sqrt(blocks * size * columns * halves)

    grads = partial_grads[0].reshape(blocks, blocks, group, rows, columns)
    middle = blocks // 2
    if in_tiles and group == 4:

        def part(array, half, high, low):
            start = (0, (half or 0) * middle, high, low, 0, 0)
            extent = (
                blocks,
                blocks if half is None else middle,
                2 if high is None else 1,
                2 if low is None else 1,
                rows,
                columns,
            )
            array = array.reshape(blocks, blocks, 2, 2, rows, columns)
            cut = lax.dynamic_slice(array, [0 if i is None else i for i in start], extent)
            return cut.reshape([n for i, n in enumerate(extent) if n > 1 or i not in (2, 3)])

        first = call(
            cut_kernel,
            (shaped((blocks, middle, 2, rows, columns)),) * 2,
            [pltpu.SemaphoreType.DMA((3 * blocks * middle,))],
            0,
            1,
            where,
            grads.reshape(blocks, blocks, 2, 2, rows, columns),
            space=pltpu.HBM,
            grant=None,
        )
        low_seen = flip(first[0], devices, 1)
        high_seen = flip(first[1], devices, 2)
        kept, low_sent, high_sent = call(
            relay_kernel,
            (shaped((blocks, blocks, rows, columns), FLOAT),)
            + (shaped((blocks, middle, rows, columns)),) * 2,
            [],
            0,
            1,
            where,
            part(grads, None, my_high, my_low),
            part(grads, 0, 1 - my_high, my_low),
            low_seen,
            part(grads, 1, my_high, 1 - my_low),
            high_seen,
        )
        parts = call(
            gather_kernel,
            tuple(shaped((blocks, rows, columns)) for _ in range(blocks)),
            [],
            0,
            1,
            where,
            kept,
            flip(low_sent, devices, 2),
            flip(high_sent, devices, 1),
        )
    else:
        halves_of = []
        masks = [1 << i for i in range(group.bit_length() - 1)]
        for half, order in enumerate((masks, masks[::-1])):
            kept = grads[:, half * middle : (half + 1) * middle].astype(FLOAT)
            kept = kept.reshape(blocks, middle, *[2] * len(masks), rows, columns)
            left = sorted(masks, reverse=True)
            for mask in order:
                axis, bit = 2 + left.index(mask), my_place // mask % 2
                sent = pick(kept, 1 - bit, axis).astype(HALF)
                left.remove(mask)
                kept = pick(kept, bit, axis) + flip(sent, devices, mask)
            halves_of.append(kept)
        total = jnp.concatenate(halves_of, axis=1).astype(HALF)
        parts = [pick(total, my_block ^ k, 0) for k in range(blocks)]

    old_state = factors[0]
    if in_tiles:
        pieces = call(
            functools.partial(choose_kernel, plan),
            tuple(shaped((rows, 5 * size)) for _ in range(blocks)),
            [pltpu.SemaphoreType.DMA((3 * blocks,))],
            0,
            2,
            where,
            slot_row,
            old_state,
            inverse_factors[0],
            probes[0],
            space=pltpu.HBM,
            grant=None,
        )
    else:
        wide = jnp.concatenate([old_state, inverse_factors[0], probes[0]], axis=2)
        pieces = [pick(wide, slot_row[my_block ^ k], 0) for k in range(blocks)]
    pieces = [pieces[0]] + [flip(pieces[k], devices, k * group) for k in range(1, blocks)]
    if in_tiles:
        quarter = call(
            functools.partial(pack_kernel, plan),
            shaped((rows, plan.packed())),
            [pltpu.VMEM((blocks, rows, 5 * size), HALF)],
            0,
            1,
            where,
            *pieces,
        )
    else:
        quarter = unflip(pieces, my_block)

    terms = [parts[0]] + [flip(parts[k], devices, k * group) for k in range(1, blocks)]
    grad_quarter, squares = call(
        functools.partial(sum_kernel, blocks),
        (shaped((blocks, rows, columns)), shaped((8, LANES), FLOAT)),
        [],
        0,
        0,
        *terms,
    )

    if in_tiles and group == 4:
        states = [quarter] + [flip(quarter, devices, k) for k in (1, 2)]
        cut = states[1][:, : plan.split()], states[2][:, plan.split() :]
        states += [flip(cut[i], devices, 2 - i) for i in range(2)]
    else:
        states = [quarter] + [flip(quarter, devices, k) for k in range(1, group)]
    quarters = [grad_quarter] + [flip(grad_quarter, devices, k) for k in range(1, group)]

    squares = functools.reduce(
        jnp.add,
        [squares] + [flip(squares, devices, k * group) for k in range(1, blocks)],
    )
    bit = 1
    while bit < halves:
        other = lax.ppermute(squares, "mp", [(i, i ^ bit) for i in range(halves)])
        squares = squares + other
        bit *= 2
    bit = 1
    while bit < group:
        squares = squares + flip(squares, devices, bit)
        bit *= 2

    gram = shaped((size, size), FLOAT)
    square = shaped((size, size))
    matmul = 2 * size**3
    if in_tiles:
        left_q, right_q, left_c, right_c = call(
            functools.partial(probe_kernel, plan),
            (square, square, gram, gram),
            [pltpu.VMEM((size, size), HALF)] * 3,
            4 * matmul,
            1,
            where,
            *states,
        )
        gradient, left_w, right_w, own_clip = call(
            functools.partial(whiten_kernel, plan, limit),
            (shaped((size, columns)), gram, gram, shaped((8, LANES), FLOAT)),
            [],
            4 * matmul,
            1,
            where,
            left_q,
            right_q,
            *quarters,
        )
        back = call(
            functools.partial(finish_kernel, plan, limit),
            tuple(shaped((rows, 2 * size + columns)) for _ in range(blocks)),
            [pltpu.VMEM((size, size), HALF)] * 4 + [pltpu.VMEM((blocks, rows, columns), HALF)],
            5 * matmul,
            1,
            where,
            squares,
            own_clip,
            left_q,
            right_q,
            gradient,
            left_w,
            right_w,
            left_c,
            right_c,
        )
    else:
        back = plain_block(plan, limit, my_block, my_place, squares, states, quarters)
    back = [back[0]] + [flip(back[k], devices, k * group) for k in range(1, blocks)]
    precond, new_state = call(
        functools.partial(place_kernel, plan),
        (shaped((blocks, rows, columns)), shaped(old_state.shape)),
        [],
        0,
        2,
        where,
        slot_row,
        old_state,
        *back,
    )
    return (precond.reshape(experts, block_rows, rows, columns), new_state[None])


def plain_block(plan, limit, my_block, my_place, squares, states, quarters):
    size, blocks, group, rows = plan.size, plan.blocks, plan.group, plan.rows
    state = unflip(states, my_place).transpose(1, 0, 2, 3).reshape(size, 5 * size)
    gradient = unflip(quarters, my_place).transpose(1, 0, 2, 3).reshape(size, -1)
    clip = clip_of(limit, squares)
    left_q, right_q, left_inv, right_inv, probe_mat = jnp.split(state, 5, axis=1)
    half_conjugate = product(left_inv, probe_mat, 0, 0).astype(HALF)
    conjugate = product(half_conjugate, right_inv).astype(HALF)
    left_times = (clip * product(left_q, gradient)).astype(HALF)
    whitened = product(left_times, right_q, 1, 1).astype(HALF)
    new_left = step_factor(
        left_q, 1.0, product(whitened, whitened, 1, 1), product(conjugate, conjugate, 1, 1)
    )
    new_right = step_factor(
        right_q, 1.0, product(whitened, whitened, 0, 0), product(conjugate, conjugate, 0, 0)
    )
    precond_left = product(new_left, new_left, 0, 0).astype(HALF)
    precond_right = product(new_right, new_right, 0, 0).astype(HALF)

    def my_rows(array):
        return pick(array.reshape(blocks, group, rows, -1), my_place, 1)

    middle = (clip * product(my_rows(precond_left).reshape(blocks * rows, size), gradient)).astype(HALF)
    result = product(middle, precond_right).astype(HALF).reshape(blocks, rows, -1)
    back = jnp.concatenate([my_rows(new_left), my_rows(new_right), result], axis=2)
    return [pick(back, my_block ^ k, 0) for k in range(blocks)]


def solution(mesh):
    return jax.shard_map(
        body,
        mesh=mesh,
        in_specs=(
            P("dp", None, None, None, "mp"),
            P("mp", None, "dp", None),
            P("mp", None, "dp", None),
            P("mp", None, "dp", None),
            P("mp", None),
        ),
        out_specs=(P(None, None, "dp", "mp"), P("mp", None, "dp", None)),
        check_vma=False,
    )
```

```python
import functools
import math

import jax
import jax.numpy as jnp
from jax import lax
from jax.experimental import pallas as pl
from jax.experimental.pallas import tpu as pltpu
from jax.sharding import PartitionSpec as P

CLIP_RMS = 0.3
LEARN_RATE = 0.1
EPS_NORM = 1e-06
LANES = 128
VMEM_GRANT = 16 * 2**20
FLOAT = jnp.float32
HALF = jnp.bfloat16


VMEM_SPEC = pl.BlockSpec(memory_space=pltpu.VMEM)
SMEM_SPEC = pl.BlockSpec(memory_space=pltpu.SMEM)


def product(left_op, right_op, left_dim=1, right_dim=0):
    return lax.dot_general(
        left_op, right_op, (((left_dim,), (right_dim,)), ((), ())), preferred_element_type=FLOAT
    )


def flip(array, devices, mask):
    pairs = [(i, i ^ mask) for i in range(devices)]
    return lax.ppermute(array, "dp", pairs)


def pick(array, index, axis):
    return lax.dynamic_index_in_dim(array, index, axis, keepdims=False)


def unflip(pieces, own):
    stacked = jnp.stack(pieces)
    return jnp.stack([pick(stacked, own ^ k, 0) for k in range(len(pieces))])


def call(kernel, out_shape, scratch, flops, smem, *operands, space=pltpu.VMEM):
    moved = sum(x.size * x.dtype.itemsize for x in (*operands, *jax.tree.leaves(out_shape)))
    return pl.pallas_call(
        kernel,
        out_shape=out_shape,
        in_specs=[SMEM_SPEC] * smem + [pl.BlockSpec(memory_space=space)] * (len(operands) - smem),
        out_specs=jax.tree.map(lambda _: VMEM_SPEC, out_shape),
        scratch_shapes=scratch,
        cost_estimate=pl.CostEstimate(flops=flops, bytes_accessed=moved, transcendentals=0),
        compiler_params=pltpu.CompilerParams(vmem_limit_bytes=VMEM_GRANT),
    )(*operands)


class Plan:
    def __init__(self, devices, blocks, size):
        self.devices, self.blocks, self.size = devices, blocks, size
        self.group = devices // blocks
        self.rows = size // devices
        self.first = [z * (size // blocks) // LANES * LANES for z in range(blocks)]

    def spots(self):
        offset = 0
        for z in range(self.blocks):
            for what in range(5):
                first = self.first[z] if what < 4 else 0
                yield z, what, first, offset
                offset += self.size - first

    def split(self):
        half = self.packed() // 2
        return min((offset for _, _, _, offset in self.spots()), key=lambda x: abs(x - half))

    def packed(self):
        return sum(self.size - first for _, _, first, _ in self.spots())


def choose_kernel(plan, where, slots, factors, inverses, probes, *refs):
    outs, done = refs[:-1], refs[-1]
    size, copies = plan.size, []
    for k, out in enumerate(outs):
        slot = slots[where[0] ^ k]
        parts = (
            (factors, out.at[:, : 2 * size]),
            (inverses, out.at[:, 2 * size : 4 * size]),
            (probes, out.at[:, 4 * size :]),
        )
        for i, (source, target) in enumerate(parts):
            copies.append(pltpu.make_async_copy(source.at[slot], target, done.at[3 * k + i]))
    for copy in copies:
        copy.start()
    for copy in copies:
        copy.wait()


def pack_kernel(plan, where, *refs):
    pieces, out, stack = refs[: plan.blocks], refs[-2], refs[-1]
    size = plan.size
    for k, piece in enumerate(pieces):
        stack[where[0] ^ k] = piece[...]
    for z, what, first, offset in plan.spots():
        out[:, offset : offset + size - first] = stack[z, :, what * size + first : (what + 1) * size]


def spread(plan, where, pieces, targets):
    size, rows = plan.size, plan.rows
    for z in range(1, plan.blocks):
        for target in targets[:4]:
            if plan.first[z]:
                span = size // plan.blocks
                target[z * span : (z + 1) * span, : plan.first[z]] = jnp.zeros((span, plan.first[z]), HALF)
    for k in range(plan.group):
        for z, what, first, offset in plan.spots():
            piece, start = pieces[k], offset
            if len(pieces) > plan.group and k == plan.group - 1 and offset >= plan.split():
                piece, start = pieces[k + 1], offset - plan.split()
            row = pl.multiple_of((z * plan.group + (where[1] ^ k)) * rows, rows)
            targets[what][pl.ds(row, rows), first:] = piece[:, start : start + size - first]


def probe_kernel(plan, where, *refs):
    pieces = refs[:-7]
    left, right, left_gram, right_gram, left_inv, right_inv, probe = refs[-7:]
    spread(plan, where, pieces, (left, right, left_inv, right_inv, probe))
    h = plan.size // 2
    half_conjugate = jnp.concatenate(
        [product(left_inv[:h, :h], probe[:h, :], 0, 0), product(left_inv[:, h:], probe[...], 0, 0)],
        axis=0,
    ).astype(HALF)
    conjugate = jnp.concatenate(
        [product(half_conjugate[:, :h], right_inv[:h, :h]), product(half_conjugate, right_inv[:, h:])],
        axis=1,
    ).astype(HALF)
    gram_rows(left_gram, conjugate)
    gram_columns(right_gram, conjugate)


def relay_kernel(where, own, low_own, low_seen, high_own, high_seen, kept, low_out, high_out):
    middle = own.shape[1] // 2

    def add(mine, seen):
        return mine.astype(FLOAT) + seen.astype(FLOAT)

    kept[:, :middle] = add(own[:, :middle], low_seen[:, :, where[3]])
    kept[:, middle:] = add(own[:, middle:], high_seen[:, :, where[2]])
    low_out[...] = add(low_own[...], low_seen[:, :, 1 - where[3]]).astype(HALF)
    high_out[...] = add(high_own[...], high_seen[:, :, 1 - where[2]]).astype(HALF)


def gather_kernel(where, kept, low_last, high_last, *outs):
    middle = kept.shape[1] // 2
    for k, out in enumerate(outs):
        block = where[0] ^ k
        out[:middle] = (kept[block, :middle] + low_last[block].astype(FLOAT)).astype(HALF)
        out[middle:] = (kept[block, middle:] + high_last[block].astype(FLOAT)).astype(HALF)


def sum_kernel(blocks, *refs):
    terms, (out, squares) = refs[:-2], refs[-2:]
    found, start = 0.0, 0
    for i in range(0, len(terms), blocks):
        total = terms[i][...].astype(FLOAT)
        for term in terms[i + 1 : i + blocks]:
            total = total + term[...].astype(FLOAT)
        out[start : start + total.shape[0]] = total.astype(HALF)
        start += total.shape[0]
        found = found + jnp.sum(jnp.sum(total * total, axis=(0, 1)))
    squares[...] = jnp.full(squares.shape, found)


def bound_of(limit, squares):
    return jnp.minimum(1.0, limit / jnp.sqrt(squares + EPS_NORM))


def whiten_kernel(plan, limit, where, *refs):
    left, right, pieces = refs[0], refs[1], refs[2 : 2 + plan.group]
    grad, left_gram, right_gram, own_clip = refs[2 + plan.group :]
    for k, piece in enumerate(pieces):
        for z in range(plan.blocks):
            row = pl.multiple_of((z * plan.group + (where[1] ^ k)) * plan.rows, plan.rows)
            grad[pl.ds(row, plan.rows), :] = piece[z]
    wide = grad[...].astype(FLOAT)
    clip = bound_of(limit, jnp.sum(wide * wide, keepdims=True))
    own_clip[...] = jnp.broadcast_to(clip, own_clip.shape)
    h = plan.size // 2
    left_times = jnp.concatenate(
        [product(left[:h, :], grad[...]), product(left[h:, h:], grad[h:, :])], axis=0
    )
    left_times = (clip * left_times).astype(HALF)
    whitened = jnp.concatenate(
        [product(left_times, right[:h, :], 1, 1), product(left_times[:, h:], right[h:, h:], 1, 1)],
        axis=1,
    ).astype(HALF)
    gram_rows(left_gram, whitened)
    gram_columns(right_gram, whitened)


def step_factor(factor, ratio, first_ref, second_ref):
    first, second = ratio * first_ref[...], second_ref[...]
    bound_value = jnp.max(jnp.abs(first + second), keepdims=True) + EPS_NORM
    row = lax.broadcasted_iota(jnp.int32, first.shape, 0)
    column = lax.broadcasted_iota(jnp.int32, first.shape, 1)
    change = jnp.where(row <= column, first - second, 0.0).astype(HALF)
    moved_rows = product(change, factor)
    return (factor.astype(FLOAT) - LEARN_RATE / bound_value * moved_rows).astype(HALF)


def clip_of(limit, squares):
    return bound_of(limit, squares[0:1, 0:1])


def gram_rows(out, matrix):
    h = out.shape[0] // 2
    out[:h, :] = product(matrix[:h, :], matrix, 1, 1)
    out[h:, h:] = product(matrix[h:, :], matrix[h:, :], 1, 1)


def gram_columns(out, matrix):
    h = out.shape[0] // 2
    out[:h, :] = product(matrix[:, :h], matrix, 0, 0)
    out[h:, h:] = product(matrix[:, h:], matrix[:, h:], 0, 0)


def move_factor(out, factor, ratio, first, second):
    h = out.shape[0] // 2
    firsts = ratio * first[:h, :], ratio * first[h:, h:]
    seconds = second[:h, :], second[h:, h:]
    peaks = [jnp.max(jnp.abs(p + q), keepdims=True) for p, q in zip(firsts, seconds)]
    scale = LEARN_RATE / (jnp.maximum(*peaks) + EPS_NORM)
    top, end = [
        jnp.where(
            lax.broadcasted_iota(jnp.int32, p.shape, 0) <= lax.broadcasted_iota(jnp.int32, p.shape, 1),
            p - q,
            0.0,
        ).astype(HALF)
        for p, q in zip(firsts, seconds)
    ]

    def moved(old, moved_rows):
        return (old.astype(FLOAT) - scale * moved_rows).astype(HALF)

    out[:h, :h] = moved(factor[:h, :h], product(top[:, :h], factor[:h, :h]))
    out[:h, h:] = moved(factor[:h, h:], product(top, factor[:, h:]))
    out[h:, :h] = jnp.zeros((h, h), HALF)
    out[h:, h:] = moved(factor[h:, h:], product(end, factor[h:, h:]))


def square_of(out, factor):
    h = out.shape[0] // 2
    out[:h, :] = product(factor[:h, :h], factor[:h, :], 0, 0).astype(HALF)
    out[h:, :h] = product(factor[:h, h:], factor[:h, :h], 0, 0).astype(HALF)
    out[h:, h:] = product(factor[:, h:], factor[:, h:], 0, 0).astype(HALF)


def finish_kernel(plan, limit, where, *refs):
    squares, own_clip, left, right, grad, left_p, right_p, left_q, right_q = refs[:9]
    outs, (new_left, new_right, left_square, right_square, result) = refs[9:-5], refs[-5:]
    clip = clip_of(limit, squares)
    ratio = clip / own_clip[0:1, 0:1]
    ratio = ratio * ratio
    size, rows = plan.size, plan.rows
    move_factor(new_left, left, ratio, left_p, left_q)
    move_factor(new_right, right, ratio, right_p, right_q)
    square_of(left_square, new_left)
    square_of(right_square, new_right)

    def at(z):
        return pl.ds(pl.multiple_of((z * plan.group + where[1]) * rows, rows), rows)

    precond_left = jnp.concatenate([left_square[at(z), :] for z in range(plan.blocks)], axis=0)
    middle = (clip * product(precond_left, grad[...])).astype(HALF)
    done = product(middle, right_square[...]).astype(HALF)
    result[...] = done.reshape(plan.blocks, rows, size)
    for k, out in enumerate(outs):
        z = where[0] ^ k
        out[:, :size] = new_left[at(z), :]
        out[:, size : 2 * size] = new_right[at(z), :]
        out[:, 2 * size :] = result[z]


def place_kernel(plan, where, slots, old_state, *refs):
    pieces, (precond, new_state) = refs[: plan.blocks], refs[plan.blocks :]
    size = plan.size
    new_state[...] = old_state[...]
    for k, piece in enumerate(pieces):
        precond[where[0] ^ k] = piece[:, 2 * size :]
        new_state[slots[where[0] ^ k]] = piece[:, : 2 * size]


def shaped(shape, dtype=HALF):
    return jax.ShapeDtypeStruct(shape, dtype)


def body(partial_grads, factors, inverse_factors, probes, slot_table):
    devices = lax.axis_size("dp")
    halves = lax.axis_size("mp")
    me = lax.axis_index("dp")
    experts, block_rows, size, columns = partial_grads.shape[1:]
    blocks = experts * block_rows
    plan = Plan(devices, blocks, size)
    group, rows = plan.group, plan.rows
    my_block = me // group
    my_place = me % group
    my_low, my_high = my_place % 2, my_place // 2
    where = jnp.stack([my_block, my_place, my_low, my_high]).astype(jnp.int32)
    slot_row = slot_table[0]
    in_tiles = rows % 16 == 0 and size % (2 * LANES) == 0
    limit = CLIP_RMS * math.sqrt(blocks * size * columns * halves)

    grads = partial_grads[0].reshape(blocks, blocks, group, rows, columns)
    middle = blocks // 2
    if in_tiles and group == 4:

        def part(array, half, high, low):
            start = (0, (half or 0) * middle, high, low, 0, 0)
            extent = (
                blocks,
                blocks if half is None else middle,
                2 if high is None else 1,
                2 if low is None else 1,
                rows,
                columns,
            )
            array = array.reshape(blocks, blocks, 2, 2, rows, columns)
            cut = lax.dynamic_slice(array, [0 if i is None else i for i in start], extent)
            return cut.reshape([n for i, n in enumerate(extent) if n > 1 or i not in (2, 3)])

        first = part(grads, 0, None, 1 - my_low), part(grads, 1, 1 - my_high, None)
        low_seen = flip(first[0], devices, 1)
        high_seen = flip(first[1], devices, 2)
        kept, low_sent, high_sent = call(
            relay_kernel,
            (shaped((blocks, blocks, rows, columns), FLOAT),)
            + (shaped((blocks, middle, rows, columns)),) * 2,
            [],
            0,
            1,
            where,
            part(grads, None, my_high, my_low),
            part(grads, 0, 1 - my_high, my_low),
            low_seen,
            part(grads, 1, my_high, 1 - my_low),
            high_seen,
        )
        parts = call(
            gather_kernel,
            tuple(shaped((blocks, rows, columns)) for _ in range(blocks)),
            [],
            0,
            1,
            where,
            kept,
            flip(low_sent, devices, 2),
            flip(high_sent, devices, 1),
        )
    else:
        halves_of = []
        masks = [1 << i for i in range(group.bit_length() - 1)]
        for half, order in enumerate((masks, masks[::-1])):
            kept = grads[:, half * middle : (half + 1) * middle].astype(FLOAT)
            kept = kept.reshape(blocks, middle, *[2] * len(masks), rows, columns)
            left = sorted(masks, reverse=True)
            for mask in order:
                axis, bit = 2 + left.index(mask), my_place // mask % 2
                sent = pick(kept, 1 - bit, axis).astype(HALF)
                left.remove(mask)
                kept = pick(kept, bit, axis) + flip(sent, devices, mask)
            halves_of.append(kept)
        total = jnp.concatenate(halves_of, axis=1).astype(HALF)
        parts = [pick(total, my_block ^ k, 0) for k in range(blocks)]

    old_state = factors[0]
    if in_tiles:
        pieces = call(
            functools.partial(choose_kernel, plan),
            tuple(shaped((rows, 5 * size)) for _ in range(blocks)),
            [pltpu.SemaphoreType.DMA((3 * blocks,))],
            0,
            2,
            where,
            slot_row,
            old_state,
            inverse_factors[0],
            probes[0],
            space=pltpu.HBM,
        )
    else:
        wide = jnp.concatenate([old_state, inverse_factors[0], probes[0]], axis=2)
        pieces = [pick(wide, slot_row[my_block ^ k], 0) for k in range(blocks)]
    pieces = [pieces[0]] + [flip(pieces[k], devices, k * group) for k in range(1, blocks)]
    if in_tiles:
        quarter = call(
            functools.partial(pack_kernel, plan),
            shaped((rows, plan.packed())),
            [pltpu.VMEM((blocks, rows, 5 * size), HALF)],
            0,
            1,
            where,
            *pieces,
        )
    else:
        quarter = unflip(pieces, my_block)

    terms = [parts[0]] + [flip(parts[k], devices, k * group) for k in range(1, blocks)]
    grad_quarter, squares = call(
        functools.partial(sum_kernel, blocks),
        (shaped((blocks, rows, columns)), shaped((8, LANES), FLOAT)),
        [],
        0,
        0,
        *terms,
    )

    if in_tiles and group == 4:
        states = [quarter] + [flip(quarter, devices, k) for k in (1, 2)]
        cut = states[1][:, : plan.split()], states[2][:, plan.split() :]
        states += [flip(cut[i], devices, 2 - i) for i in range(2)]
    else:
        states = [quarter] + [flip(quarter, devices, k) for k in range(1, group)]
    quarters = [grad_quarter] + [flip(grad_quarter, devices, k) for k in range(1, group)]

    squares = functools.reduce(
        jnp.add,
        [squares] + [flip(squares, devices, k * group) for k in range(1, blocks)],
    )
    bit = 1
    while bit < halves:
        other = lax.ppermute(squares, "mp", [(i, i ^ bit) for i in range(halves)])
        squares = squares + other
        bit *= 2
    bit = 1
    while bit < group:
        squares = squares + flip(squares, devices, bit)
        bit *= 2

    gram = shaped((size, size), FLOAT)
    square = shaped((size, size))
    matmul = 2 * size**3
    if in_tiles:
        left_q, right_q, left_c, right_c = call(
            functools.partial(probe_kernel, plan),
            (square, square, gram, gram),
            [pltpu.VMEM((size, size), HALF)] * 3,
            4 * matmul,
            1,
            where,
            *states,
        )
        gradient, left_w, right_w, own_clip = call(
            functools.partial(whiten_kernel, plan, limit),
            (shaped((size, columns)), gram, gram, shaped((8, LANES), FLOAT)),
            [],
            4 * matmul,
            1,
            where,
            left_q,
            right_q,
            *quarters,
        )
        back = call(
            functools.partial(finish_kernel, plan, limit),
            tuple(shaped((rows, 2 * size + columns)) for _ in range(blocks)),
            [pltpu.VMEM((size, size), HALF)] * 4 + [pltpu.VMEM((blocks, rows, columns), HALF)],
            5 * matmul,
            1,
            where,
            squares,
            own_clip,
            left_q,
            right_q,
            gradient,
            left_w,
            right_w,
            left_c,
            right_c,
        )
    else:
        back = plain_block(plan, limit, my_block, my_place, squares, states, quarters)
    back = [back[0]] + [flip(back[k], devices, k * group) for k in range(1, blocks)]
    precond, new_state = call(
        functools.partial(place_kernel, plan),
        (shaped((blocks, rows, columns)), shaped(old_state.shape)),
        [],
        0,
        2,
        where,
        slot_row,
        old_state,
        *back,
    )
    return (precond.reshape(experts, block_rows, rows, columns), new_state[None])


def plain_block(plan, limit, my_block, my_place, squares, states, quarters):
    size, blocks, group, rows = plan.size, plan.blocks, plan.group, plan.rows
    state = unflip(states, my_place).transpose(1, 0, 2, 3).reshape(size, 5 * size)
    gradient = unflip(quarters, my_place).transpose(1, 0, 2, 3).reshape(size, -1)
    clip = clip_of(limit, squares)
    left_q, right_q, left_inv, right_inv, probe_mat = jnp.split(state, 5, axis=1)
    half_conjugate = product(left_inv, probe_mat, 0, 0).astype(HALF)
    conjugate = product(half_conjugate, right_inv).astype(HALF)
    left_times = (clip * product(left_q, gradient)).astype(HALF)
    whitened = product(left_times, right_q, 1, 1).astype(HALF)
    new_left = step_factor(
        left_q, 1.0, product(whitened, whitened, 1, 1), product(conjugate, conjugate, 1, 1)
    )
    new_right = step_factor(
        right_q, 1.0, product(whitened, whitened, 0, 0), product(conjugate, conjugate, 0, 0)
    )
    precond_left = product(new_left, new_left, 0, 0).astype(HALF)
    precond_right = product(new_right, new_right, 0, 0).astype(HALF)

    def my_rows(array):
        return pick(array.reshape(blocks, group, rows, -1), my_place, 1)

    middle = (clip * product(my_rows(precond_left).reshape(blocks * rows, size), gradient)).astype(HALF)
    result = product(middle, precond_right).astype(HALF).reshape(blocks, rows, -1)
    back = jnp.concatenate([my_rows(new_left), my_rows(new_right), result], axis=2)
    return [pick(back, my_block ^ k, 0) for k in range(blocks)]


def solution(mesh):
    return jax.shard_map(
        body,
        mesh=mesh,
        in_specs=(
            P("dp", None, None, None, "mp"),
            P("mp", None, "dp", None),
            P("mp", None, "dp", None),
            P("mp", None, "dp", None),
            P("mp", None),
        ),
        out_specs=(P(None, None, "dp", "mp"), P("mp", None, "dp", None)),
        check_vma=False,
    )
```
